32 devices in a mesh: dp: 8 (over z, x), mp: 4 (over y, core).
Axes of the slice: x: 2, y: 2, z: 4, core: 2. Of those that a mesh axis runs over, the one named last changes fastest.
Arguments:
- encoder_rows: bfloat16 [16384, 768], P('dp'), may hold values from -6 to 6
- piece_extent_sequence: int32 [32, 8], P('dp'), may hold values from 1 to 192, 512 in all within a row
- triple_projection_matrix: bfloat16 [3, 768, 768], P(None, None, 'mp'), may hold values from -0.21875 to 0.21875
- asker_content_shifts: float32 [2, 768], P(None, 'mp'), may hold values from -3 to 3
- mixing_result_matrix: bfloat16 [768, 768], P('mp'), may hold values from -1.75 to 1.75
- mixing_result_offset_vector: float32 [768], replicated, may hold values from -2 to 2
- mixing_normalizer_scale: float32 [768], replicated, may hold values from 0.25 to 1.75
- mixing_normalizer_shift: float32 [768], replicated, may hold values from -2 to 2
- widen_matrix: bfloat16 [768, 3072], P(None, 'mp'), may hold values from -0.21875 to 0.21875
- widen_shift_vector: float32 [3072], P('mp'), may hold values from -3 to 3
- narrow_matrix: bfloat16 [3072, 768], P('mp'), may hold values from -0.15625 to 0.15625
- narrow_shift_vector: float32 [768], replicated, may hold values from -2 to 2
- perceptron_normalizer_scale: float32 [768], replicated, may hold values from 0.25 to 1.75
- perceptron_normalizer_shift: float32 [768], replicated, may hold values from -2 to 2
- document_vectors: bfloat16 [131072, 768], P(('dp', 'mp')), may hold values from -0.36084392 to 0.36084392
- sharpness_factor: float32 [1], replicated, may hold values from 0.4 to 0.52
- correct_document_position: int32 [256], replicated, may hold values from 0 to 131071
- upstream_sensitivity: float32 [16384, 768], P('dp'), may hold values from -0.12 to 0.12
Outputs:
- layer_out: bfloat16 [16384, 768], P('dp')
- seg_loss: float32 [256], replicated
- grad_tokens: float32 [16384, 768], P('dp')
- grad_head_weight: float32 [3, 768, 768], P(None, None, 'mp')
- grad_head_bias: float32 [2, 768], P(None, 'mp')
- grad_out_weight: float32 [768, 768], P('mp')
- grad_out_bias: float32 [768], replicated
- grad_first_gain: float32 [768], replicated
- grad_first_shift: float32 [768], replicated
- grad_up_weight: float32 [768, 3072], P(None, 'mp')
- grad_up_bias: float32 [3072], P('mp')
- grad_down_weight: float32 [3072, 768], P('mp')
- grad_down_bias: float32 [768], replicated
- grad_second_gain: float32 [768], replicated
- grad_second_shift: float32 [768], replicated
- sharpness_derivative: float32 [1], replicated
The draws below stay inside these ranges and needn't reach their ends.
Inputs may be any that keep to these rules, and one draw needn't show every extreme that they name: `piece_extent_sequence`: each row holds the lengths of the 8 segments of one block in order and sums to 512; the longest segment of each row has exactly 192 tokens.
All inputs are finite; a program needn't handle non-finite values.
Results may differ from the reference program's by a relative error of at most 0.013.
The reference program's roundings to bfloat16 on the way count: a program that leaves them out, or rounds other values in their place, can miss the bound.
Values may be sent and summed in bfloat16 or wider, within the bound.
A program may use at most 192 MiB of HBM per device.

```python
import math
import jax
import jax.numpy as jnp
import numpy as np
from jax import lax

D = 768
HEADS = 12
HEAD = 64
FF = 3072
BLOCK = 512
SEG_BLK = 8
SEG_MOST = 192
P_DEV = 4096
BLOCKS = 32
TOKENS = 16384
NSEG = 256
PASSAGES = 131072
DEVICES = 32


def draw_document_vectors(key, part):
    row_key, column_key, base_key = jax.random.split(key, 3)
    row_scale = jnp.exp(jax.random.uniform(row_key, (PASSAGES, 1), jnp.float32, 0.0, math.log(2.5)))
    column_scale = jnp.exp(jax.random.uniform(column_key, (1, D), jnp.float32, 0.0, math.log(3.0)))
    factor = 1.0 / (3.0 * math.sqrt(D))
    base = jax.random.truncated_normal(base_key, -4.0, 4.0, (PASSAGES, D), jnp.float32)
    values = base * row_scale * column_scale * factor
    return values.astype(jnp.bfloat16)


def place_ends(values, own_key, smallest, largest):
    place = [jax.random.randint(jax.random.fold_in(own_key, axis), (), 0, length) for axis, length in enumerate(values.shape)]
    main_axis = values.shape.index(max(values.shape))
    neighbour = place[:main_axis] + [(place[main_axis] + 1) % values.shape[main_axis]] + place[main_axis + 1:]
    return values.at[tuple(place)].set(smallest).at[tuple(neighbour)].set(largest)


def shard_levels(rng, dims, cuts, least, high):
    factor_of = 1.0
    for position, blocks in cuts:
        steps = jax.random.uniform(jax.random.fold_in(jax.random.fold_in(rng, 6), position), (blocks,), jnp.float32, least / len(cuts), high / len(cuts))
        factor_of = factor_of * jnp.repeat(jnp.exp(steps), dims[position] // blocks).reshape((-1,) + (1,) * (len(dims) - 1 - position))
    return factor_of


def split_up(count, total, limit, skew):
    loads = [(1 << 20) // math.isqrt(grade ** skew) + 1 for grade in range(2, count + 1)]
    surplus, counts = total - limit - (count - 1), [1] * (count - 1)
    while surplus > 0:
        candidates = [i for i in range(count - 1) if counts[i] < limit]
        whole, left = sum([loads[i] for i in candidates]), surplus
        for i in candidates:
            more = min(limit - counts[i], max(1, left * loads[i] // whole), surplus)
            counts[i] = counts[i] + more
            surplus = surplus - more
    return np.array([limit] + counts)


def ragged_sizes(key, count, total, most, skew):
    if count == 2:
        one = jax.random.randint(key, (), max(1, total - most), min(most, total - 1) + 1)
        return jnp.stack([one, total - one])
    sizes = jnp.asarray(split_up(count, total, most, skew), jnp.int32)
    couples = (count - 1) // 2
    donor, taker = sizes[1:1 + 2 * couples:2], sizes[2:2 + 2 * couples:2]
    slack = jnp.minimum(donor - 1, most - taker)
    passed = jax.random.randint(jax.random.fold_in(key, 1), (couples,), 0, 1 << 20) % (slack + 1)
    sizes = sizes.at[1:1 + 2 * couples:2].set(donor - passed).at[2:2 + 2 * couples:2].set(taker + passed)
    return sizes[jax.random.permutation(jax.random.fold_in(key, 2), count)]


def bell_draw(key, extent, width, reach, shards=(), held_as=jnp.bfloat16):
    entries = width * jax.random.normal(key, extent, jnp.float32)
    if shards:
        entries = entries * shard_levels(key, extent, shards, -0.22, 0.18)
    return jnp.clip(entries, -reach, reach).astype(held_as)


def setup_inputs(seed: int = 0) -> dict:
    seeds = jax.random.split(jax.random.key(seed), 19)
    return {
        "encoder_rows": bell_draw(seeds[0], (TOKENS, D), 1.0, 6.0, ((0, 8),)),
        "piece_extent_sequence": jax.vmap(lambda own: ragged_sizes(own, SEG_BLK, BLOCK, SEG_MOST, 2))(jax.random.split(seeds[1], BLOCKS)).reshape((BLOCKS, SEG_BLK)).astype(jnp.int32),
        "triple_projection_matrix": bell_draw(seeds[2], (3, D, D), D ** -0.5, 0.21875, ((2, 4),)),
        "asker_content_shifts": bell_draw(seeds[3], (2, D), 0.5, 3.0, ((1, 4),), jnp.float32),
        "mixing_result_matrix": bell_draw(seeds[4], (D, D), (D // 64) ** -0.5, 1.75, ((0, 4),)),
        "mixing_result_offset_vector": bell_draw(seeds[5], (D,), 0.3, 2.0, (), jnp.float32),
        "mixing_normalizer_scale": jnp.clip(1.0 + 0.15 * jax.random.normal(seeds[6], (D,), jnp.float32), 0.25, 1.75),
        "mixing_normalizer_shift": bell_draw(seeds[7], (D,), 0.3, 2.0, (), jnp.float32),
        "widen_matrix": bell_draw(seeds[8], (D, FF), D ** -0.5, 0.21875, ((1, 4),)),
        "widen_shift_vector": bell_draw(seeds[9], (FF,), 0.5, 3.0, ((0, 4),), jnp.float32),
        "narrow_matrix": bell_draw(seeds[10], (FF, D), (FF // 2) ** -0.5, 0.15625, ((0, 4),)),
        "narrow_shift_vector": bell_draw(seeds[11], (D,), 0.3, 2.0, (), jnp.float32),
        "perceptron_normalizer_scale": jnp.clip(1.0 + 0.15 * jax.random.normal(seeds[12], (D,), jnp.float32), 0.25, 1.75),
        "perceptron_normalizer_shift": bell_draw(seeds[13], (D,), 0.3, 2.0, (), jnp.float32),
        "document_vectors": draw_document_vectors(jax.random.fold_in(seeds[18], 71), 0),
        "sharpness_factor": jnp.clip(jnp.exp(jax.random.uniform(seeds[15], (1,), jnp.float32, math.log(0.4), math.log(0.52))), 0.4, 0.52),
        "correct_document_position": place_ends(jax.random.randint(seeds[16], (NSEG,), 0, PASSAGES), jax.random.fold_in(seeds[16], 1), 0, PASSAGES - 1).astype(jnp.int32),
        "upstream_sensitivity": bell_draw(seeds[17], (TOKENS, D), 0.02, 0.12, ((0, 8),), jnp.float32),
    }


@jax.custom_vjp
def low(v):
    return lax.optimization_barrier(v.astype(jnp.bfloat16)).astype(jnp.float32)

@jax.custom_vjp
def low_back(v):
    return v

def low_keep(v):
    return (low(v), None)

def low_pass(kept, grad):
    return (grad,)

def back_keep(v):
    return (v, None)

def back_low(kept, grad):
    return (low(grad),)
low.defvjp(low_keep, low_pass)
low_back.defvjp(back_keep, back_low)
norm_epsilon = 1e-05
masked_score = -1e+30

def layer_norm(resid, gain, shift):
    centre = lax.optimization_barrier(jnp.mean(resid, axis=-1, keepdims=True))
    centred = resid - centre
    spread = lax.optimization_barrier(jnp.mean(centred * centred, axis=-1, keepdims=True))
    return centred * lax.rsqrt(spread + norm_epsilon) * gain + shift

def segment_layout(piece_extent_sequence):
    ends = jnp.cumsum(piece_extent_sequence, axis=1)
    starts = ends - piece_extent_sequence
    places = jnp.arange(BLOCK, dtype=jnp.int32)
    seg_index = lax.optimization_barrier(jnp.sum((places[None, :, None] >= ends[:, None, :]).astype(jnp.int32), axis=2))
    firsts = (jnp.arange(piece_extent_sequence.shape[0], dtype=jnp.int32)[:, None] * BLOCK + starts).reshape(-1)
    return (seg_index, firsts.astype(jnp.int32))

def block_attention(queries, keys, values, seg_index):
    raw_scores = low_back(jnp.einsum('qhe,khe->hqk', queries, keys, precision=lax.Precision.HIGHEST))
    scores = raw_scores * HEAD ** (-0.5)
    same = seg_index[:, None] == seg_index[None, :]
    scores = jnp.where(same[None], scores, masked_score)
    probs = low(jax.nn.softmax(scores, axis=-1))
    return jnp.einsum('hqk,khe->qhe', probs, values, precision=lax.Precision.HIGHEST)

def reference(encoder_rows, piece_extent_sequence, triple_projection_matrix, asker_content_shifts, mixing_result_matrix, mixing_result_offset_vector, mixing_normalizer_scale, mixing_normalizer_shift, widen_matrix, widen_shift_vector, narrow_matrix, narrow_shift_vector, perceptron_normalizer_scale, perceptron_normalizer_shift, document_vectors, sharpness_factor, correct_document_position, upstream_sensitivity):
    highest = lax.Precision.HIGHEST
    seg_index, firsts = segment_layout(piece_extent_sequence)
    pass_blocks = document_vectors.astype(jnp.float32).reshape(DEVICES, P_DEV, D)
    id_blocks = jnp.arange(PASSAGES, dtype=jnp.int32).reshape(DEVICES, P_DEV)

    def evaluate_encoder(argument_tuple, mixing_matrix, mixing_shift, projection_matrix, projection_shift, first_scaling, first_centering, expand_matrix, expand_shift, contract_matrix, contract_shift, second_scaling, second_centering, sharpness_scalar):
        proj = jnp.einsum('td,kde->kte', argument_tuple, mixing_matrix, precision=highest)
        queries = low_back(low(proj[0] + mixing_shift[0]))
        keys = low_back(low(proj[1]))
        values = low_back(low(proj[2] + mixing_shift[1]))
        shape_four = (BLOCKS, BLOCK, HEADS, HEAD)
        mixed = lax.map(jax.checkpoint(lambda item: block_attention(*item)), (queries.reshape(shape_four), keys.reshape(shape_four), values.reshape(shape_four), seg_index))
        mixed = low_back(low(mixed.reshape(TOKENS, D)))
        attn_out = low_back(jnp.dot(mixed, projection_matrix, precision=highest))
        hidden_a = layer_norm(argument_tuple + attn_out + projection_shift, first_scaling, first_centering)
        upper = low_back(jnp.dot(low(hidden_a), expand_matrix, precision=highest) + expand_shift)
        active = low(jax.nn.gelu(upper, approximate=False))
        ffn_out = low_back(jnp.dot(active, contract_matrix, precision=highest))
        hidden_b = layer_norm(hidden_a + ffn_out + contract_shift, second_scaling, second_centering)
        query_vecs = low(hidden_b[firsts])

        def score_step(carry, item):
            top, objective_accumulated, gold_sum = carry
            pblock, idblock = item
            unscaled_scores = low_back(jnp.dot(query_vecs, pblock.T, precision=highest))
            similarity_scores = unscaled_scores / sharpness_scalar[0]
            new_top = jnp.maximum(top, lax.optimization_barrier(jnp.max(similarity_scores, axis=1)))
            objective_accumulated = objective_accumulated * jnp.exp(top - new_top) + lax.optimization_barrier(jnp.sum(jnp.exp(similarity_scores - new_top[:, None]), axis=1))
            match_mask = correct_document_position[:, None] == idblock[None, :]
            gold_sum = gold_sum + lax.optimization_barrier(jnp.sum(jnp.where(match_mask, similarity_scores, 0.0), axis=1))
            return ((new_top, objective_accumulated, gold_sum), None)
        start = (jnp.full((NSEG,), masked_score, jnp.float32), jnp.zeros((NSEG,), jnp.float32), jnp.zeros((NSEG,), jnp.float32))
        (top, objective_accumulated, gold_sum), unused = lax.scan(jax.checkpoint(score_step), start, (pass_blocks, id_blocks))
        seg_loss = top + jnp.log(objective_accumulated) - gold_sum
        return (hidden_b, seg_loss)
    saved_arguments = (encoder_rows.astype(jnp.float32), triple_projection_matrix.astype(jnp.float32), asker_content_shifts, mixing_result_matrix.astype(jnp.float32), mixing_result_offset_vector, mixing_normalizer_scale, mixing_normalizer_shift, widen_matrix.astype(jnp.float32), widen_shift_vector, narrow_matrix.astype(jnp.float32), narrow_shift_vector, perceptron_normalizer_scale, perceptron_normalizer_shift, sharpness_factor)
    (hidden_b, seg_loss), pullback = jax.vjp(evaluate_encoder, *saved_arguments)
    grads = pullback((upstream_sensitivity, jnp.ones((NSEG,), jnp.float32)))
    return (hidden_b.astype(jnp.bfloat16), seg_loss, grads[0], grads[1], grads[2], grads[3], grads[4], grads[5], grads[6], grads[7], grads[8], grads[9], grads[10], grads[11], grads[12], grads[13])
```

```python
import functools

import jax
import jax.numpy as jnp
from jax import lax
from jax.experimental import pallas as pl
from jax.experimental.pallas import tpu as pltpu
from jax.sharding import PartitionSpec as P

HEAD = 64
F32 = jnp.float32
BF16 = jnp.bfloat16
MESH = pl.DeviceIdType.MESH
norm_epsilon = 1e-05
masked_score = -1e30


def dot(a, b, ca, cb):
    return lax.dot_general(a, b, (((ca,), (cb,)), ((), ())), preferred_element_type=F32)


def norm_stats(resid):
    centre = jnp.mean(resid, axis=-1, keepdims=True)
    centred = resid - centre
    spread = jnp.mean(centred * centred, axis=-1, keepdims=True)
    inv = lax.rsqrt(spread + norm_epsilon)
    return centred * inv, inv


def norm_back(d_out, normed, inv, gain):
    e = d_out * gain
    return inv * (
        e - jnp.mean(e, axis=-1, keepdims=True) - normed * jnp.mean(e * normed, axis=-1, keepdims=True)
    )


def swap(value, width, distance):
    return lax.ppermute(value, "mp", [(i, i ^ distance) for i in range(width)])


def spread_over_mp(own, width):
    held = [own]
    order = [0]
    step = width // 2
    while step:
        held = held + [swap(h, width, step) for h in held]
        order = order + [o ^ step for o in order]
        step //= 2
    return [held[order.index(r)] for r in range(width)]


def gather_back(parts, width):
    parts = list(parts)
    step = 1
    while step < width:
        new = {}
        for r in range(width):
            if not (r & (step - 1)) and not (r & step):
                got = swap(parts[r | step].astype(BF16), width, step)
                new[r] = parts[r] + got.astype(F32)
        for r, v in new.items():
            parts[r] = v
        step *= 2
    return parts[0]


def retrieval_kernel(
    ndp, nmp, query_ref, docs_hbm, gold_ref, sharp_ref, dq_ref, loss_ref, ds_ref,
    queries, docs, low, stats, columns, part_u, part_g, send, got, doc_sem, q_send, q_recv, s_send, s_recv, d_send, d_recv,
):
    n = ndp * nmp
    own = query_ref.shape[0]
    nseg = gold_ref.shape[0]
    tile = 256 if nseg <= 256 else 128
    dp, mp = lax.axis_index("dp"), lax.axis_index("mp")
    me = dp * nmp + mp
    load = pltpu.make_async_copy(docs_hbm, docs, doc_sem)
    load.start()
    barrier = pltpu.get_barrier_semaphore()

    def device(step):
        other = lax.rem(me + step, n)
        return other, (other // nmp, lax.rem(other, nmp))

    @pl.loop(1, n)
    def _(step):
        _, where = device(step)
        pl.semaphore_signal(barrier, inc=1, device_id=where, device_id_type=MESH)

    pl.semaphore_wait(barrier, n - 1)

    def push(source, target, send_sems, recv_sems):
        @pl.loop(1, n)
        def _(step):
            other, where = device(step)
            pltpu.make_async_remote_copy(
                source(other), target, send_sems.at[step], recv_sems.at[step], device_id=where, device_id_type=MESH
            ).start()

    def drain(source, target, send_sems, recv_sems):
        @pl.loop(1, n)
        def _(step):
            other, where = device(step)
            copy = pltpu.make_async_remote_copy(
                source(other), target, send_sems.at[step], recv_sems.at[step], device_id=where, device_id_type=MESH
            )
            copy.wait()

    push(lambda other: query_ref, queries.at[me], q_send, q_recv)
    queries[me] = query_ref[...]
    drain(lambda other: query_ref, queries.at[me], q_send, q_recv)
    load.wait()

    sharp = sharp_ref[0]
    offset = me * docs.shape[0]
    ids = lax.broadcasted_iota(jnp.int32, (tile, docs.shape[0]), 1)
    lane = lax.broadcasted_iota(jnp.int32, (tile, 128), 1)
    per = tile // own

    @pl.loop(0, nseg // tile)
    def _(i):
        span = pl.ds(pl.multiple_of(i * tile, tile), tile)
        q = queries[pl.ds(i * per, per)].reshape(tile, queries.shape[2])
        logit = lax.dot_general(q, docs[...], (((1,), (1,)), ((), ())), preferred_element_type=F32) / sharp
        match = ids == gold_ref[span, :] - offset
        top = jnp.max(logit, axis=1, keepdims=True)
        expo = jnp.exp(logit - top)
        total = jnp.sum(expo, axis=1, keepdims=True)
        tilt = jnp.sum(expo * logit, axis=1, keepdims=True)
        gold = jnp.sum(jnp.where(match, logit, 0.0), axis=1, keepdims=True)
        packed = jnp.where(lane == 0, top, jnp.where(lane == 1, total, jnp.where(lane == 2, tilt, gold)))
        stats[me, :, span] = packed.T[:4]
        low[span, :] = jnp.where(match, 0.0, expo).astype(BF16)

    push(lambda other: stats.at[me], stats.at[me], s_send, s_recv)

    @pl.loop(0, nseg // tile)
    def _(i):
        span = pl.ds(pl.multiple_of(i * tile, tile), tile)
        part_u[span, :] = jnp.dot(low[span, :], docs[...], preferred_element_type=F32)
        match = ids == gold_ref[span, :] - offset
        part_g[span, :] = jnp.dot(
            match.astype(F32).astype(BF16), docs[...], preferred_element_type=F32
        ).astype(BF16)

    drain(lambda other: stats.at[me], stats.at[me], s_send, s_recv)

    tops = stats[:, 0, :]
    top = jnp.max(tops, axis=0, keepdims=True)
    share = jnp.exp(tops - top)
    total = jnp.sum(stats[:, 1, :] * share, axis=0, keepdims=True)
    tilt = jnp.sum(stats[:, 2, :] * share, axis=0, keepdims=True)
    gold = jnp.sum(stats[:, 3, :], axis=0, keepdims=True)
    lse = top + jnp.log(total)
    loss_ref[...] = lse - gold
    ds_ref[...] = -jnp.sum(tilt / total - gold, axis=1, keepdims=True) / sharp
    scale = jnp.exp(stats[me, 0:1, :] - lse) / sharp
    gold_scale = (jnp.exp(gold - lse) - 1.0) / sharp
    row = lax.broadcasted_iota(jnp.int32, (128, nseg), 0)
    columns[...] = jnp.where(row == 0, scale, gold_scale).T

    @pl.loop(0, nseg // tile)
    def _(i):
        span = pl.ds(pl.multiple_of(i * tile, tile), tile)
        value = part_u[span, :] * columns[span, 0:1] + part_g[span, :].astype(F32) * columns[span, 1:2]
        send[pl.ds(i * per, per)] = value.astype(BF16).reshape(per, own, value.shape[1])

    push(lambda other: send.at[other], got.at[me], d_send, d_recv)
    got[me] = send[me]
    drain(lambda other: send.at[other], got.at[me], d_send, d_recv)
    dq_ref[...] = jnp.sum(got[...].astype(F32), axis=0)


def retrieval(query, docs, gold, sharp, ndp, nmp):
    n = ndp * nmp
    own, width = query.shape
    nseg = gold.shape[0]
    vmem = pl.BlockSpec(memory_space=pltpu.VMEM)
    return pl.pallas_call(
        functools.partial(retrieval_kernel, ndp, nmp),
        out_shape=(
            jax.ShapeDtypeStruct((own, width), F32),
            jax.ShapeDtypeStruct((1, nseg), F32),
            jax.ShapeDtypeStruct((1, 1), F32),
        ),
        in_specs=[vmem, pl.BlockSpec(memory_space=pl.ANY), vmem, pl.BlockSpec(memory_space=pltpu.SMEM)],
        out_specs=(vmem, vmem, vmem),
        scratch_shapes=[
            pltpu.VMEM((n, own, width), BF16),
            pltpu.VMEM(docs.shape, BF16),
            pltpu.VMEM((nseg, docs.shape[0]), BF16),
            pltpu.VMEM((n, 4, nseg), F32),
            pltpu.VMEM((nseg, 128), F32),
            pltpu.VMEM((nseg, width), F32),
            pltpu.VMEM((nseg, width), BF16),
            pltpu.VMEM((n, own, width), BF16),
            pltpu.VMEM((n, own, width), BF16),
            pltpu.SemaphoreType.DMA,
        ]
        + [pltpu.SemaphoreType.DMA((n,))] * 6,
        compiler_params=pltpu.CompilerParams(
            collective_id=0, has_side_effects=True, vmem_limit_bytes=60 * 2**20
        ),
        name="retrieval",
    )(query, docs, gold, sharp)


def attention(q, k, v, same):
    rows, feat = q.shape
    heads = feat // HEAD
    shape = (rows, heads, HEAD)
    scores = jnp.einsum("qhe,khe->hqk", q.reshape(shape), k.reshape(shape), preferred_element_type=F32)
    scores = jnp.where(same[None], scores * HEAD ** (-0.5), masked_score)
    top = jnp.max(scores, axis=-1, keepdims=True)
    expo = jnp.exp(scores - top)
    total = jnp.sum(expo, axis=-1, keepdims=True)
    probs = (expo / total).astype(BF16)
    mixed = jnp.einsum("hqk,khe->qhe", probs, v.reshape(shape), preferred_element_type=F32)
    return mixed.reshape(rows, feat).astype(BF16), top + jnp.log(total)


def attention_back(q, k, v, lse, d_mixed, same):
    rows, feat = q.shape
    heads = feat // HEAD
    shape = (rows, heads, HEAD)
    scale = HEAD ** (-0.5)
    q, k, v, d_mixed = (t.reshape(shape) for t in (q, k, v, d_mixed))
    scores = jnp.einsum("qhe,khe->hqk", q, k, preferred_element_type=F32)
    scores = jnp.where(same[None], scores * scale, masked_score)
    probs = jnp.exp(scores - lse)
    d_v = jnp.einsum("hqk,qhe->khe", probs.astype(BF16), d_mixed, preferred_element_type=F32)
    d_p = jnp.einsum("qhe,khe->hqk", d_mixed, v, preferred_element_type=F32)
    d_s = (probs * (d_p - jnp.sum(d_p * probs, axis=-1, keepdims=True)) * scale).astype(BF16)
    d_q = jnp.einsum("hqk,khe->qhe", d_s, k, preferred_element_type=F32)
    d_k = jnp.einsum("hqk,qhe->khe", d_s, q, preferred_element_type=F32)
    return tuple(t.reshape(rows, feat).astype(BF16) for t in (d_q, d_k, d_v))


def local(
    encoder_rows,
    piece_extent_sequence,
    triple_projection_matrix,
    asker_content_shifts,
    mixing_result_matrix,
    mixing_result_offset_vector,
    mixing_normalizer_scale,
    mixing_normalizer_shift,
    widen_matrix,
    widen_shift_vector,
    narrow_matrix,
    narrow_shift_vector,
    perceptron_normalizer_scale,
    perceptron_normalizer_shift,
    document_vectors,
    sharpness_factor,
    correct_document_position,
    upstream_sensitivity,
    *,
    width,
    depth,
):
    everyone = ("dp", "mp")
    me = lax.axis_index("mp")
    nblock, nseg_block = piece_extent_sequence.shape
    block = encoder_rows.shape[0] // nblock
    own_blocks = nblock // width
    rows = own_blocks * block
    feat = triple_projection_matrix.shape[2]
    quarters = range(width)

    x = lax.dynamic_slice_in_dim(encoder_rows, me * rows, rows, 0)
    upstream = lax.dynamic_slice_in_dim(upstream_sensitivity, me * rows, rows, 0)
    extents = lax.dynamic_slice_in_dim(piece_extent_sequence, me * own_blocks, own_blocks, 0)

    w_qkv = spread_over_mp(triple_projection_matrix, width)
    small = spread_over_mp(
        jnp.concatenate([asker_content_shifts.reshape(-1), widen_shift_vector])[None], width
    )
    w_out = spread_over_mp(mixing_result_matrix, width)
    w_up = spread_over_mp(widen_matrix, width)
    w_down = spread_over_mp(narrow_matrix, width)
    b_q = [s[:, :feat] for s in small]
    b_v = [s[:, feat : 2 * feat] for s in small]
    b_up = [s[:, 2 * feat :] for s in small]

    ends = jnp.cumsum(extents, axis=1)
    starts = ends - extents
    places = jnp.arange(rows, dtype=jnp.int32)
    base = (jnp.arange(own_blocks, dtype=jnp.int32) * block)[:, None]
    seg = jnp.sum((places[:, None] >= (ends + base).reshape(-1)[None]).astype(jnp.int32), axis=1)
    same = seg[:, None] == seg[None, :]
    firsts = (starts + base).reshape(-1)
    select = firsts[:, None] == places[None, :]
    pick = select.astype(BF16)

    qs, ks, vs, lses, mixed = [], [], [], [], []
    for r in quarters:
        proj = jnp.einsum("td,kde->kte", x, w_qkv[r], preferred_element_type=F32)
        q = (proj[0] + b_q[r]).astype(BF16)
        k = proj[1].astype(BF16)
        v = (proj[2] + b_v[r]).astype(BF16)
        m, lse = attention(q, k, v, same)
        qs.append(q), ks.append(k), vs.append(v), lses.append(lse), mixed.append(m)
    attn_out = sum(dot(mixed[r], w_out[r], 1, 0) for r in quarters)
    n1, inv1 = norm_stats(x.astype(F32) + attn_out + mixing_result_offset_vector)
    h1 = n1 * mixing_normalizer_scale + mixing_normalizer_shift
    h1_low = h1.astype(BF16)
    acts, slopes = [], []
    for r in quarters:
        upper = dot(h1_low, w_up[r], 1, 0) + b_up[r]
        act, back = jax.vjp(lambda u: jax.nn.gelu(u, approximate=False), upper)
        acts.append(act.astype(BF16))
        slopes.append(back(jnp.ones_like(upper))[0])
    ffn_out = sum(dot(acts[r], w_down[r], 1, 0) for r in quarters)
    n2, inv2 = norm_stats(h1 + ffn_out + narrow_shift_vector)
    h2 = n2 * perceptron_normalizer_scale + perceptron_normalizer_shift
    own_out = h2.astype(BF16)
    layer_out = lax.all_gather(own_out, "mp", axis=0, tiled=True)

    query = dot(pick, own_out, 1, 0).astype(BF16)
    d_query, seg_loss, sharpness_derivative = retrieval(
        query, document_vectors, correct_document_position[:, None], sharpness_factor, depth, width
    )
    seg_loss = seg_loss[0]
    sharpness_derivative = sharpness_derivative[0]
    d_h2 = upstream + lax.dot_general(
        select.astype(F32), d_query, (((0,), (0,)), ((), ())), precision=lax.Precision.HIGHEST
    )
    d_r2 = norm_back(d_h2, n2, inv2, perceptron_normalizer_scale)
    g_second_gain = jnp.sum(d_h2 * n2, axis=0)
    g_second_shift = jnp.sum(d_h2, axis=0)
    g_down_bias = jnp.sum(d_r2, axis=0)
    d_ffn = d_r2.astype(BF16)
    g_down = gather_back([dot(acts[r], d_ffn, 0, 0) for r in quarters], width)
    d_up = [(dot(d_ffn, w_down[r], 1, 1) * slopes[r]).astype(BF16) for r in quarters]
    g_up_bias = [jnp.sum(d.astype(F32), axis=0) for d in d_up]
    g_up = gather_back([dot(h1_low, d_up[r], 0, 0) for r in quarters], width)
    d_h1 = d_r2 + sum(dot(d_up[r], w_up[r], 1, 1) for r in quarters)
    d_r1 = norm_back(d_h1, n1, inv1, mixing_normalizer_scale)
    g_first_gain = jnp.sum(d_h1 * n1, axis=0)
    g_first_shift = jnp.sum(d_h1, axis=0)
    g_out_bias = jnp.sum(d_r1, axis=0)
    d_attn = d_r1.astype(BF16)
    g_out = gather_back([dot(mixed[r], d_attn, 0, 0) for r in quarters], width)
    d_tokens = d_r1
    g_qkv, g_head_bias = [], []
    for r in quarters:
        d_mixed = dot(d_attn, w_out[r], 1, 1).astype(BF16)
        d_q, d_k, d_v = attention_back(qs[r], ks[r], vs[r], lses[r], d_mixed, same)
        d_proj = (d_q, d_k, d_v)
        g_qkv.append(jnp.stack([dot(x, d, 0, 0) for d in d_proj]))
        g_head_bias.append(
            jnp.concatenate([jnp.sum(d_q.astype(F32), axis=0), jnp.sum(d_v.astype(F32), axis=0)])
        )
        d_tokens = d_tokens + sum(dot(d_proj[k], w_qkv[r][k], 1, 1) for k in range(3))
    g_qkv = gather_back(g_qkv, width)
    grad_tokens = lax.all_gather(d_tokens.astype(BF16), "mp", axis=0, tiled=True).astype(F32)

    def over_dp(part):
        return lax.psum(part.astype(BF16), "dp").astype(F32)

    whole = jnp.stack(
        [g_out_bias, g_first_gain, g_first_shift, g_down_bias, g_second_gain, g_second_shift]
    )
    split = jnp.zeros((width, 1, 2 * feat + g_up_bias[0].shape[0]), F32)
    for r in quarters:
        split = lax.dynamic_update_slice(
            split, jnp.concatenate([g_head_bias[r], g_up_bias[r]])[None, None], (me ^ r, 0, 0)
        )
    whole, split = lax.psum((whole, split), everyone)
    mine = lax.dynamic_slice_in_dim(split, me, 1, 0)[0, 0]
    return (
        layer_out,
        seg_loss,
        grad_tokens,
        over_dp(g_qkv),
        mine[: 2 * feat].reshape(2, feat),
        over_dp(g_out),
        whole[0],
        whole[1],
        whole[2],
        over_dp(g_up),
        mine[2 * feat :],
        over_dp(g_down),
        whole[3],
        whole[4],
        whole[5],
        sharpness_derivative,
    )


def solution(mesh):
    in_specs = (
        P("dp", None),
        P("dp", None),
        P(None, None, "mp"),
        P(None, "mp"),
        P("mp", None),
        P(),
        P(),
        P(),
        P(None, "mp"),
        P("mp"),
        P("mp", None),
        P(),
        P(),
        P(),
        P(("dp", "mp"), None),
        P(),
        P(),
        P("dp", None),
    )
    out_specs = (
        P("dp", None),
        P(),
        P("dp", None),
        P(None, None, "mp"),
        P(None, "mp"),
        P("mp", None),
        P(),
        P(),
        P(),
        P(None, "mp"),
        P("mp"),
        P("mp", None),
        P(),
        P(),
        P(),
        P(),
    )
    width = mesh.shape["mp"]

    def step(*args):
        return local(*args, width=width, depth=mesh.shape["dp"])

    return jax.shard_map(step, mesh=mesh, in_specs=in_specs, out_specs=out_specs, check_vma=False)
```

```python
import functools

import jax
import jax.numpy as jnp
from jax import lax
from jax.experimental import pallas as pl
from jax.experimental.pallas import tpu as pltpu
from jax.sharding import PartitionSpec as P

HEAD = 64
F32 = jnp.float32
BF16 = jnp.bfloat16
MESH = pl.DeviceIdType.MESH
norm_epsilon = 1e-05
masked_score = -1e30


def dot(a, b, ca, cb):
    return lax.dot_general(a, b, (((ca,), (cb,)), ((), ())), preferred_element_type=F32)


def norm_stats(resid):
    centre = jnp.mean(resid, axis=-1, keepdims=True)
    centred = resid - centre
    spread = jnp.mean(centred * centred, axis=-1, keepdims=True)
    inv = lax.rsqrt(spread + norm_epsilon)
    return centred * inv, inv


def norm_back(d_out, normed, inv, gain):
    e = d_out * gain
    return inv * (
        e - jnp.mean(e, axis=-1, keepdims=True) - normed * jnp.mean(e * normed, axis=-1, keepdims=True)
    )


def swap(value, width, distance):
    return lax.ppermute(value, "mp", [(i, i ^ distance) for i in range(width)])


def spread_over_mp(own, width):
    held = [own]
    order = [0]
    step = width // 2
    while step:
        held = held + [swap(h, width, step) for h in held]
        order = order + [o ^ step for o in order]
        step //= 2
    return [held[order.index(r)] for r in range(width)]


def retrieval_kernel(
    ndp, nmp, query_ref, docs_hbm, gold_ref, sharp_ref, dq_ref, loss_ref, ds_ref,
    queries, docs, low, stats, columns, part_u, part_g, send, got, doc_sem, q_send, q_recv, s_send, s_recv, d_send, d_recv,
):
    n = ndp * nmp
    own = query_ref.shape[0]
    nseg = gold_ref.shape[0]
    tile = 256 if nseg <= 256 else 128
    dp, mp = lax.axis_index("dp"), lax.axis_index("mp")
    me = dp * nmp + mp
    load = pltpu.make_async_copy(docs_hbm, docs, doc_sem)
    load.start()
    barrier = pltpu.get_barrier_semaphore()

    def device(step):
        other = lax.rem(me + step, n)
        return other, (other // nmp, lax.rem(other, nmp))

    @pl.loop(1, n)
    def _(step):
        _, where = device(step)
        pl.semaphore_signal(barrier, inc=1, device_id=where, device_id_type=MESH)

    pl.semaphore_wait(barrier, n - 1)

    def push(source, target, send_sems, recv_sems):
        @pl.loop(1, n)
        def _(step):
            other, where = device(step)
            pltpu.make_async_remote_copy(
                source(other), target, send_sems.at[step], recv_sems.at[step], device_id=where, device_id_type=MESH
            ).start()

    def drain(source, target, send_sems, recv_sems):
        @pl.loop(1, n)
        def _(step):
            other, where = device(step)
            copy = pltpu.make_async_remote_copy(
                source(other), target, send_sems.at[step], recv_sems.at[step], device_id=where, device_id_type=MESH
            )
            copy.wait()

    push(lambda other: query_ref, queries.at[me], q_send, q_recv)
    queries[me] = query_ref[...]
    drain(lambda other: query_ref, queries.at[me], q_send, q_recv)
    load.wait()

    sharp = sharp_ref[0]
    offset = me * docs.shape[0]
    ids = lax.broadcasted_iota(jnp.int32, (tile, docs.shape[0]), 1)
    lane = lax.broadcasted_iota(jnp.int32, (tile, 128), 1)
    per = tile // own

    @pl.loop(0, nseg // tile)
    def _(i):
        span = pl.ds(pl.multiple_of(i * tile, tile), tile)
        q = queries[pl.ds(i * per, per)].reshape(tile, queries.shape[2])
        logit = lax.dot_general(q, docs[...], (((1,), (1,)), ((), ())), preferred_element_type=F32) / sharp
        match = ids == gold_ref[span, :] - offset
        top = jnp.max(logit, axis=1, keepdims=True)
        expo = jnp.exp(logit - top)
        total = jnp.sum(expo, axis=1, keepdims=True)
        tilt = jnp.sum(expo * logit, axis=1, keepdims=True)
        gold = jnp.sum(jnp.where(match, logit, 0.0), axis=1, keepdims=True)
        packed = jnp.where(lane == 0, top, jnp.where(lane == 1, total, jnp.where(lane == 2, tilt, gold)))
        stats[me, :, span] = packed.T[:4]
        low[span, :] = jnp.where(match, 0.0, expo).astype(BF16)

    push(lambda other: stats.at[me], stats.at[me], s_send, s_recv)

    @pl.loop(0, nseg // tile)
    def _(i):
        span = pl.ds(pl.multiple_of(i * tile, tile), tile)
        part_u[span, :] = jnp.dot(low[span, :], docs[...], preferred_element_type=F32)
        match = ids == gold_ref[span, :] - offset
        part_g[span, :] = jnp.dot(
            match.astype(F32).astype(BF16), docs[...], preferred_element_type=F32
        ).astype(BF16)

    drain(lambda other: stats.at[me], stats.at[me], s_send, s_recv)

    tops = stats[:, 0, :]
    top = jnp.max(tops, axis=0, keepdims=True)
    share = jnp.exp(tops - top)
    total = jnp.sum(stats[:, 1, :] * share, axis=0, keepdims=True)
    tilt = jnp.sum(stats[:, 2, :] * share, axis=0, keepdims=True)
    gold = jnp.sum(stats[:, 3, :], axis=0, keepdims=True)
    lse = top + jnp.log(total)
    loss_ref[...] = lse - gold
    ds_ref[...] = -jnp.sum(tilt / total - gold, axis=1, keepdims=True) / sharp
    scale = jnp.exp(stats[me, 0:1, :] - lse) / sharp
    gold_scale = (jnp.exp(gold - lse) - 1.0) / sharp
    row = lax.broadcasted_iota(jnp.int32, (128, nseg), 0)
    columns[...] = jnp.where(row == 0, scale, gold_scale).T

    @pl.loop(0, nseg // tile)
    def _(i):
        span = pl.ds(pl.multiple_of(i * tile, tile), tile)
        value = part_u[span, :] * columns[span, 0:1] + part_g[span, :].astype(F32) * columns[span, 1:2]
        send[pl.ds(i * per, per)] = value.astype(BF16).reshape(per, own, value.shape[1])

    push(lambda other: send.at[other], got.at[me], d_send, d_recv)
    got[me] = send[me]
    drain(lambda other: send.at[other], got.at[me], d_send, d_recv)
    dq_ref[...] = jnp.sum(got[...].astype(F32), axis=0)


def retrieval(query, docs, gold, sharp, ndp, nmp):
    n = ndp * nmp
    own, width = query.shape
    nseg = gold.shape[0]
    vmem = pl.BlockSpec(memory_space=pltpu.VMEM)
    return pl.pallas_call(
        functools.partial(retrieval_kernel, ndp, nmp),
        out_shape=(
            jax.ShapeDtypeStruct((own, width), F32),
            jax.ShapeDtypeStruct((1, nseg), F32),
            jax.ShapeDtypeStruct((1, 1), F32),
        ),
        in_specs=[vmem, pl.BlockSpec(memory_space=pl.ANY), vmem, pl.BlockSpec(memory_space=pltpu.SMEM)],
        out_specs=(vmem, vmem, vmem),
        scratch_shapes=[
            pltpu.VMEM((n, own, width), BF16),
            pltpu.VMEM(docs.shape, BF16),
            pltpu.VMEM((nseg, docs.shape[0]), BF16),
            pltpu.VMEM((n, 4, nseg), F32),
            pltpu.VMEM((nseg, 128), F32),
            pltpu.VMEM((nseg, width), F32),
            pltpu.VMEM((nseg, width), BF16),
            pltpu.VMEM((n, own, width), BF16),
            pltpu.VMEM((n, own, width), BF16),
            pltpu.SemaphoreType.DMA,
        ]
        + [pltpu.SemaphoreType.DMA((n,))] * 6,
        compiler_params=pltpu.CompilerParams(
            collective_id=0, has_side_effects=True, vmem_limit_bytes=60 * 2**20
        ),
        name="retrieval",
    )(query, docs, gold, sharp)


def attention(q, k, v, same):
    rows, feat = q.shape
    heads = feat // HEAD
    shape = (rows, heads, HEAD)
    scores = jnp.einsum("qhe,khe->hqk", q.reshape(shape), k.reshape(shape), preferred_element_type=F32)
    scores = jnp.where(same[None], scores * HEAD ** (-0.5), masked_score)
    top = jnp.max(scores, axis=-1, keepdims=True)
    expo = jnp.exp(scores - top)
    total = jnp.sum(expo, axis=-1, keepdims=True)
    probs = (expo / total).astype(BF16)
    mixed = jnp.einsum("hqk,khe->qhe", probs, v.reshape(shape), preferred_element_type=F32)
    return mixed.reshape(rows, feat).astype(BF16)


def attention_back_kernel(
    q_ref, k_ref, v_ref, mixed_ref, d_attn_ref, x_ref, w_out_ref, w_qkv_ref, seg_ref, seg_row_ref, tokens_ref,
    weights_ref, bias_ref, d_tokens_ref, d_proj,
):
    feat = q_ref.shape[1]
    d_attn = d_attn_ref[...]
    d_mixed = dot(d_attn, w_out_ref[...], 1, 1).astype(BF16)
    same = seg_ref[...] == seg_row_ref[...]
    scale = HEAD ** (-0.5)
    for h in range(feat // HEAD):
        lanes = slice(h * HEAD, (h + 1) * HEAD)
        q = q_ref[:, lanes] * BF16(scale)
        k = k_ref[:, lanes]
        v = v_ref[:, lanes]
        d_o = d_mixed[:, lanes]
        scores = jnp.where(same, dot(q, k, 1, 1), masked_score)
        expo = jnp.exp(scores - jnp.max(scores, axis=1, keepdims=True))
        probs = expo * (1.0 / jnp.sum(expo, axis=1, keepdims=True))
        d_p = dot(d_o, v, 1, 1)
        d_s = probs * (d_p - jnp.sum(d_p * probs, axis=1, keepdims=True))
        d_s = d_s.astype(BF16)
        d_proj[:, h * HEAD : (h + 1) * HEAD] = (dot(d_s, k, 1, 0) * scale).astype(BF16)
        d_proj[:, feat + h * HEAD : feat + (h + 1) * HEAD] = dot(d_s, q, 0, 0).astype(BF16)
        d_proj[:, 2 * feat + h * HEAD : 2 * feat + (h + 1) * HEAD] = dot(probs.astype(BF16), d_o, 0, 0).astype(BF16)
    weights_ref[:feat] = dot(mixed_ref[...], d_attn, 0, 0).astype(BF16)
    weights_ref[feat:] = dot(d_proj[...], x_ref[...], 0, 0).astype(BF16)
    bias_ref[...] = jnp.sum(d_proj[...].astype(F32), axis=0, keepdims=True)
    tokens = tokens_ref[...]
    for j in range(3):
        tokens = tokens + dot(d_proj[:, j * feat : (j + 1) * feat], w_qkv_ref[j], 1, 1)
    d_tokens_ref[...] = tokens


def attention_back(q, k, v, mixed, d_attn, x, w_out, w_qkv, seg, tokens):
    rows, feat = q.shape
    wide = x.shape[1]
    vmem = pl.BlockSpec(memory_space=pltpu.VMEM)
    return pl.pallas_call(
        attention_back_kernel,
        out_shape=(
            jax.ShapeDtypeStruct((4 * feat, wide), BF16),
            jax.ShapeDtypeStruct((1, 3 * feat), F32),
            jax.ShapeDtypeStruct((rows, wide), F32),
        ),
        in_specs=[vmem] * 11,
        out_specs=(vmem,) * 3,
        scratch_shapes=[pltpu.VMEM((rows, 3 * feat), BF16)],
        compiler_params=pltpu.CompilerParams(vmem_limit_bytes=40 * 2**20),
        cost_estimate=pl.CostEstimate(
            flops=8 * rows * wide * feat * 2, bytes_accessed=8 * 2**20, transcendentals=feat // HEAD * rows * rows
        ),
        name="attention_back",
    )(q, k, v, mixed, d_attn, x, w_out, w_qkv, seg[:, None], seg[None], tokens)


PIECES = 8
CHUNKS = 6


def flip(index, step):
    return index + step * (1 - 2 * lax.rem(index // step, 2))


def reduce_kernel(ndp, nmp, kinds, *refs):
    parts = [refs[k * nmp : (k + 1) * nmp] for k in range(kinds)]
    refs = refs[kinds * nmp :]
    vec_ref, tok_ref, out, vec_out, tok = refs[:5]
    (
        near, mine, theirs, got_y, got_x, got_1, got_2, got_e, vec_a, vec_b, vec_s, vec_r,
        a_s, a_r, y_s, y_r, x_s, x_r, p_s, p_r, q_s, q_r, e_s, e_r, gq_s, gq_r, gp_s, gp_r, gx_s, gx_r,
        va_s, va_r, v_s, v_r, t_s, t_r, own_sem,
    ) = refs[5:]
    total = kinds * CHUNKS
    bits = ndp.bit_length() - 1
    extra = bits - 3
    dp, mp = lax.axis_index("dp"), lax.axis_index("mp")
    near_dev, far_dev = (dp, flip(mp, 1)), (dp, flip(mp, 2))
    dp_dev = [(flip(dp, 1 << b), mp) for b in range(bits)]
    b0, b1, b2 = (lax.rem(dp // (1 << b), 2) for b in range(3))
    ident = b0 * 4 + b1 * 2 + b2

    barrier = pltpu.get_barrier_semaphore()
    for where in [near_dev, far_dev] + dp_dev:
        pl.semaphore_signal(barrier, inc=1, device_id=where, device_id_type=MESH)
    pl.semaphore_wait(barrier, 2 + bits)

    def remote(source, target, send, recv, where):
        return pltpu.make_async_remote_copy(
            source, target, send, recv, device_id=where, device_id_type=MESH
        )

    def near_copy(k, j):
        return remote(parts[k][2 * j + 1], near.at[k, j], a_s.at[2 * k + j], a_r.at[2 * k + j], near_dev)

    def far_copy(c):
        return remote(theirs.at[c], got_y.at[c], y_s.at[c], y_r.at[c], far_dev)

    def x_copy(c):
        return remote(mine.at[c, pl.ds((1 - b0) * 4, 4)], got_x.at[c], x_s.at[c], x_r.at[c], dp_dev[0])

    def p_copy(c):
        return remote(mine.at[c, pl.ds(b0 * 4 + (1 - b1) * 2, 2)], got_1.at[c], p_s.at[c], p_r.at[c], dp_dev[1])

    def q_copy(c):
        return remote(mine.at[c, ident + 1 - 2 * b2], got_2.at[c], q_s.at[c], q_r.at[c], dp_dev[2])

    def e_copy(c, e):
        return remote(mine.at[c, ident], got_e.at[e, c], e_s.at[e, c], e_r.at[e, c], dp_dev[3 + e])

    def gq_copy(c):
        return remote(out.at[c, ident], out.at[c, ident], gq_s.at[c], gq_r.at[c], dp_dev[2])

    def gp_copy(c):
        span = pl.ds(b0 * 4 + b1 * 2, 2)
        return remote(out.at[c, span], out.at[c, span], gp_s.at[c], gp_r.at[c], dp_dev[1])

    def gx_copy(c):
        span = pl.ds(b0 * 4, 4)
        return remote(out.at[c, span], out.at[c, span], gx_s.at[c], gx_r.at[c], dp_dev[0])

    vec_near = [remote(vec_ref.at[2 * j + 1], vec_a.at[j], va_s.at[j], va_r.at[j], near_dev) for j in range(2)]
    vec_far = remote(vec_b, vec_r.at[0], v_s.at[0], v_r.at[0], far_dev)
    vec_dp = [
        remote(vec_s.at[b], vec_r.at[1 + b], v_s.at[1 + b], v_r.at[1 + b], dp_dev[b]) for b in range(bits)
    ]
    tok_near = remote(tok_ref, tok.at[mp], t_s.at[0], t_r.at[0], near_dev)
    tok_far = remote(tok_ref, tok.at[mp], t_s.at[1], t_r.at[1], far_dev)
    other = flip(mp, 2)
    tok_pass = remote(tok.at[other], tok.at[other], t_s.at[2], t_r.at[2], near_dev)
    tok_own = pltpu.make_async_copy(tok_ref, tok.at[mp], own_sem)

    for copy in vec_near:
        copy.start()
    for k in range(kinds):
        for j in range(2):
            near_copy(k, j).start()
    tok_near.start()
    tok_own.start()
    for copy in vec_near:
        copy.wait_recv()
    vec_b[...] = vec_ref[2] + vec_a[1]
    vec_far.start()
    vec_s[0] = vec_ref[0] + vec_a[0]

    def add(a, b):
        return (a.astype(F32) + b.astype(F32)).astype(BF16)

    def first(k):
        for j in range(2):
            near_copy(k, j).wait_recv()

        @pl.loop(0, CHUNKS)
        def _(i):
            c = k * CHUNKS + i
            theirs[c] = add(parts[k][2][i], near[k, 1, i])
            far_copy(c).start()
            mine[c] = add(parts[k][0][i], near[k, 0, i])

    first(0)
    last = 6 + extra
    for t in range(kinds):
        if t + 1 < kinds:
            first(t + 1)
        elif True:
            tok_far.start()

        @pl.loop(t * CHUNKS, (t + 1) * CHUNKS + (last if t == kinds - 1 else 0))
        def _(i):
            def at(lag, do):
                @pl.when((i >= lag) & (i - lag < total))
                def _():
                    do(i - lag)

            @functools.partial(at, last)
            def _(c):
                gx_copy(c).wait_recv()

            @functools.partial(at, last - 1)
            def _(c):
                gp_copy(c).wait_recv()
                gx_copy(c).start()

            @functools.partial(at, last - 2)
            def _(c):
                gq_copy(c).wait_recv()
                gp_copy(c).start()

            for e in reversed(range(extra)):
                @functools.partial(at, 4 + e)
                def _(c, e=e):
                    e_copy(c, e).wait()
                    mine[c, ident] = add(mine[c, ident], got_e[e, c])
                    if e + 1 < extra:
                        e_copy(c, e + 1).start()
                    else:
                        out[c, ident] = mine[c, ident]
                        gq_copy(c).start()

            @functools.partial(at, 3)
            def _(c):
                q_copy(c).wait_recv()
                value = add(mine[c, ident], got_2[c])
                if extra:
                    mine[c, ident] = value
                    e_copy(c, 0).start()
                else:
                    out[c, ident] = value
                    gq_copy(c).start()

            @functools.partial(at, 2)
            def _(c):
                p_copy(c).wait_recv()
                span = pl.ds(b0 * 4 + b1 * 2, 2)
                mine[c, span] = add(mine[c, span], got_1[c])
                q_copy(c).start()

            @functools.partial(at, 1)
            def _(c):
                x_copy(c).wait_recv()
                span = pl.ds(b0 * 4, 4)
                mine[c, span] = add(mine[c, span], got_x[c])
                p_copy(c).start()

            @functools.partial(at, 0)
            def _(c):
                far_copy(c).wait_recv()
                mine[c] = add(mine[c], got_y[c])
                x_copy(c).start()

        if t == 0:
            vec_far.wait()
            vec_s[0] = vec_s[0] + vec_r[0]
            vec_dp[0].start()
        if t == 1:
            for b in range(bits):
                vec_dp[b].wait()
                value = vec_s[b] + vec_r[1 + b]
                if b + 1 < bits:
                    vec_s[b + 1] = value
                    vec_dp[b + 1].start()
                else:
                    vec_out[...] = value

    tok_far.wait_recv()
    tok_pass.start()
    for copy in vec_near:
        copy.wait_send()
    for k in range(kinds):
        for j in range(2):
            near_copy(k, j).wait_send()

    @pl.loop(0, total)
    def _(c):
        for copy in (far_copy, x_copy, p_copy, q_copy, gq_copy, gp_copy, gx_copy):
            copy(c).wait_send()

    tok_near.wait()
    tok_far.wait_send()
    tok_own.wait()
    tok_pass.wait()


def reduce_all(parts, vectors, tokens, ndp, nmp):
    kinds = len(parts)
    total = kinds * CHUNKS
    rows, wide = parts[0][0].shape
    small = rows // (CHUNKS * PIECES)
    bits = ndp.bit_length() - 1
    extra = bits - 3
    flat = [p.reshape(CHUNKS, PIECES, small, wide) for kind in parts for p in kind]
    vmem = pl.BlockSpec(memory_space=pltpu.VMEM)
    dma = pltpu.SemaphoreType.DMA

    def buffer(*lead):
        return pltpu.VMEM(lead + (small, wide), BF16)

    pair = lambda *shape: [dma(shape), dma(shape)]
    out = pl.pallas_call(
        functools.partial(reduce_kernel, ndp, nmp, kinds),
        out_shape=(
            jax.ShapeDtypeStruct((total, PIECES, small, wide), BF16),
            jax.ShapeDtypeStruct(vectors.shape[1:], F32),
            jax.ShapeDtypeStruct((nmp,) + tokens.shape, BF16),
        ),
        in_specs=[vmem] * (len(flat) + 2),
        out_specs=(vmem,) * 3,
        scratch_shapes=[
            buffer(kinds, 2, CHUNKS, PIECES),
            buffer(total, PIECES),
            buffer(total, PIECES),
            buffer(total, PIECES),
            buffer(total, 4),
            buffer(total, 2),
            buffer(total),
            buffer(max(extra, 1), total),
            pltpu.VMEM((2,) + vectors.shape[1:], F32),
            pltpu.VMEM(vectors.shape[1:], F32),
            pltpu.VMEM((bits,) + vectors.shape[1:], F32),
            pltpu.VMEM((bits + 1,) + vectors.shape[1:], F32),
        ]
        + pair(2 * kinds) + pair(total) * 4 + pair(max(extra, 1), total) + pair(total) * 3
        + pair(2) + pair(bits + 1) + pair(3) + [dma],
        compiler_params=pltpu.CompilerParams(
            collective_id=1, has_side_effects=True, vmem_limit_bytes=62 * 2**20
        ),
        name="reduce_all",
    )(*flat, vectors, tokens)
    return out[0].reshape(kinds, rows, wide), out[1], out[2].reshape(-1, wide)


def local(
    encoder_rows,
    piece_extent_sequence,
    triple_projection_matrix,
    asker_content_shifts,
    mixing_result_matrix,
    mixing_result_offset_vector,
    mixing_normalizer_scale,
    mixing_normalizer_shift,
    widen_matrix,
    widen_shift_vector,
    narrow_matrix,
    narrow_shift_vector,
    perceptron_normalizer_scale,
    perceptron_normalizer_shift,
    document_vectors,
    sharpness_factor,
    correct_document_position,
    upstream_sensitivity,
    *,
    width,
    depth,
):
    everyone = ("dp", "mp")
    me = lax.axis_index("mp")
    nblock, nseg_block = piece_extent_sequence.shape
    block = encoder_rows.shape[0] // nblock
    own_blocks = nblock // width
    rows = own_blocks * block
    feat = triple_projection_matrix.shape[2]
    quarters = range(width)

    x = lax.dynamic_slice_in_dim(encoder_rows, me * rows, rows, 0)
    upstream = lax.dynamic_slice_in_dim(upstream_sensitivity, me * rows, rows, 0)
    extents = lax.dynamic_slice_in_dim(piece_extent_sequence, me * own_blocks, own_blocks, 0)

    w_qkv = spread_over_mp(triple_projection_matrix, width)
    small = spread_over_mp(
        jnp.concatenate([asker_content_shifts.reshape(-1), widen_shift_vector])[None], width
    )
    w_out = spread_over_mp(mixing_result_matrix, width)
    w_up = spread_over_mp(widen_matrix, width)
    w_down = spread_over_mp(narrow_matrix, width)
    b_q = [s[:, :feat] for s in small]
    b_v = [s[:, feat : 2 * feat] for s in small]
    b_up = [s[:, 2 * feat :] for s in small]

    ends = jnp.cumsum(extents, axis=1)
    starts = ends - extents
    places = jnp.arange(rows, dtype=jnp.int32)
    base = (jnp.arange(own_blocks, dtype=jnp.int32) * block)[:, None]
    seg = jnp.sum((places[:, None] >= (ends + base).reshape(-1)[None]).astype(jnp.int32), axis=1)
    same = seg[:, None] == seg[None, :]
    firsts = (starts + base).reshape(-1)
    select = firsts[:, None] == places[None, :]
    pick = select.astype(BF16)

    qs, ks, vs, mixed = [], [], [], []
    for r in quarters:
        proj = jnp.einsum("td,kde->kte", x, w_qkv[r], preferred_element_type=F32)
        q = (proj[0] + b_q[r]).astype(BF16)
        k = proj[1].astype(BF16)
        v = (proj[2] + b_v[r]).astype(BF16)
        qs.append(q), ks.append(k), vs.append(v), mixed.append(attention(q, k, v, same))
    attn_out = sum(dot(mixed[r], w_out[r], 1, 0) for r in quarters)
    n1, inv1 = norm_stats(x.astype(F32) + attn_out + mixing_result_offset_vector)
    h1 = n1 * mixing_normalizer_scale + mixing_normalizer_shift
    h1_low = h1.astype(BF16)
    acts, slopes = [], []
    for r in quarters:
        upper = dot(h1_low, w_up[r], 1, 0) + b_up[r]
        act, back = jax.vjp(lambda u: jax.nn.gelu(u, approximate=False), upper)
        acts.append(act.astype(BF16))
        slopes.append(back(jnp.ones_like(upper))[0])
    ffn_out = sum(dot(acts[r], w_down[r], 1, 0) for r in quarters)
    n2, inv2 = norm_stats(h1 + ffn_out + narrow_shift_vector)
    h2 = n2 * perceptron_normalizer_scale + perceptron_normalizer_shift
    own_out = h2.astype(BF16)
    layer_out = jnp.zeros((encoder_rows.shape[0], own_out.shape[1]), BF16)
    for r, piece in enumerate(spread_over_mp(own_out, width)):
        layer_out = lax.dynamic_update_slice(layer_out, piece, ((me ^ r) * rows, 0))

    query = dot(pick, own_out, 1, 0).astype(BF16)
    d_query, seg_loss, sharpness_derivative = retrieval(
        query, document_vectors, correct_document_position[:, None], sharpness_factor, depth, width
    )
    seg_loss = seg_loss[0]
    sharpness_derivative = sharpness_derivative[0]
    d_h2 = upstream + lax.dot_general(
        select.astype(F32), d_query, (((0,), (0,)), ((), ())), precision=lax.Precision.HIGHEST
    )
    d_r2 = norm_back(d_h2, n2, inv2, perceptron_normalizer_scale)
    g_second_gain = jnp.sum(d_h2 * n2, axis=0)
    g_second_shift = jnp.sum(d_h2, axis=0)
    g_down_bias = jnp.sum(d_r2, axis=0)
    d_ffn = d_r2.astype(BF16)
    g_down = [dot(acts[r], d_ffn, 0, 0).astype(BF16) for r in quarters]
    d_up = [(dot(d_ffn, w_down[r], 1, 1) * slopes[r]).astype(BF16) for r in quarters]
    g_up_bias = [jnp.sum(d.astype(F32), axis=0) for d in d_up]
    g_up = [dot(h1_low, d_up[r], 0, 0).astype(BF16) for r in quarters]
    d_h1 = d_r2 + sum(dot(d_up[r], w_up[r], 1, 1) for r in quarters)
    d_r1 = norm_back(d_h1, n1, inv1, mixing_normalizer_scale)
    g_first_gain = jnp.sum(d_h1 * n1, axis=0)
    g_first_shift = jnp.sum(d_h1, axis=0)
    g_out_bias = jnp.sum(d_r1, axis=0)
    d_attn = d_r1.astype(BF16)
    d_tokens = d_r1
    g_attn, g_head_bias = [], []
    for r in quarters:
        weights, bias, d_tokens = attention_back(
            qs[r], ks[r], vs[r], mixed[r], d_attn, x, w_out[r], w_qkv[r], seg, d_tokens
        )
        g_attn.append(weights)
        g_head_bias.append(jnp.concatenate([bias[0, :feat], bias[0, 2 * feat :]]))
    whole = jnp.stack(
        [g_out_bias, g_first_gain, g_first_shift, g_down_bias, g_second_gain, g_second_shift]
    )
    hidden = g_up_bias[0].shape[0]
    wide = whole.shape[1]
    vectors = jnp.stack(
        [
            jnp.concatenate(
                [whole, jnp.pad(g_head_bias[r], (0, wide - 2 * feat))[None], jnp.pad(g_up_bias[r], (0, wide - hidden))[None]]
            )
            for r in quarters
        ]
    )
    sums, vectors, grad_tokens = reduce_all(
        [g_down, g_up, g_attn], vectors, d_tokens.astype(BF16), depth, width
    )
    grad_tokens = grad_tokens.astype(F32)
    sums = sums.astype(F32)
    grad_qkv = sums[2, feat:].reshape(3, feat, wide).transpose(0, 2, 1)
    return (
        layer_out,
        seg_loss,
        grad_tokens,
        grad_qkv,
        vectors[6, : 2 * feat].reshape(2, feat),
        sums[2, :feat],
        vectors[0],
        vectors[1],
        vectors[2],
        sums[1],
        vectors[7, :hidden],
        sums[0],
        vectors[3],
        vectors[4],
        vectors[5],
        sharpness_derivative,
    )


def solution(mesh):
    in_specs = (
        P("dp", None),
        P("dp", None),
        P(None, None, "mp"),
        P(None, "mp"),
        P("mp", None),
        P(),
        P(),
        P(),
        P(None, "mp"),
        P("mp"),
        P("mp", None),
        P(),
        P(),
        P(),
        P(("dp", "mp"), None),
        P(),
        P(),
        P("dp", None),
    )
    out_specs = (
        P("dp", None),
        P(),
        P("dp", None),
        P(None, None, "mp"),
        P(None, "mp"),
        P("mp", None),
        P(),
        P(),
        P(),
        P(None, "mp"),
        P("mp"),
        P("mp", None),
        P(),
        P(),
        P(),
        P(),
    )
    width = mesh.shape["mp"]

    def step(*args):
        return local(*args, width=width, depth=mesh.shape["dp"])

    return jax.shard_map(step, mesh=mesh, in_specs=in_specs, out_specs=out_specs, check_vma=False)
```

```python
import functools
import math

import jax
import jax.numpy as jnp
from jax import lax
from jax.experimental import pallas as pl
from jax.experimental.pallas import tpu as pltpu
from jax.sharding import PartitionSpec as P

HEAD = 64
F32 = jnp.float32
BF16 = jnp.bfloat16
MESH = pl.DeviceIdType.MESH
norm_epsilon = 1e-05
masked_score = -1e30


def dot(a, b, ca, cb):
    return lax.dot_general(a, b, (((ca,), (cb,)), ((), ())), preferred_element_type=F32)


def norm_stats(resid):
    centre = jnp.mean(resid, axis=-1, keepdims=True)
    centred = resid - centre
    spread = jnp.mean(centred * centred, axis=-1, keepdims=True)
    inv = lax.rsqrt(spread + norm_epsilon)
    return centred * inv, inv


def norm_back(d_out, normed, inv, gain):
    e = d_out * gain
    return inv * (
        e - jnp.mean(e, axis=-1, keepdims=True) - normed * jnp.mean(e * normed, axis=-1, keepdims=True)
    )


def swap(value, width, distance):
    return lax.ppermute(value, "mp", [(i, i ^ distance) for i in range(width)])


def spread_over_mp(own, width):
    held = [own]
    order = [0]
    step = width // 2
    while step:
        held = held + [swap(h, width, step) for h in held]
        order = order + [o ^ step for o in order]
        step //= 2
    return [held[order.index(r)] for r in range(width)]


def flip(index, step):
    return index + step * (1 - 2 * lax.rem(index // step, 2))


def retrieval_kernel(
    ndp, nmp, query_ref, docs_hbm, gold_ref, sharp_ref, dq_ref, loss_ref, ds_ref,
    queries, docs, low, stats, columns, part_u, part_g, send, got, doc_sem, q_send, q_recv, s_send, s_recv, d_send, d_recv,
):
    n = ndp * nmp
    own = query_ref.shape[0]
    nseg = gold_ref.shape[0]
    tile = 256 if nseg <= 256 else 128
    dp, mp = lax.axis_index("dp"), lax.axis_index("mp")
    me = dp * nmp + mp
    load = pltpu.make_async_copy(docs_hbm, docs, doc_sem)
    load.start()
    barrier = pltpu.get_barrier_semaphore()

    def device(step):
        other = lax.rem(me + step, n)
        return other, (other // nmp, lax.rem(other, nmp))

    @pl.loop(1, n)
    def _(step):
        _, where = device(step)
        pl.semaphore_signal(barrier, inc=1, device_id=where, device_id_type=MESH)

    pl.semaphore_wait(barrier, n - 1)

    def push(source, target, send_sems, recv_sems):
        @pl.loop(1, n)
        def _(step):
            other, where = device(step)
            pltpu.make_async_remote_copy(
                source(other), target, send_sems.at[step], recv_sems.at[step], device_id=where, device_id_type=MESH
            ).start()

    def drain(source, target, send_sems, recv_sems):
        @pl.loop(1, n)
        def _(step):
            other, where = device(step)
            copy = pltpu.make_async_remote_copy(
                source(other), target, send_sems.at[step], recv_sems.at[step], device_id=where, device_id_type=MESH
            )
            copy.wait()

    push(lambda other: query_ref, queries.at[me], q_send, q_recv)
    queries[me] = query_ref[...]
    drain(lambda other: query_ref, queries.at[me], q_send, q_recv)
    load.wait()

    sharp = sharp_ref[0]
    offset = me * docs.shape[0]
    ids = lax.broadcasted_iota(jnp.int32, (tile, docs.shape[0]), 1)
    lane = lax.broadcasted_iota(jnp.int32, (tile, 128), 1)
    per = tile // own

    @pl.loop(0, nseg // tile)
    def _(i):
        span = pl.ds(pl.multiple_of(i * tile, tile), tile)
        q = queries[pl.ds(i * per, per)].reshape(tile, queries.shape[2])
        logit = lax.dot_general(q, docs[...], (((1,), (1,)), ((), ())), preferred_element_type=F32) / sharp
        match = ids == gold_ref[span, :] - offset
        top = jnp.max(logit, axis=1, keepdims=True)
        expo = jnp.exp(logit - top)
        total = jnp.sum(expo, axis=1, keepdims=True)
        tilt = jnp.sum(expo * logit, axis=1, keepdims=True)
        gold = jnp.sum(jnp.where(match, logit, 0.0), axis=1, keepdims=True)
        packed = jnp.where(lane == 0, top, jnp.where(lane == 1, total, jnp.where(lane == 2, tilt, gold)))
        stats[me, :, span] = packed.T[:4]
        low[span, :] = jnp.where(match, 0.0, expo).astype(BF16)

    push(lambda other: stats.at[me], stats.at[me], s_send, s_recv)

    @pl.loop(0, nseg // tile)
    def _(i):
        span = pl.ds(pl.multiple_of(i * tile, tile), tile)
        part_u[span, :] = jnp.dot(low[span, :], docs[...], preferred_element_type=F32)
        match = ids == gold_ref[span, :] - offset
        part_g[span, :] = jnp.dot(
            match.astype(F32).astype(BF16), docs[...], preferred_element_type=F32
        ).astype(BF16)

    drain(lambda other: stats.at[me], stats.at[me], s_send, s_recv)

    tops = stats[:, 0, :]
    top = jnp.max(tops, axis=0, keepdims=True)
    share = jnp.exp(tops - top)
    total = jnp.sum(stats[:, 1, :] * share, axis=0, keepdims=True)
    tilt = jnp.sum(stats[:, 2, :] * share, axis=0, keepdims=True)
    gold = jnp.sum(stats[:, 3, :], axis=0, keepdims=True)
    lse = top + jnp.log(total)
    loss_ref[...] = lse - gold
    ds_ref[...] = -jnp.sum(tilt / total - gold, axis=1, keepdims=True) / sharp
    scale = jnp.exp(stats[me, 0:1, :] - lse) / sharp
    gold_scale = (jnp.exp(gold - lse) - 1.0) / sharp
    row = lax.broadcasted_iota(jnp.int32, (128, nseg), 0)
    columns[...] = jnp.where(row == 0, scale, gold_scale).T

    @pl.loop(0, nseg // tile)
    def _(i):
        span = pl.ds(pl.multiple_of(i * tile, tile), tile)
        value = part_u[span, :] * columns[span, 0:1] + part_g[span, :].astype(F32) * columns[span, 1:2]
        send[pl.ds(i * per, per)] = value.astype(BF16).reshape(per, own, value.shape[1])

    push(lambda other: send.at[other], got.at[me], d_send, d_recv)
    got[me] = send[me]
    drain(lambda other: send.at[other], got.at[me], d_send, d_recv)
    dq_ref[...] = jnp.sum(got[...].astype(F32), axis=0)


def retrieval(query, docs, gold, sharp, ndp, nmp):
    n = ndp * nmp
    own, width = query.shape
    nseg = gold.shape[0]
    vmem = pl.BlockSpec(memory_space=pltpu.VMEM)
    return pl.pallas_call(
        functools.partial(retrieval_kernel, ndp, nmp),
        out_shape=(
            jax.ShapeDtypeStruct((own, width), F32),
            jax.ShapeDtypeStruct((1, nseg), F32),
            jax.ShapeDtypeStruct((1, 1), F32),
        ),
        in_specs=[vmem, pl.BlockSpec(memory_space=pl.ANY), vmem, pl.BlockSpec(memory_space=pltpu.SMEM)],
        out_specs=(vmem, vmem, vmem),
        scratch_shapes=[
            pltpu.VMEM((n, own, width), BF16),
            pltpu.VMEM(docs.shape, BF16),
            pltpu.VMEM((nseg, docs.shape[0]), BF16),
            pltpu.VMEM((n, 4, nseg), F32),
            pltpu.VMEM((nseg, 128), F32),
            pltpu.VMEM((nseg, width), F32),
            pltpu.VMEM((nseg, width), BF16),
            pltpu.VMEM((n, own, width), BF16),
            pltpu.VMEM((n, own, width), BF16),
            pltpu.SemaphoreType.DMA,
        ]
        + [pltpu.SemaphoreType.DMA((n,))] * 6,
        compiler_params=pltpu.CompilerParams(
            collective_id=0, has_side_effects=True, vmem_limit_bytes=60 * 2**20
        ),
        name="retrieval",
    )(query, docs, gold, sharp)


def gelu_with_slope(u):
    z = jnp.abs(u) * (0.5**0.5)
    t = 1.0 / (1.0 + 0.5 * z)
    poly = 0.17087277
    for c in (
        -0.82215223, 1.48851587, -1.13520398, 0.27886807, -0.18628806, 0.09678418, 0.37409196, 1.00002368,
    ):
        poly = poly * t + c
    square = z * z
    tail = 0.5 * t * jnp.exp(poly * t - 1.26551223 - square)
    cdf = jnp.where(u < 0, tail, 1.0 - tail)
    return u * cdf, cdf + u * (jnp.exp(-square) * ((2 * math.pi) ** -0.5))


def encode_kernel(nmp, block, *refs):
    (
        rows_hbm, extents, w_qkv, w_out, w_up, w_down, small_ref, out_bias, gain1, shift1, down_bias, gain2, shift2,
    ) = refs[:13]
    (
        qkv_o, mixed_o, n1_o, inv1_o, n2_o, inv2_o, low_o, act_o, slope_o, w_qkv_o, w_out_o, w_up_o, w_down_o,
        own_o, query_o, x_o,
    ) = refs[13:29]
    (
        x, qkv, mixed, n1, n2, h1_low, act, slope, all_qkv, all_out, all_up, all_down, small, total,
        x_sem, save_sem, n_s, n_r, m_s, m_r, y_s, y_r, f_s, f_r, g_s, g_r, h_s, h_r, sm_s, sm_r,
    ) = refs[29:]
    dp, mp = lax.axis_index("dp"), lax.axis_index("mp")
    near, far, side = (dp, flip(mp, 1)), (dp, flip(mp, 2)), (flip(dp, 1), mp)
    b = lax.rem(dp, 2)
    rows = x.shape[0]
    feat = w_out.shape[0] * w_out.shape[1]
    scale = HEAD ** (-0.5)

    load = pltpu.make_async_copy(rows_hbm.at[pl.ds(pl.multiple_of(mp * rows, rows), rows)], x, x_sem)
    load.start()
    barrier = pltpu.get_barrier_semaphore()
    for where in (near, far, side):
        pl.semaphore_signal(barrier, inc=1, device_id=where, device_id_type=MESH)
    pl.semaphore_wait(barrier, 3)

    def remote(source, target, send, recv, where):
        return pltpu.make_async_remote_copy(source, target, send, recv, device_id=where, device_id_type=MESH)

    pieces = [(w_qkv.at[k], all_qkv, k) for k in range(3)] + [(w_out, all_out, None)]
    pieces += [(w_up.at[s], all_up, s) for s in range(w_up.shape[0])]
    pieces += [(w_down.at[s], all_down, s) for s in range(w_down.shape[0])]
    count = len(pieces)

    def slot(i, r):
        _, held, s = pieces[i]
        return held.at[r] if s is None else held.at[r, s]

    near_own = [remote(pieces[i][0], slot(i, 1), n_s.at[i], n_r.at[i], near) for i in range(count)]
    far_own = [remote(pieces[i][0].at[b], slot(i, 2).at[b], y_s.at[i], y_r.at[i], far) for i in range(count)]
    pass_side = [remote(slot(i, 2).at[b], slot(i, 2).at[b], f_s.at[i], f_r.at[i], side) for i in range(count)]
    pass_near = [remote(slot(i, 2).at[b], slot(i, 3).at[b], g_s.at[i], g_r.at[i], near) for i in range(count)]
    pass_other = [
        remote(slot(i, 2).at[1 - b], slot(i, 3).at[1 - b], h_s.at[i], h_r.at[i], near) for i in range(count)
    ]
    small_near = remote(small_ref, small.at[1], sm_s.at[0], sm_r.at[0], near)
    small_far = remote(small_ref, small.at[2], sm_s.at[1], sm_r.at[1], far)
    small_pass = remote(small.at[2], small.at[3], sm_s.at[2], sm_r.at[2], near)

    small_near.start()
    small_far.start()
    for i in range(count):
        far_own[i].start()
        near_own[i].start()
    small[0] = small_ref[...]
    saves = []

    def save(source, target):
        copy = pltpu.make_async_copy(source, target, save_sem.at[len(saves)])
        copy.start()
        saves.append(copy)

    for source, target in ((w_qkv, w_qkv_o), (w_out, w_out_o), (w_up, w_up_o), (w_down, w_down_o)):
        save(source, target.at[0])

    def relay(i):
        far_own[i].wait_recv()
        pass_side[i].start()
        pass_near[i].start()

    def relay_other(i):
        pass_side[i].wait_recv()
        pass_other[i].start()

    def last_arrived(i):
        pass_near[i].wait_recv()
        pass_other[i].wait_recv()

    iota_row = lax.broadcasted_iota(jnp.int32, (1, rows), 1)
    iota_col = lax.broadcasted_iota(jnp.int32, (rows, 1), 0)
    nblk = rows // block
    nseg = extents.shape[1]
    seg_row, seg_col = jnp.zeros_like(iota_row), jnp.zeros_like(iota_col)
    starts = []
    for i in range(nblk):
        end = jnp.int32(i * block)
        for j in range(nseg):
            starts.append(end)
            end = end + extents[mp * nblk + i, j]
            seg_row = seg_row + (iota_row >= end).astype(jnp.int32)
            seg_col = seg_col + (iota_col >= end).astype(jnp.int32)
    load.wait()
    save(x, x_o)

    def project(r):
        source = w_qkv if r == 0 else all_qkv.at[r]
        for k in range(3):
            value = jnp.dot(
                x[...], source[k].reshape(x.shape[1], feat), preferred_element_type=F32
            )
            if k == 0:
                value = value + small[r, 0:1, :feat]
            if k == 2:
                value = value + small[r, 1:2, :feat]
            qkv[r, k] = value.astype(BF16)
        save(qkv.at[r], qkv_o.at[r])

    def head(r, h):
        lanes = slice(h * HEAD, (h + 1) * HEAD)
        q = qkv[r, 0, :, lanes] * BF16(scale)
        scores = dot(q, qkv[r, 1, :, lanes], 1, 1)
        scores = jnp.where(seg_col == seg_row, scores, masked_score)
        expo = jnp.exp(scores - jnp.max(scores, axis=1, keepdims=True))
        probs = (expo * (1.0 / jnp.sum(expo, axis=1, keepdims=True))).astype(BF16)
        mixed[r, :, lanes] = jnp.dot(probs, qkv[r, 2, :, lanes], preferred_element_type=F32).astype(BF16)

    def mix(r, *between):
        for h in range(feat // HEAD):
            head(r, h)
            if h < len(between):
                between[h]()
        save(mixed.at[r], mixed_o.at[r])

    project(0)
    mix(0)
    for i in range(3):
        near_own[i].wait_recv()
    small_near.wait_recv()
    project(1)
    mix(1)
    small_far.wait_recv()
    small_pass.start()
    relay(0)
    relay(1)
    relay_other(0)
    relay(2)
    relay_other(1)
    relay(3)
    relay_other(2)
    project(2)
    save(all_qkv.at[2], w_qkv_o.at[2])
    save(all_qkv.at[1], w_qkv_o.at[1])

    def both(i):
        relay(i)
        relay_other(i - 1)

    mix(2, lambda: relay_other(3), lambda: relay(4))
    for i in range(3):
        last_arrived(i)
    small_pass.wait_recv()
    project(3)
    save(all_qkv.at[3], w_qkv_o.at[3])
    mix(3, lambda: both(5))
    near_own[3].wait_recv()
    last_arrived(3)
    attn = jnp.zeros((rows, x.shape[1]), F32)
    for r in range(4):
        w = w_out[...] if r == 0 else all_out[r]
        attn = attn + jnp.dot(mixed[r], w.reshape(feat, x.shape[1]), preferred_element_type=F32)
        if r:
            save(all_out.at[r], w_out_o.at[r])
    normed, inv = norm_stats(x[...].astype(F32) + attn + out_bias[...])
    n1[...] = normed
    save(n1, n1_o)
    inv1_o[...] = jnp.broadcast_to(inv, inv1_o.shape)
    h1 = normed * gain1[...] + shift1[...]
    total[...] = h1 + down_bias[...]
    h1_low[...] = h1.astype(BF16)
    save(h1_low, low_o)
    ups, downs = range(4, 4 + w_up.shape[0]), range(4 + w_up.shape[0], count)
    wide = x.shape[1]

    def widen(r):
        w = w_up[...] if r == 0 else all_up[r]
        upper = jnp.dot(h1_low[...], w.reshape(wide, -1), preferred_element_type=F32) + small[r, 2:3, :]
        value, gradient = gelu_with_slope(upper)
        act[r] = value.astype(BF16)
        slope[r] = gradient.astype(BF16)
        save(act.at[r], act_o.at[r])
        save(slope.at[r], slope_o.at[r])
        if r:
            save(all_up.at[r], w_up_o.at[r])

    def narrow(r):
        w = w_down[...] if r == 0 else all_down[r]
        total[...] += jnp.dot(act[r], w.reshape(-1, wide), preferred_element_type=F32)
        if r:
            save(all_down.at[r], w_down_o.at[r])

    both(6)
    widen(0)
    both(7)
    narrow(0)
    for i in ups:
        near_own[i].wait_recv()
    widen(1)
    both(8)
    for i in downs:
        near_own[i].wait_recv()
    narrow(1)
    widen(2)
    both(9)
    for i in ups:
        last_arrived(i)
    widen(3)
    relay_other(9)
    narrow(2)
    for i in downs:
        last_arrived(i)
    narrow(3)
    normed, inv = norm_stats(total[...])
    n2[...] = normed
    save(n2, n2_o)
    inv2_o[...] = jnp.broadcast_to(inv, inv2_o.shape)
    own = (normed * gain2[...] + shift2[...]).astype(BF16)
    own_o[...] = own
    line = lax.broadcasted_iota(jnp.int32, (len(starts), rows), 0)
    first = jnp.zeros((len(starts), rows), jnp.int32)
    for j, start in enumerate(starts):
        first = jnp.where(line == j, start, first)
    pick = (lax.broadcasted_iota(jnp.int32, first.shape, 1) == first).astype(F32).astype(BF16)
    query_o[...] = jnp.dot(pick, own, preferred_element_type=F32).astype(BF16)
    for copy in saves:
        copy.wait()
    for copy in near_own + far_own + pass_side + pass_near + pass_other + [small_near, small_far, small_pass]:
        copy.wait_send()


STRIPS = 3


def encode(
    encoder_rows, extents, w_qkv, w_out, w_up, w_down, small, out_bias, gain1, shift1, down_bias, gain2, shift2,
    block, nmp,
):
    rows = encoder_rows.shape[0] // nmp
    wide = encoder_rows.shape[1]
    feat, hidden = w_qkv.shape[2], w_up.shape[1]
    nseg = extents.shape[0] * extents.shape[1] // nmp
    cut_qkv = w_qkv.reshape(3, 2, wide // 2, feat)
    cut_out = w_out.reshape(2, feat // 2, wide)
    cut_up = w_up.reshape(STRIPS, 2, wide // (2 * STRIPS), hidden)
    cut_down = w_down.reshape(STRIPS, 2, hidden // (2 * STRIPS), wide)
    vmem, anywhere = pl.BlockSpec(memory_space=pltpu.VMEM), pl.BlockSpec(memory_space=pl.ANY)
    sds = jax.ShapeDtypeStruct
    dma = pltpu.SemaphoreType.DMA
    every = lambda a: (nmp,) + a.shape
    held = [
        sds((nmp, 3, rows, feat), BF16),
        sds((nmp, rows, feat), BF16),
        sds((rows, wide), F32),
        sds((rows, 128), F32),
        sds((rows, wide), F32),
        sds((rows, 128), F32),
        sds((rows, wide), BF16),
        sds((nmp, rows, hidden), BF16),
        sds((nmp, rows, hidden), BF16),
        sds(every(cut_qkv), BF16),
        sds(every(cut_out), BF16),
        sds(every(cut_up), BF16),
        sds(every(cut_down), BF16),
        sds((rows, wide), BF16),
        sds((nseg, wide), BF16),
        sds((rows, wide), BF16),
    ]
    count = 4 + 2 * STRIPS
    scratch = [
        pltpu.VMEM((rows, wide), BF16),
        pltpu.VMEM(held[0].shape, BF16),
        pltpu.VMEM(held[1].shape, BF16),
        pltpu.VMEM((rows, wide), F32),
        pltpu.VMEM((rows, wide), F32),
        pltpu.VMEM((rows, wide), BF16),
        pltpu.VMEM(held[7].shape, BF16),
        pltpu.VMEM(held[8].shape, BF16),
    ]
    scratch += [pltpu.VMEM(h.shape, BF16) for h in held[9:13]]
    scratch += [pltpu.VMEM(every(small), F32), pltpu.VMEM((rows, wide), F32), dma, dma((40,))]
    scratch += [dma((count,))] * 12 + [dma((3,))] * 2
    vectors = [v[None] for v in (out_bias, gain1, shift1, down_bias, gain2, shift2)]
    outs = pl.pallas_call(
        functools.partial(encode_kernel, nmp, block),
        out_shape=tuple(held),
        in_specs=[anywhere, pl.BlockSpec(memory_space=pltpu.SMEM)] + [vmem] * 11,
        out_specs=tuple(vmem if i in (3, 5, 13, 14) else anywhere for i in range(len(held))),
        scratch_shapes=scratch,
        compiler_params=pltpu.CompilerParams(collective_id=2, has_side_effects=True, vmem_limit_bytes=62 * 2**20),
        name="encode",
    )(encoder_rows, extents, cut_qkv, cut_out, cut_up, cut_down, small, *vectors)
    outs = list(outs)
    outs[9] = outs[9].reshape(nmp, 3, wide, feat)
    outs[10] = outs[10].reshape(nmp, feat, wide)
    outs[11] = outs[11].reshape(nmp, wide, hidden)
    outs[12] = outs[12].reshape(nmp, hidden, wide)
    return outs


def ffn_back_kernel(
    upstream, d_query, extents, n1, inv1, n2, inv2, gain1, gain2, h1_low, act, slope, w_up, w_down,
    down_o, up_o, sums_o, bias_o, d_r1_o, d_attn_o, d_ffn, d_h1, *, block,
):
    r = pl.program_id(0)
    rows = upstream.shape[0]

    @pl.when(r == 0)
    def _():
        mp = lax.axis_index("mp")
        nblk = rows // block
        line = lax.broadcasted_iota(jnp.int32, (rows, 1), 0)
        d_h2 = upstream[...]
        for i in range(nblk):
            start = jnp.int32(i * block)
            for j in range(extents.shape[1]):
                d_h2 = d_h2 + jnp.where(line == start, d_query[i * extents.shape[1] + j, :][None], 0.0)
                start = start + extents[mp * nblk + i, j]
        sums_o[5:6] = jnp.sum(d_h2, axis=0, keepdims=True)
        sums_o[4:5] = jnp.sum(d_h2 * n2[...], axis=0, keepdims=True)
        d_r2 = norm_back(d_h2, n2[...], inv2[:, 0:1], gain2[...])
        sums_o[3:4] = jnp.sum(d_r2, axis=0, keepdims=True)
        d_ffn[...] = d_r2.astype(BF16)
        d_h1[...] = d_r2

    down_o[0] = dot(act[0], d_ffn[...], 0, 0).astype(BF16)
    d_up = (dot(d_ffn[...], w_down[0], 1, 1) * slope[0].astype(F32)).astype(BF16)
    bias_o[0] = jnp.sum(d_up.astype(F32), axis=0, keepdims=True)
    up_o[0] = dot(h1_low[...], d_up, 0, 0).astype(BF16)
    d_h1[...] += dot(d_up, w_up[0], 1, 1)

    @pl.when(r == pl.num_programs(0) - 1)
    def _():
        grad = d_h1[...]
        sums_o[2:3] = jnp.sum(grad, axis=0, keepdims=True)
        sums_o[1:2] = jnp.sum(grad * n1[...], axis=0, keepdims=True)
        d_r1 = norm_back(grad, n1[...], inv1[:, 0:1], gain1[...])
        sums_o[0:1] = jnp.sum(d_r1, axis=0, keepdims=True)
        d_r1_o[...] = d_r1
        d_attn_o[...] = d_r1.astype(BF16)


def whole(shape, grid=True):
    return pl.BlockSpec(shape, lambda r: (0,) * len(shape))


def quarter(shape):
    return pl.BlockSpec((1,) + shape[1:], lambda r: (r,) + (0,) * (len(shape) - 1))


def ffn_back(upstream, d_query, extents, n1, inv1, n2, inv2, gain1, gain2, h1_low, act, slope, w_up, w_down, block):
    nmp, rows, hidden = act.shape
    wide = n1.shape[1]
    sds = jax.ShapeDtypeStruct
    out = (
        sds((nmp, hidden, wide), BF16),
        sds((nmp, wide, hidden), BF16),
        sds((6, wide), F32),
        sds((nmp, 1, hidden), F32),
        sds((rows, wide), F32),
        sds((rows, wide), BF16),
    )
    gains = [gain1[None], gain2[None]]
    return pl.pallas_call(
        functools.partial(ffn_back_kernel, block=block),
        grid=(nmp,),
        out_shape=out,
        in_specs=[
            pl.BlockSpec((rows, wide), lambda r: (lax.axis_index("mp"), 0)),
            whole(d_query.shape),
            pl.BlockSpec(memory_space=pltpu.SMEM),
        ]
        + [whole(a.shape) for a in (n1, inv1, n2, inv2, *gains, h1_low)]
        + [quarter(a.shape) for a in (act, slope, w_up, w_down)],
        out_specs=[quarter(out[0].shape), quarter(out[1].shape), whole(out[2].shape), quarter(out[3].shape)]
        + [whole(out[4].shape), whole(out[5].shape)],
        scratch_shapes=[pltpu.VMEM((rows, wide), BF16), pltpu.VMEM((rows, wide), F32)],
        compiler_params=pltpu.CompilerParams(vmem_limit_bytes=56 * 2**20),
        cost_estimate=pl.CostEstimate(
            flops=8 * nmp * rows * wide * hidden, bytes_accessed=40 * 2**20, transcendentals=0
        ),
        name="ffn_back",
    )(upstream, d_query, extents, n1, inv1, n2, inv2, *gains, h1_low, act, slope, w_up, w_down)


def attention_back_kernel(
    qkv, mixed, d_attn_ref, d_r1, x_ref, w_out, w_qkv, extents, weights_o, bias_o, tokens_o, d_proj, tokens, *, block
):
    r = pl.program_id(0)
    rows, feat = mixed.shape[1:]
    mp = lax.axis_index("mp")
    nblk = rows // block
    iota_row = lax.broadcasted_iota(jnp.int32, (1, rows), 1)
    iota_col = lax.broadcasted_iota(jnp.int32, (rows, 1), 0)
    seg_row, seg_col = jnp.zeros_like(iota_row), jnp.zeros_like(iota_col)
    for i in range(nblk):
        end = jnp.int32(i * block)
        for j in range(extents.shape[1]):
            end = end + extents[mp * nblk + i, j]
            seg_row = seg_row + (iota_row >= end).astype(jnp.int32)
            seg_col = seg_col + (iota_col >= end).astype(jnp.int32)

    @pl.when(r == 0)
    def _():
        tokens[...] = d_r1[...]

    d_attn = d_attn_ref[...]
    d_mixed = dot(d_attn, w_out[0], 1, 1).astype(BF16)
    scale = HEAD ** (-0.5)
    for h in range(feat // HEAD):
        lanes = slice(h * HEAD, (h + 1) * HEAD)
        q = qkv[0, 0, :, lanes] * BF16(scale)
        k = qkv[0, 1, :, lanes]
        v = qkv[0, 2, :, lanes]
        d_o = d_mixed[:, lanes]
        scores = jnp.where(seg_col == seg_row, dot(q, k, 1, 1), masked_score)
        expo = jnp.exp(scores - jnp.max(scores, axis=1, keepdims=True))
        probs = expo * (1.0 / jnp.sum(expo, axis=1, keepdims=True))
        d_p = dot(d_o, v, 1, 1)
        d_s = (probs * (d_p - jnp.sum(d_p * probs, axis=1, keepdims=True))).astype(BF16)
        d_proj[:, h * HEAD : (h + 1) * HEAD] = (dot(d_s, k, 1, 0) * scale).astype(BF16)
        d_proj[:, feat + h * HEAD : feat + (h + 1) * HEAD] = dot(d_s, q, 0, 0).astype(BF16)
        d_proj[:, 2 * feat + h * HEAD : 2 * feat + (h + 1) * HEAD] = dot(probs.astype(BF16), d_o, 0, 0).astype(BF16)
    weights_o[0, :feat] = dot(mixed[0], d_attn, 0, 0).astype(BF16)
    weights_o[0, feat:] = dot(d_proj[...], x_ref[...], 0, 0).astype(BF16)
    bias_o[0] = jnp.sum(d_proj[...].astype(F32), axis=0, keepdims=True)
    value = tokens[...]
    for j in range(3):
        value = value + dot(d_proj[:, j * feat : (j + 1) * feat], w_qkv[0, j], 1, 1)
    tokens[...] = value

    @pl.when(r == pl.num_programs(0) - 1)
    def _():
        tokens_o[...] = tokens[...].astype(BF16)


def attention_back(qkv, mixed, d_attn, d_r1, x, w_out, w_qkv, extents, block):
    nmp, rows, feat = mixed.shape
    wide = x.shape[1]
    sds = jax.ShapeDtypeStruct
    out = (sds((nmp, 4 * feat, wide), BF16), sds((nmp, 1, 3 * feat), F32), sds((rows, wide), BF16))
    return pl.pallas_call(
        functools.partial(attention_back_kernel, block=block),
        grid=(nmp,),
        out_shape=out,
        in_specs=[quarter(qkv.shape), quarter(mixed.shape), whole(d_attn.shape), whole(d_r1.shape), whole(x.shape)]
        + [quarter(w_out.shape), quarter(w_qkv.shape), pl.BlockSpec(memory_space=pltpu.SMEM)],
        out_specs=[quarter(out[0].shape), quarter(out[1].shape), whole(out[2].shape)],
        scratch_shapes=[pltpu.VMEM((rows, 3 * feat), BF16), pltpu.VMEM((rows, wide), F32)],
        compiler_params=pltpu.CompilerParams(vmem_limit_bytes=48 * 2**20),
        cost_estimate=pl.CostEstimate(
            flops=64 * nmp * rows * wide * feat, bytes_accessed=24 * 2**20, transcendentals=rows * rows * 12
        ),
        name="attention_back",
    )(qkv, mixed, d_attn, d_r1, x, w_out, w_qkv, extents)


PIECES = 8
CHUNKS = 6


def reduce_kernel(ndp, nmp, kinds, *refs):
    parts = refs[:kinds]
    refs = refs[kinds:]
    vec_ref, tok_ref, out, vec_out, tok = refs[:5]
    (
        near, mine, theirs, got_y, got_x, got_1, got_2, got_e, vec_a, vec_b, vec_s, vec_r,
        a_s, a_r, y_s, y_r, x_s, x_r, p_s, p_r, q_s, q_r, e_s, e_r, gq_s, gq_r, gp_s, gp_r, gx_s, gx_r,
        va_s, va_r, v_s, v_r, t_s, t_r, own_sem,
    ) = refs[5:]
    total = kinds * CHUNKS
    bits = ndp.bit_length() - 1
    extra = bits - 3
    dp, mp = lax.axis_index("dp"), lax.axis_index("mp")
    near_dev, far_dev = (dp, flip(mp, 1)), (dp, flip(mp, 2))
    dp_dev = [(flip(dp, 1 << b), mp) for b in range(bits)]
    b0, b1, b2 = (lax.rem(dp // (1 << b), 2) for b in range(3))
    ident = b0 * 4 + b1 * 2 + b2

    barrier = pltpu.get_barrier_semaphore()
    for where in [near_dev, far_dev] + dp_dev:
        pl.semaphore_signal(barrier, inc=1, device_id=where, device_id_type=MESH)
    pl.semaphore_wait(barrier, 2 + bits)

    def remote(source, target, send, recv, where):
        return pltpu.make_async_remote_copy(
            source, target, send, recv, device_id=where, device_id_type=MESH
        )

    def near_copy(k, j):
        return remote(parts[k].at[2 * j + 1], near.at[k, j], a_s.at[2 * k + j], a_r.at[2 * k + j], near_dev)

    def far_copy(c):
        return remote(theirs.at[c], got_y.at[c], y_s.at[c], y_r.at[c], far_dev)

    def x_copy(c):
        return remote(mine.at[c, pl.ds((1 - b0) * 4, 4)], got_x.at[c], x_s.at[c], x_r.at[c], dp_dev[0])

    def p_copy(c):
        return remote(mine.at[c, pl.ds(b0 * 4 + (1 - b1) * 2, 2)], got_1.at[c], p_s.at[c], p_r.at[c], dp_dev[1])

    def q_copy(c):
        return remote(mine.at[c, ident + 1 - 2 * b2], got_2.at[c], q_s.at[c], q_r.at[c], dp_dev[2])

    def e_copy(c, e):
        return remote(mine.at[c, ident], got_e.at[e, c], e_s.at[e, c], e_r.at[e, c], dp_dev[3 + e])

    def gq_copy(c):
        return remote(out.at[c, ident], out.at[c, ident], gq_s.at[c], gq_r.at[c], dp_dev[2])

    def gp_copy(c):
        span = pl.ds(b0 * 4 + b1 * 2, 2)
        return remote(out.at[c, span], out.at[c, span], gp_s.at[c], gp_r.at[c], dp_dev[1])

    def gx_copy(c):
        span = pl.ds(b0 * 4, 4)
        return remote(out.at[c, span], out.at[c, span], gx_s.at[c], gx_r.at[c], dp_dev[0])

    vec_near = [remote(vec_ref.at[2 * j + 1], vec_a.at[j], va_s.at[j], va_r.at[j], near_dev) for j in range(2)]
    vec_far = remote(vec_b, vec_r.at[0], v_s.at[0], v_r.at[0], far_dev)
    vec_dp = [
        remote(vec_s.at[b], vec_r.at[1 + b], v_s.at[1 + b], v_r.at[1 + b], dp_dev[b]) for b in range(bits)
    ]
    tok_near = remote(tok_ref, tok.at[mp], t_s.at[0], t_r.at[0], near_dev)
    tok_far = remote(tok_ref, tok.at[mp], t_s.at[1], t_r.at[1], far_dev)
    other = flip(mp, 2)
    tok_pass = remote(tok.at[other], tok.at[other], t_s.at[2], t_r.at[2], near_dev)
    tok_own = pltpu.make_async_copy(tok_ref, tok.at[mp], own_sem)

    for copy in vec_near:
        copy.start()
    for k in range(kinds):
        for j in range(2):
            near_copy(k, j).start()
    tok_near.start()
    tok_own.start()
    for copy in vec_near:
        copy.wait_recv()
    vec_b[...] = vec_ref[2] + vec_a[1]
    vec_far.start()
    vec_s[0] = vec_ref[0] + vec_a[0]

    def add(a, b):
        return (a.astype(F32) + b.astype(F32)).astype(BF16)

    def first(k):
        for j in range(2):
            near_copy(k, j).wait_recv()

        @pl.loop(0, CHUNKS)
        def _(i):
            c = k * CHUNKS + i
            theirs[c] = add(parts[k][2, i], near[k, 1, i])
            far_copy(c).start()
            mine[c] = add(parts[k][0, i], near[k, 0, i])

    first(0)
    last = 6 + extra
    for t in range(kinds):
        if t + 1 < kinds:
            first(t + 1)
        else:
            tok_far.start()

        @pl.loop(t * CHUNKS, (t + 1) * CHUNKS + (last if t == kinds - 1 else 0))
        def _(i):
            def at(lag, do):
                @pl.when((i >= lag) & (i - lag < total))
                def _():
                    do(i - lag)

            @functools.partial(at, last)
            def _(c):
                gx_copy(c).wait_recv()

            @functools.partial(at, last - 1)
            def _(c):
                gp_copy(c).wait_recv()
                gx_copy(c).start()

            @functools.partial(at, last - 2)
            def _(c):
                gq_copy(c).wait_recv()
                gp_copy(c).start()

            for e in reversed(range(extra)):
                @functools.partial(at, 4 + e)
                def _(c, e=e):
                    e_copy(c, e).wait()
                    mine[c, ident] = add(mine[c, ident], got_e[e, c])
                    if e + 1 < extra:
                        e_copy(c, e + 1).start()
                    else:
                        out[c, ident] = mine[c, ident]
                        gq_copy(c).start()

            @functools.partial(at, 3)
            def _(c):
                q_copy(c).wait_recv()
                value = add(mine[c, ident], got_2[c])
                if extra:
                    mine[c, ident] = value
                    e_copy(c, 0).start()
                else:
                    out[c, ident] = value
                    gq_copy(c).start()

            @functools.partial(at, 2)
            def _(c):
                p_copy(c).wait_recv()
                span = pl.ds(b0 * 4 + b1 * 2, 2)
                mine[c, span] = add(mine[c, span], got_1[c])
                q_copy(c).start()

            @functools.partial(at, 1)
            def _(c):
                x_copy(c).wait_recv()
                span = pl.ds(b0 * 4, 4)
                mine[c, span] = add(mine[c, span], got_x[c])
                p_copy(c).start()

            @functools.partial(at, 0)
            def _(c):
                far_copy(c).wait_recv()
                mine[c] = add(mine[c], got_y[c])
                x_copy(c).start()

        if t == 0:
            vec_far.wait()
            vec_s[0] = vec_s[0] + vec_r[0]
            vec_dp[0].start()
        if t == 1:
            for b in range(bits):
                vec_dp[b].wait()
                value = vec_s[b] + vec_r[1 + b]
                if b + 1 < bits:
                    vec_s[b + 1] = value
                    vec_dp[b + 1].start()
                else:
                    vec_out[...] = value

    tok_far.wait_recv()
    tok_pass.start()
    for copy in vec_near:
        copy.wait_send()
    for k in range(kinds):
        for j in range(2):
            near_copy(k, j).wait_send()

    @pl.loop(0, total)
    def _(c):
        for copy in (far_copy, x_copy, p_copy, q_copy, gq_copy, gp_copy, gx_copy):
            copy(c).wait_send()

    tok_near.wait()
    tok_far.wait_send()
    tok_own.wait()
    tok_pass.wait()


def reduce_all(parts, vectors, tokens, ndp, nmp):
    kinds = len(parts)
    total = kinds * CHUNKS
    _, rows, wide = parts[0].shape
    small = rows // (CHUNKS * PIECES)
    bits = ndp.bit_length() - 1
    extra = bits - 3
    flat = [p.reshape(nmp, CHUNKS, PIECES, small, wide) for p in parts]
    vmem = pl.BlockSpec(memory_space=pltpu.VMEM)
    dma = pltpu.SemaphoreType.DMA

    def buffer(*lead):
        return pltpu.VMEM(lead + (small, wide), BF16)

    pair = lambda *shape: [dma(shape), dma(shape)]
    out = pl.pallas_call(
        functools.partial(reduce_kernel, ndp, nmp, kinds),
        out_shape=(
            jax.ShapeDtypeStruct((total, PIECES, small, wide), BF16),
            jax.ShapeDtypeStruct(vectors.shape[1:], F32),
            jax.ShapeDtypeStruct((nmp,) + tokens.shape, BF16),
        ),
        in_specs=[vmem] * (len(flat) + 2),
        out_specs=(vmem,) * 3,
        scratch_shapes=[
            buffer(kinds, 2, CHUNKS, PIECES),
            buffer(total, PIECES),
            buffer(total, PIECES),
            buffer(total, PIECES),
            buffer(total, 4),
            buffer(total, 2),
            buffer(total),
            buffer(max(extra, 1), total),
            pltpu.VMEM((2,) + vectors.shape[1:], F32),
            pltpu.VMEM(vectors.shape[1:], F32),
            pltpu.VMEM((bits,) + vectors.shape[1:], F32),
            pltpu.VMEM((bits + 1,) + vectors.shape[1:], F32),
        ]
        + pair(2 * kinds) + pair(total) * 4 + pair(max(extra, 1), total) + pair(total) * 3
        + pair(2) + pair(bits + 1) + pair(3) + [dma],
        compiler_params=pltpu.CompilerParams(
            collective_id=1, has_side_effects=True, vmem_limit_bytes=62 * 2**20
        ),
        name="reduce_all",
    )(*flat, vectors, tokens)
    return out[0].reshape(kinds, rows, wide), out[1], out[2].reshape(-1, wide)


def local(
    encoder_rows,
    piece_extent_sequence,
    triple_projection_matrix,
    asker_content_shifts,
    mixing_result_matrix,
    mixing_result_offset_vector,
    mixing_normalizer_scale,
    mixing_normalizer_shift,
    widen_matrix,
    widen_shift_vector,
    narrow_matrix,
    narrow_shift_vector,
    perceptron_normalizer_scale,
    perceptron_normalizer_shift,
    document_vectors,
    sharpness_factor,
    correct_document_position,
    upstream_sensitivity,
    *,
    width,
    depth,
):
    me = lax.axis_index("mp")
    nblock = piece_extent_sequence.shape[0]
    block = encoder_rows.shape[0] // nblock
    rows = encoder_rows.shape[0] // width
    feat = triple_projection_matrix.shape[2]
    hidden = widen_matrix.shape[1]
    wide = encoder_rows.shape[1]

    small = jnp.concatenate(
        [jnp.pad(asker_content_shifts, ((0, 0), (0, hidden - feat))), widen_shift_vector[None]]
    )
    (
        qkv, mixed, n1, inv1, n2, inv2, h1_low, act, slope, w_qkv, w_out, w_up, w_down, own_out, query, x,
    ) = encode(
        encoder_rows, piece_extent_sequence, triple_projection_matrix, mixing_result_matrix, widen_matrix,
        narrow_matrix, small, mixing_result_offset_vector, mixing_normalizer_scale, mixing_normalizer_shift,
        narrow_shift_vector, perceptron_normalizer_scale, perceptron_normalizer_shift, block, width,
    )
    d_query, seg_loss, sharpness_derivative = retrieval(
        query, document_vectors, correct_document_position[:, None], sharpness_factor, depth, width
    )
    own_out, d_query = lax.optimization_barrier((own_out, d_query))
    layer_out = jnp.zeros((encoder_rows.shape[0], wide), BF16)
    for r, piece in enumerate(spread_over_mp(own_out, width)):
        layer_out = lax.dynamic_update_slice(layer_out, piece, ((me ^ r) * rows, 0))
    g_down, g_up, row_sums, g_up_bias, d_r1, d_attn = ffn_back(
        upstream_sensitivity, d_query, piece_extent_sequence, n1, inv1, n2, inv2, mixing_normalizer_scale,
        perceptron_normalizer_scale, h1_low, act, slope, w_up, w_down, block,
    )
    g_attn, g_bias, d_tokens = attention_back(
        qkv, mixed, d_attn, d_r1, x, w_out, w_qkv, piece_extent_sequence, block
    )
    g_head_bias = jnp.concatenate([g_bias[:, :, :feat], g_bias[:, :, 2 * feat :]], axis=2)
    vectors = jnp.concatenate(
        [
            jnp.broadcast_to(row_sums[None], (width,) + row_sums.shape),
            jnp.pad(g_head_bias, ((0, 0), (0, 0), (0, wide - 2 * feat))),
            jnp.pad(g_up_bias, ((0, 0), (0, 0), (0, wide - hidden))),
        ],
        axis=1,
    )
    sums, vectors, grad_tokens = reduce_all([g_down, g_up, g_attn], vectors, d_tokens, depth, width)
    grad_tokens = grad_tokens.astype(F32)
    sums = sums.astype(F32)
    grad_qkv = sums[2, feat:].reshape(3, feat, wide).transpose(0, 2, 1)
    return (
        layer_out,
        seg_loss[0],
        grad_tokens,
        grad_qkv,
        vectors[6, : 2 * feat].reshape(2, feat),
        sums[2, :feat],
        vectors[0],
        vectors[1],
        vectors[2],
        sums[1],
        vectors[7, :hidden],
        sums[0],
        vectors[3],
        vectors[4],
        vectors[5],
        sharpness_derivative[0],
    )


def solution(mesh):
    in_specs = (
        P("dp", None),
        P("dp", None),
        P(None, None, "mp"),
        P(None, "mp"),
        P("mp", None),
        P(),
        P(),
        P(),
        P(None, "mp"),
        P("mp"),
        P("mp", None),
        P(),
        P(),
        P(),
        P(("dp", "mp"), None),
        P(),
        P(),
        P("dp", None),
    )
    out_specs = (
        P("dp", None),
        P(),
        P("dp", None),
        P(None, None, "mp"),
        P(None, "mp"),
        P("mp", None),
        P(),
        P(),
        P(),
        P(None, "mp"),
        P("mp"),
        P("mp", None),
        P(),
        P(),
        P(),
        P(),
    )
    width = mesh.shape["mp"]

    def step(*args):
        return local(*args, width=width, depth=mesh.shape["dp"])

    return jax.shard_map(step, mesh=mesh, in_specs=in_specs, out_specs=out_specs, check_vma=False)
```

```python
import functools
import math

import jax
import jax.numpy as jnp
from jax import lax
from jax.experimental import pallas as pl
from jax.experimental.pallas import tpu as pltpu
from jax.sharding import PartitionSpec as P

HEAD = 64
F32 = jnp.float32
BF16 = jnp.bfloat16
MESH = pl.DeviceIdType.MESH
norm_epsilon = 1e-05
masked_score = -1e30


def dot(a, b, ca, cb):
    return lax.dot_general(a, b, (((ca,), (cb,)), ((), ())), preferred_element_type=F32)


def norm_stats(resid):
    centre = jnp.mean(resid, axis=-1, keepdims=True)
    centred = resid - centre
    spread = jnp.mean(centred * centred, axis=-1, keepdims=True)
    inv = lax.rsqrt(spread + norm_epsilon)
    return centred * inv, inv


def norm_back(d_out, normed, inv, gain):
    e = d_out * gain
    return inv * (
        e - jnp.mean(e, axis=-1, keepdims=True) - normed * jnp.mean(e * normed, axis=-1, keepdims=True)
    )


def flip(index, step):
    return index + step * (1 - 2 * lax.rem(index // step, 2))


def retrieval_kernel(
    ndp, nmp, query_ref, own_ref, docs_hbm, gold_ref, sharp_ref, dq_ref, loss_ref, ds_ref, layer,
    queries, docs, low, stats, columns, part_u, part_g, send, got, doc_sem, q_send, q_recv, s_send, s_recv, d_send, d_recv,
    l_s, l_r, own_sem,
):
    n = ndp * nmp
    own = query_ref.shape[0]
    nseg = gold_ref.shape[0]
    tile = 256 if nseg <= 256 else 128
    dp, mp = lax.axis_index("dp"), lax.axis_index("mp")
    me = dp * nmp + mp
    load = pltpu.make_async_copy(docs_hbm, docs, doc_sem)
    load.start()
    barrier = pltpu.get_barrier_semaphore()

    def device(step):
        other = lax.rem(me + step, n)
        return other, (other // nmp, lax.rem(other, nmp))

    @pl.loop(1, n)
    def _(step):
        _, where = device(step)
        pl.semaphore_signal(barrier, inc=1, device_id=where, device_id_type=MESH)

    pl.semaphore_wait(barrier, n - 1)

    def push(source, target, send_sems, recv_sems):
        @pl.loop(1, n)
        def _(step):
            other, where = device(step)
            pltpu.make_async_remote_copy(
                source(other), target, send_sems.at[step], recv_sems.at[step], device_id=where, device_id_type=MESH
            ).start()

    def drain(source, target, send_sems, recv_sems):
        @pl.loop(1, n)
        def _(step):
            other, where = device(step)
            copy = pltpu.make_async_remote_copy(
                source(other), target, send_sems.at[step], recv_sems.at[step], device_id=where, device_id_type=MESH
            )
            copy.wait()

    push(lambda other: query_ref, queries.at[me], q_send, q_recv)
    queries[me] = query_ref[...]
    drain(lambda other: query_ref, queries.at[me], q_send, q_recv)
    near, far, across = (dp, flip(mp, 1)), (dp, flip(mp, 2)), flip(mp, 2)

    def spread(source, slot, i, where):
        return pltpu.make_async_remote_copy(
            source, layer.at[slot], l_s.at[i], l_r.at[i], device_id=where, device_id_type=MESH
        )

    to_near, to_far = spread(own_ref, mp, 0, near), spread(own_ref, mp, 1, far)
    to_pass = spread(layer.at[across], across, 2, near)
    keep = pltpu.make_async_copy(own_ref, layer.at[mp], own_sem)
    to_far.start()
    to_near.start()
    keep.start()
    load.wait()

    sharp = sharp_ref[0]
    offset = me * docs.shape[0]
    ids = lax.broadcasted_iota(jnp.int32, (tile, docs.shape[0]), 1)
    lane = lax.broadcasted_iota(jnp.int32, (tile, 128), 1)
    per = tile // own

    @pl.loop(0, nseg // tile)
    def _(i):
        span = pl.ds(pl.multiple_of(i * tile, tile), tile)
        q = queries[pl.ds(i * per, per)].reshape(tile, queries.shape[2])
        logit = lax.dot_general(q, docs[...], (((1,), (1,)), ((), ())), preferred_element_type=F32) / sharp
        match = ids == gold_ref[span, :] - offset
        top = jnp.max(logit, axis=1, keepdims=True)
        expo = jnp.exp(logit - top)
        total = jnp.sum(expo, axis=1, keepdims=True)
        tilt = jnp.sum(expo * logit, axis=1, keepdims=True)
        gold = jnp.sum(jnp.where(match, logit, 0.0), axis=1, keepdims=True)
        packed = jnp.where(lane == 0, top, jnp.where(lane == 1, total, jnp.where(lane == 2, tilt, gold)))
        stats[me, :, span] = packed.T[:4]
        low[span, :] = jnp.where(match, 0.0, expo).astype(BF16)

    push(lambda other: stats.at[me], stats.at[me], s_send, s_recv)

    @pl.loop(0, nseg // tile)
    def _(i):
        span = pl.ds(pl.multiple_of(i * tile, tile), tile)
        part_u[span, :] = jnp.dot(low[span, :], docs[...], preferred_element_type=F32)
        match = ids == gold_ref[span, :] - offset
        part_g[span, :] = jnp.dot(
            match.astype(F32).astype(BF16), docs[...], preferred_element_type=F32
        ).astype(BF16)

    drain(lambda other: stats.at[me], stats.at[me], s_send, s_recv)
    to_far.wait_recv()
    to_pass.start()

    tops = stats[:, 0, :]
    top = jnp.max(tops, axis=0, keepdims=True)
    share = jnp.exp(tops - top)
    total = jnp.sum(stats[:, 1, :] * share, axis=0, keepdims=True)
    tilt = jnp.sum(stats[:, 2, :] * share, axis=0, keepdims=True)
    gold = jnp.sum(stats[:, 3, :], axis=0, keepdims=True)
    lse = top + jnp.log(total)
    loss_ref[...] = lse - gold
    ds_ref[...] = -jnp.sum(tilt / total - gold, axis=1, keepdims=True) / sharp
    scale = jnp.exp(stats[me, 0:1, :] - lse) / sharp
    gold_scale = (jnp.exp(gold - lse) - 1.0) / sharp
    row = lax.broadcasted_iota(jnp.int32, (128, nseg), 0)
    columns[...] = jnp.where(row == 0, scale, gold_scale).T

    @pl.loop(0, nseg // tile)
    def _(i):
        span = pl.ds(pl.multiple_of(i * tile, tile), tile)
        value = part_u[span, :] * columns[span, 0:1] + part_g[span, :].astype(F32) * columns[span, 1:2]
        send[pl.ds(i * per, per)] = value.astype(BF16).reshape(per, own, value.shape[1])

    push(lambda other: send.at[other], got.at[me], d_send, d_recv)
    got[me] = send[me]
    drain(lambda other: send.at[other], got.at[me], d_send, d_recv)
    dq_ref[...] = jnp.sum(got[...].astype(F32), axis=0)
    to_near.wait()
    to_far.wait_send()
    to_pass.wait()
    keep.wait()


def retrieval(query, own_out, docs, gold, sharp, ndp, nmp):
    n = ndp * nmp
    own, width = query.shape
    nseg = gold.shape[0]
    vmem = pl.BlockSpec(memory_space=pltpu.VMEM)
    return pl.pallas_call(
        functools.partial(retrieval_kernel, ndp, nmp),
        out_shape=(
            jax.ShapeDtypeStruct((own, width), F32),
            jax.ShapeDtypeStruct((1, nseg), F32),
            jax.ShapeDtypeStruct((1, 1), F32),
            jax.ShapeDtypeStruct((nmp,) + own_out.shape, BF16),
        ),
        in_specs=[vmem, vmem, pl.BlockSpec(memory_space=pl.ANY), vmem, pl.BlockSpec(memory_space=pltpu.SMEM)],
        out_specs=(vmem, vmem, vmem, pl.BlockSpec(memory_space=pl.ANY)),
        scratch_shapes=[
            pltpu.VMEM((n, own, width), BF16),
            pltpu.VMEM(docs.shape, BF16),
            pltpu.VMEM((nseg, docs.shape[0]), BF16),
            pltpu.VMEM((n, 4, nseg), F32),
            pltpu.VMEM((nseg, 128), F32),
            pltpu.VMEM((nseg, width), F32),
            pltpu.VMEM((nseg, width), BF16),
            pltpu.VMEM((n, own, width), BF16),
            pltpu.VMEM((n, own, width), BF16),
            pltpu.SemaphoreType.DMA,
        ]
        + [pltpu.SemaphoreType.DMA((n,))] * 6
        + [pltpu.SemaphoreType.DMA((3,))] * 2
        + [pltpu.SemaphoreType.DMA],
        compiler_params=pltpu.CompilerParams(
            collective_id=0, has_side_effects=True, vmem_limit_bytes=60 * 2**20
        ),
        name="retrieval",
    )(query, own_out, docs, gold, sharp)


def gelu_with_slope(u):
    z = jnp.abs(u) * (0.5**0.5)
    t = 1.0 / (1.0 + 0.5 * z)
    poly = 0.17087277
    for c in (
        -0.82215223, 1.48851587, -1.13520398, 0.27886807, -0.18628806, 0.09678418, 0.37409196, 1.00002368,
    ):
        poly = poly * t + c
    square = z * z
    tail = 0.5 * t * jnp.exp(poly * t - 1.26551223 - square)
    cdf = jnp.where(u < 0, tail, 1.0 - tail)
    return u * cdf, cdf + u * (jnp.exp(-square) * ((2 * math.pi) ** -0.5))


def encode_kernel(nmp, block, *refs):
    (
        rows_hbm, extents, w_qkv, w_out, w_up, w_down, small_ref, vectors,
    ) = refs[:8]
    out_bias, gain1, shift1, down_bias, gain2, shift2 = (vectors.at[i : i + 1] for i in range(6))
    (
        qkv_o, mixed_o, n1_o, inv1_o, n2_o, inv2_o, low_o, act_o, slope_o, w_qkv_o, w_out_o, w_up_o, w_down_o,
        own_o, query_o, x_o,
    ) = refs[8:24]
    (
        x, qkv, mixed, n1, n2, h1_low, act, slope, all_qkv, all_out, all_up, all_down, small, total,
        x_sem, save_sem, n_s, n_r, m_s, m_r, y_s, y_r, f_s, f_r, g_s, g_r, h_s, h_r, sm_s, sm_r,
    ) = refs[24:]
    dp, mp = lax.axis_index("dp"), lax.axis_index("mp")
    near, far, side = (dp, flip(mp, 1)), (dp, flip(mp, 2)), (flip(dp, 1), mp)
    b = lax.rem(dp, 2)
    rows = x.shape[0]
    feat = w_out.shape[0] * w_out.shape[1]
    scale = HEAD ** (-0.5)

    load = pltpu.make_async_copy(rows_hbm.at[pl.ds(pl.multiple_of(mp * rows, rows), rows)], x, x_sem)
    load.start()
    barrier = pltpu.get_barrier_semaphore()
    for where in (near, far, side):
        pl.semaphore_signal(barrier, inc=1, device_id=where, device_id_type=MESH)
    pl.semaphore_wait(barrier, 3)

    def remote(source, target, send, recv, where):
        return pltpu.make_async_remote_copy(source, target, send, recv, device_id=where, device_id_type=MESH)

    pieces = [(w_qkv.at[k], all_qkv, k) for k in range(3)] + [(w_out, all_out, None)]
    pieces += [(w_up.at[s], all_up, s) for s in range(w_up.shape[0])]
    pieces += [(w_down.at[s], all_down, s) for s in range(w_down.shape[0])]
    count = len(pieces)

    def slot(i, r):
        _, held, s = pieces[i]
        return held.at[r] if s is None else held.at[r, s]

    near_own = [remote(pieces[i][0], slot(i, 1), n_s.at[i], n_r.at[i], near) for i in range(count)]
    far_own = [remote(pieces[i][0].at[b], slot(i, 2).at[b], y_s.at[i], y_r.at[i], far) for i in range(count)]
    pass_side = [remote(slot(i, 2).at[b], slot(i, 2).at[b], f_s.at[i], f_r.at[i], side) for i in range(count)]
    pass_near = [remote(slot(i, 2).at[b], slot(i, 3).at[b], g_s.at[i], g_r.at[i], near) for i in range(count)]
    pass_other = [
        remote(slot(i, 2).at[1 - b], slot(i, 3).at[1 - b], h_s.at[i], h_r.at[i], near) for i in range(count)
    ]
    small_near = remote(small_ref, small.at[1], sm_s.at[0], sm_r.at[0], near)
    small_far = remote(small_ref, small.at[2], sm_s.at[1], sm_r.at[1], far)
    small_pass = remote(small.at[2], small.at[3], sm_s.at[2], sm_r.at[2], near)

    small_near.start()
    small_far.start()
    for i in range(count):
        far_own[i].start()
        near_own[i].start()
    small[0] = small_ref[...]
    saves = []

    def save(source, target):
        copy = pltpu.make_async_copy(source, target, save_sem.at[len(saves)])
        copy.start()
        saves.append(copy)

    for source, target in ((w_qkv, w_qkv_o), (w_out, w_out_o), (w_up, w_up_o), (w_down, w_down_o)):
        save(source, target.at[0])

    def relay(i):
        far_own[i].wait_recv()
        pass_side[i].start()
        pass_near[i].start()

    def relay_other(i):
        pass_side[i].wait_recv()
        pass_other[i].start()

    def last_arrived(i):
        pass_near[i].wait_recv()
        pass_other[i].wait_recv()

    iota_row = lax.broadcasted_iota(jnp.int32, (1, rows), 1)
    iota_col = lax.broadcasted_iota(jnp.int32, (rows, 1), 0)
    nblk = rows // block
    nseg = extents.shape[1]
    seg_row, seg_col = jnp.zeros_like(iota_row), jnp.zeros_like(iota_col)
    starts = []
    for i in range(nblk):
        end = jnp.int32(i * block)
        for j in range(nseg):
            starts.append(end)
            end = end + extents[mp * nblk + i, j]
            seg_row = seg_row + (iota_row >= end).astype(jnp.int32)
            seg_col = seg_col + (iota_col >= end).astype(jnp.int32)
    load.wait()
    save(x, x_o)

    def project(r):
        source = w_qkv if r == 0 else all_qkv.at[r]
        for k in range(3):
            value = dot(x[...], source[k].reshape(feat, x.shape[1]), 1, 1)
            if k == 0:
                value = value + small[r, 0:1, :feat]
            if k == 2:
                value = value + small[r, 1:2, :feat]
            qkv[r, k] = value.astype(BF16)
        save(qkv.at[r], qkv_o.at[r])

    def head(r, h):
        lanes = slice(h * HEAD, (h + 1) * HEAD)
        q = qkv[r, 0, :, lanes] * BF16(scale)
        scores = dot(q, qkv[r, 1, :, lanes], 1, 1)
        scores = jnp.where(seg_col == seg_row, scores, masked_score)
        expo = jnp.exp(scores - jnp.max(scores, axis=1, keepdims=True))
        probs = (expo * (1.0 / jnp.sum(expo, axis=1, keepdims=True))).astype(BF16)
        mixed[r, :, lanes] = jnp.dot(probs, qkv[r, 2, :, lanes], preferred_element_type=F32).astype(BF16)

    def mix(r, *between):
        for h in range(feat // HEAD):
            head(r, h)
            if h < len(between):
                between[h]()
        save(mixed.at[r], mixed_o.at[r])

    project(0)
    mix(0)
    for i in range(3):
        near_own[i].wait_recv()
    small_near.wait_recv()
    project(1)
    mix(1)
    small_far.wait_recv()
    small_pass.start()
    relay(0)
    relay(1)
    relay_other(0)
    relay(2)
    relay_other(1)
    relay(3)
    relay_other(2)
    project(2)
    save(all_qkv.at[2], w_qkv_o.at[2])
    save(all_qkv.at[1], w_qkv_o.at[1])

    def both(i):
        relay(i)
        relay_other(i - 1)

    mix(2, lambda: relay_other(3), lambda: relay(4))
    for i in range(3):
        last_arrived(i)
    small_pass.wait_recv()
    project(3)
    save(all_qkv.at[3], w_qkv_o.at[3])
    mix(3, lambda: both(5))
    near_own[3].wait_recv()
    last_arrived(3)
    attn = jnp.zeros((rows, x.shape[1]), F32)
    for r in range(4):
        w = w_out[...] if r == 0 else all_out[r]
        attn = attn + jnp.dot(mixed[r], w.reshape(feat, x.shape[1]), preferred_element_type=F32)
        if r:
            save(all_out.at[r], w_out_o.at[r])
    normed, inv = norm_stats(x[...].astype(F32) + attn + out_bias[...])
    n1[...] = normed
    save(n1, n1_o)
    inv1_o[...] = jnp.broadcast_to(inv, inv1_o.shape)
    h1 = normed * gain1[...] + shift1[...]
    total[...] = h1 + down_bias[...]
    h1_low[...] = h1.astype(BF16)
    save(h1_low, low_o)
    ups, downs = range(4, 4 + w_up.shape[0]), range(4 + w_up.shape[0], count)
    wide = x.shape[1]

    def widen(r):
        w = w_up[...] if r == 0 else all_up[r]
        upper = jnp.dot(h1_low[...], w.reshape(wide, -1), preferred_element_type=F32) + small[r, 2:3, :]
        value, gradient = gelu_with_slope(upper)
        act[r] = value.astype(BF16)
        slope[r] = gradient.astype(BF16)
        save(act.at[r], act_o.at[r])
        save(slope.at[r], slope_o.at[r])
        if r:
            save(all_up.at[r], w_up_o.at[r])

    def narrow(r):
        w = w_down[...] if r == 0 else all_down[r]
        total[...] += jnp.dot(act[r], w.reshape(-1, wide), preferred_element_type=F32)
        if r:
            save(all_down.at[r], w_down_o.at[r])

    both(6)
    widen(0)
    both(7)
    narrow(0)
    for i in ups:
        near_own[i].wait_recv()
    widen(1)
    both(8)
    for i in downs:
        near_own[i].wait_recv()
    narrow(1)
    widen(2)
    both(9)
    for i in ups:
        last_arrived(i)
    widen(3)
    relay_other(9)
    narrow(2)
    for i in downs:
        last_arrived(i)
    narrow(3)
    normed, inv = norm_stats(total[...])
    n2[...] = normed
    save(n2, n2_o)
    inv2_o[...] = jnp.broadcast_to(inv, inv2_o.shape)
    own = (normed * gain2[...] + shift2[...]).astype(BF16)
    own_o[...] = own
    line = lax.broadcasted_iota(jnp.int32, (len(starts), rows), 0)
    first = jnp.zeros((len(starts), rows), jnp.int32)
    for j, start in enumerate(starts):
        first = jnp.where(line == j, start, first)
    pick = (lax.broadcasted_iota(jnp.int32, first.shape, 1) == first).astype(F32).astype(BF16)
    query_o[...] = jnp.dot(pick, own, preferred_element_type=F32).astype(BF16)
    for copy in saves:
        copy.wait()
    for copy in near_own + far_own + pass_side + pass_near + pass_other + [small_near, small_far, small_pass]:
        copy.wait_send()


STRIPS = 3


def encode(
    encoder_rows, extents, w_qkv, w_out, w_up, w_down, small, out_bias, gain1, shift1, down_bias, gain2, shift2,
    block, nmp,
):
    rows = encoder_rows.shape[0] // nmp
    wide = encoder_rows.shape[1]
    feat, hidden = w_qkv.shape[1], w_up.shape[1]
    nseg = extents.shape[0] * extents.shape[1] // nmp
    cut_qkv = w_qkv.reshape(3, 2, feat // 2, wide)
    cut_out = w_out.reshape(2, feat // 2, wide)
    cut_up = w_up.reshape(STRIPS, 2, wide // (2 * STRIPS), hidden)
    cut_down = w_down.reshape(STRIPS, 2, hidden // (2 * STRIPS), wide)
    vmem, anywhere = pl.BlockSpec(memory_space=pltpu.VMEM), pl.BlockSpec(memory_space=pl.ANY)
    sds = jax.ShapeDtypeStruct
    dma = pltpu.SemaphoreType.DMA
    every = lambda a: (nmp,) + a.shape
    held = [
        sds((nmp, 3, rows, feat), BF16),
        sds((nmp, rows, feat), BF16),
        sds((rows, wide), F32),
        sds((rows, 128), F32),
        sds((rows, wide), F32),
        sds((rows, 128), F32),
        sds((rows, wide), BF16),
        sds((nmp, rows, hidden), BF16),
        sds((nmp, rows, hidden), BF16),
        sds(every(cut_qkv), BF16),
        sds(every(cut_out), BF16),
        sds(every(cut_up), BF16),
        sds(every(cut_down), BF16),
        sds((rows, wide), BF16),
        sds((nseg, wide), BF16),
        sds((rows, wide), BF16),
    ]
    count = 4 + 2 * STRIPS
    scratch = [
        pltpu.VMEM((rows, wide), BF16),
        pltpu.VMEM(held[0].shape, BF16),
        pltpu.VMEM(held[1].shape, BF16),
        pltpu.VMEM((rows, wide), F32),
        pltpu.VMEM((rows, wide), F32),
        pltpu.VMEM((rows, wide), BF16),
        pltpu.VMEM(held[7].shape, BF16),
        pltpu.VMEM(held[8].shape, BF16),
    ]
    scratch += [pltpu.VMEM(h.shape, BF16) for h in held[9:13]]
    scratch += [pltpu.VMEM(every(small), F32), pltpu.VMEM((rows, wide), F32), dma, dma((40,))]
    scratch += [dma((count,))] * 12 + [dma((3,))] * 2
    vectors = jnp.stack([out_bias, gain1, shift1, down_bias, gain2, shift2])
    outs = pl.pallas_call(
        functools.partial(encode_kernel, nmp, block),
        out_shape=tuple(held),
        in_specs=[anywhere, pl.BlockSpec(memory_space=pltpu.SMEM)] + [vmem] * 6,
        out_specs=tuple(vmem if i in (3, 5, 13, 14) else anywhere for i in range(len(held))),
        scratch_shapes=scratch,
        compiler_params=pltpu.CompilerParams(collective_id=2, has_side_effects=True, vmem_limit_bytes=62 * 2**20),
        name="encode",
    )(encoder_rows, extents, cut_qkv, cut_out, cut_up, cut_down, small, vectors)
    outs = list(outs)
    outs[9] = outs[9].reshape(nmp, 3, feat, wide)
    outs[10] = outs[10].reshape(nmp, feat, wide)
    outs[11] = outs[11].reshape(nmp, wide, hidden)
    outs[12] = outs[12].reshape(nmp, hidden, wide)
    return outs, vectors


PIECES = 8
CHUNKS = 6
KINDS = 3


def backward_kernel(ndp, nmp, block, *refs):
    (
        d_query, extents, small_vectors, upstream_h, n1_h, inv1_h, n2_h, inv2_h, low_h, act_h, slope_h, up_h, down_h,
        qkv_h, mixed_h, w_out_h, w_qkv_h, x_h,
    ) = refs[:18]
    out, vec_out, tok = refs[18:21]
    (
        total, n1, inv1, n2, inv2, h1_low, x, act, slope, w_up, w_down, qkv, mixed, w_out, w_qkv,
        d_ffn, d_attn, d_proj, low_tok, parts, vec, near, got_y, got_x, got_1, got_2, got_e,
        vec_a, vec_b, vec_s, vec_r,
        load_sem, ffn_sem, attn_sem, a_s, a_r, y_s, y_r, x_s, x_r, p_s, p_r, q_s, q_r, e_s, e_r,
        gq_s, gq_r, gp_s, gp_r, gx_s, gx_r, va_s, va_r, v_s, v_r, t_s, t_r, own_sem,
    ) = refs[21:]
    count = KINDS * CHUNKS
    bits = ndp.bit_length() - 1
    extra = bits - 3
    rows, wide = total.shape
    feat = mixed.shape[2]
    hidden = act.shape[2]
    dp, mp = lax.axis_index("dp"), lax.axis_index("mp")
    near_dev, far_dev = (dp, flip(mp, 1)), (dp, flip(mp, 2))
    dp_dev = [(flip(dp, 1 << b), mp) for b in range(bits)]
    b0, b1, b2 = (lax.rem(dp // (1 << b), 2) for b in range(3))
    ident = b0 * 4 + b1 * 2 + b2
    gain1, gain2 = small_vectors.at[1:2], small_vectors.at[4:5]

    own_rows = upstream_h.at[pl.ds(pl.multiple_of(mp * rows, rows), rows)]
    loads = [
        pltpu.make_async_copy(source, target, load_sem.at[i])
        for i, (source, target) in enumerate(
            [
                (own_rows, total), (n2_h, n2), (inv2_h, inv2), (act_h, act), (low_h, h1_low), (n1_h, n1),
                (inv1_h, inv1), (x_h, x),
            ]
        )
    ]

    def ffn_loads(i):
        r, slot = 3 - i, lax.rem(i, 2)
        return [
            pltpu.make_async_copy(source.at[r], target.at[slot], ffn_sem.at[slot, j])
            for j, (source, target) in enumerate([(down_h, w_down), (slope_h, slope), (up_h, w_up)])
        ]

    def attn_loads(i):
        r, slot = 3 - i, lax.rem(i, 2)
        return [
            pltpu.make_async_copy(source.at[r], target.at[slot], attn_sem.at[slot, j])
            for j, (source, target) in enumerate([(w_out_h, w_out), (qkv_h, qkv), (mixed_h, mixed), (w_qkv_h, w_qkv)])
        ]

    for copy in loads + ffn_loads(0):
        copy.start()
    barrier = pltpu.get_barrier_semaphore()
    for where in [near_dev, far_dev] + dp_dev:
        pl.semaphore_signal(barrier, inc=1, device_id=where, device_id_type=MESH)
    pl.semaphore_wait(barrier, 2 + bits)

    def remote(source, target, send, recv, where):
        return pltpu.make_async_remote_copy(source, target, send, recv, device_id=where, device_id_type=MESH)

    def part(c, r, first=0, many=PIECES):
        k = c // CHUNKS
        return parts.at[k, r, pl.ds((c - k * CHUNKS) * PIECES + first, many)]

    def near_copy(k, j):
        return remote(parts.at[k, 2 * j + 1], near.at[k, j], a_s.at[2 * k + j], a_r.at[2 * k + j], near_dev)

    def far_copy(c):
        return remote(part(c, 2), got_y.at[c], y_s.at[c], y_r.at[c], far_dev)

    def x_copy(c):
        return remote(part(c, 0, (1 - b0) * 4, 4), got_x.at[c], x_s.at[c], x_r.at[c], dp_dev[0])

    def p_copy(c):
        return remote(part(c, 0, b0 * 4 + (1 - b1) * 2, 2), got_1.at[c], p_s.at[c], p_r.at[c], dp_dev[1])

    def q_copy(c):
        return remote(part(c, 0, ident + 1 - 2 * b2, 1), got_2.at[c], q_s.at[c], q_r.at[c], dp_dev[2])

    def e_copy(c, e):
        return remote(part(c, 0, ident, 1), got_e.at[e, c], e_s.at[e, c], e_r.at[e, c], dp_dev[3 + e])

    def gq_copy(c):
        return remote(out.at[c, ident], out.at[c, ident], gq_s.at[c], gq_r.at[c], dp_dev[2])

    def gp_copy(c):
        span = pl.ds(b0 * 4 + b1 * 2, 2)
        return remote(out.at[c, span], out.at[c, span], gp_s.at[c], gp_r.at[c], dp_dev[1])

    def gx_copy(c):
        span = pl.ds(b0 * 4, 4)
        return remote(out.at[c, span], out.at[c, span], gx_s.at[c], gx_r.at[c], dp_dev[0])

    vec_near = [remote(vec.at[2 * j + 1], vec_a.at[j], va_s.at[j], va_r.at[j], near_dev) for j in range(2)]
    vec_far = remote(vec_b, vec_r.at[0], v_s.at[0], v_r.at[0], far_dev)
    vec_dp = [remote(vec_s.at[b], vec_r.at[1 + b], v_s.at[1 + b], v_r.at[1 + b], dp_dev[b]) for b in range(bits)]
    across = flip(mp, 2)
    tok_near = remote(low_tok, tok.at[mp], t_s.at[0], t_r.at[0], near_dev)
    tok_far = remote(low_tok, tok.at[mp], t_s.at[1], t_r.at[1], far_dev)
    tok_pass = remote(tok.at[across], tok.at[across], t_s.at[2], t_r.at[2], near_dev)
    tok_own = pltpu.make_async_copy(low_tok, tok.at[mp], own_sem)

    def add(a, b):
        return (a.astype(F32) + b.astype(F32)).astype(BF16)

    def exchange(k, r):
        j = r // 2

        @pl.when(lax.rem(r, 2) == 1)
        def _():
            near_copy(k, j).start()

        @pl.when(lax.rem(r, 2) == 0)
        def _():
            near_copy(k, j).wait_recv()

            @pl.loop(0, CHUNKS)
            def _(i):
                span = pl.ds(i * PIECES, PIECES)
                parts[k, r, span] = add(parts[k, r, span], near[k, j, span])

                @pl.when(j == 1)
                def _():
                    far_copy(k * CHUNKS + i).start()

    def tick(i):
        def at(lag, do):
            @pl.when((i >= lag) & (i - lag < count))
            def _():
                do(i - lag)

        def update(c, first, many, got):
            target = part(c, 0, first, many)
            target[...] = add(target[...], got[c])

        @functools.partial(at, 6 + extra)
        def _(c):
            gx_copy(c).wait_recv()

        @functools.partial(at, 5 + extra)
        def _(c):
            gp_copy(c).wait_recv()
            gx_copy(c).start()

        @functools.partial(at, 4 + extra)
        def _(c):
            gq_copy(c).wait_recv()
            gp_copy(c).start()

        for e in reversed(range(extra)):
            @functools.partial(at, 4 + e)
            def _(c, e=e):
                e_copy(c, e).wait()
                update(c, ident, 1, got_e.at[e])
                if e + 1 < extra:
                    e_copy(c, e + 1).start()
                else:
                    out[c, ident] = part(c, 0, ident, 1)[0]
                    gq_copy(c).start()

        @functools.partial(at, 3)
        def _(c):
            q_copy(c).wait_recv()
            if extra:
                update(c, ident, 1, got_2)
                e_copy(c, 0).start()
            else:
                out[c, ident] = add(part(c, 0, ident, 1)[0], got_2[c, 0])
                gq_copy(c).start()

        @functools.partial(at, 2)
        def _(c):
            p_copy(c).wait_recv()
            update(c, b0 * 4 + b1 * 2, 2, got_1)
            q_copy(c).start()

        @functools.partial(at, 1)
        def _(c):
            x_copy(c).wait_recv()
            update(c, b0 * 4, 4, got_x)
            p_copy(c).start()

        @functools.partial(at, 0)
        def _(c):
            far_copy(c).wait_recv()
            update(c, 0, PIECES, got_y)
            x_copy(c).start()

    tile = 128
    nblk = rows // block
    nseg = extents.shape[1]
    vec[...] = jnp.zeros_like(vec)
    for copy in loads[:3]:
        copy.wait()

    def count_up(row, value):
        vec[0, row : row + 1] += jnp.sum(value, axis=0, keepdims=True)

    @pl.loop(0, rows // tile)
    def _(t):
        span = pl.ds(pl.multiple_of(t * tile, tile), tile)
        line = lax.broadcasted_iota(jnp.int32, (tile, 1), 0) + t * tile
        d_h2 = total[span]
        for i in range(nblk):
            start = jnp.int32(i * block)
            for j in range(nseg):
                d_h2 = d_h2 + jnp.where(line == start, d_query[i * nseg + j, :][None], 0.0)
                start = start + extents[mp * nblk + i, j]
        normed = n2[span]
        count_up(5, d_h2)
        count_up(4, d_h2 * normed)
        d_r2 = norm_back(d_h2, normed, inv2[span, 0:1], gain2[...])
        count_up(3, d_r2)
        d_ffn[span] = d_r2.astype(BF16)
        total[span] = d_r2

    def store(k, r, first, value):
        pieces = value.shape[0] // parts.shape[3]
        parts[k, r, first : first + pieces] = value.astype(BF16).reshape(pieces, parts.shape[3], wide)

    loads[3].wait()

    @pl.loop(0, nmp)
    def _(i):
        r = 3 - i
        store(0, r, 0, dot(act[r], d_ffn[...], 0, 0))
        exchange(0, r)

    for copy in loads[4:]:
        copy.wait()
    for copy in attn_loads(0):
        copy.start()

    @pl.loop(0, nmp)
    def _(i):
        r, slot = 3 - i, lax.rem(i, 2)
        for copy in ffn_loads(i):
            copy.wait()

        @pl.when(i + 1 < nmp)
        def _():
            for copy in ffn_loads(i + 1):
                copy.start()

        d_up = (dot(d_ffn[...], w_down[slot], 1, 1) * slope[slot].astype(F32)).astype(BF16)
        vec[r, 7:8, :hidden] = jnp.sum(d_up.astype(F32), axis=0, keepdims=True)
        store(1, r, 0, dot(h1_low[...], d_up, 0, 0))
        exchange(1, r)
        total[...] += dot(d_up, w_up[slot], 1, 1)

        @pl.loop(i - (i + 2) // 3, i + i // 3)
        def _(n):
            tick(n)

    @pl.loop(0, rows // tile)
    def _(t):
        span = pl.ds(pl.multiple_of(t * tile, tile), tile)
        d_h1 = total[span]
        normed = n1[span]
        count_up(2, d_h1)
        count_up(1, d_h1 * normed)
        d_r1 = norm_back(d_h1, normed, inv1[span, 0:1], gain1[...])
        count_up(0, d_r1)
        d_attn[span] = d_r1.astype(BF16)
        total[span] = d_r1

    for r in range(1, nmp):
        vec[r, 0:6] = vec[0, 0:6]

    iota_row = lax.broadcasted_iota(jnp.int32, (1, rows), 1)
    iota_col = lax.broadcasted_iota(jnp.int32, (rows, 1), 0)
    seg_row, seg_col = jnp.zeros_like(iota_row), jnp.zeros_like(iota_col)
    for i in range(nblk):
        end = jnp.int32(i * block)
        for j in range(nseg):
            end = end + extents[mp * nblk + i, j]
            seg_row = seg_row + (iota_row >= end).astype(jnp.int32)
            seg_col = seg_col + (iota_col >= end).astype(jnp.int32)
    scale = HEAD ** (-0.5)

    @pl.loop(0, nmp)
    def _(i):
        r, slot = 3 - i, lax.rem(i, 2)
        for copy in attn_loads(i):
            copy.wait()

        @pl.when(i + 1 < nmp)
        def _():
            for copy in attn_loads(i + 1):
                copy.start()

        d_mixed = dot(d_attn[...], w_out[slot], 1, 1).astype(BF16)
        for h in range(feat // HEAD):
            lanes = slice(h * HEAD, (h + 1) * HEAD)
            q = qkv[slot, 0, :, lanes] * BF16(scale)
            k = qkv[slot, 1, :, lanes]
            v = qkv[slot, 2, :, lanes]
            d_o = d_mixed[:, lanes]
            scores = jnp.where(seg_col == seg_row, dot(q, k, 1, 1), masked_score)
            expo = jnp.exp(scores - jnp.max(scores, axis=1, keepdims=True))
            probs = expo * (1.0 / jnp.sum(expo, axis=1, keepdims=True))
            d_p = dot(d_o, v, 1, 1)
            d_s = (probs * (d_p - jnp.sum(d_p * probs, axis=1, keepdims=True))).astype(BF16)
            d_proj[:, h * HEAD : (h + 1) * HEAD] = (dot(d_s, k, 1, 0) * scale).astype(BF16)
            d_proj[:, feat + h * HEAD : feat + (h + 1) * HEAD] = dot(d_s, q, 0, 0).astype(BF16)
            d_proj[:, 2 * feat + h * HEAD : 2 * feat + (h + 1) * HEAD] = dot(probs.astype(BF16), d_o, 0, 0).astype(BF16)
        small = parts.shape[3]
        store(2, r, 0, dot(mixed[slot], d_attn[...], 0, 0))
        store(2, r, feat // small, dot(d_proj[...], x[...], 0, 0))
        exchange(2, r)
        vec[r, 6:7, : 3 * feat] = jnp.sum(d_proj[...].astype(F32), axis=0, keepdims=True)
        value = total[...]
        for j in range(3):
            value = value + dot(d_proj[:, j * feat : (j + 1) * feat], w_qkv[slot, j], 1, 0)
        total[...] = value

        @pl.loop(4 + i + (i + 1) // 2, 6 + i + i // 2)
        def _(n):
            tick(n)

    for copy in vec_near:
        copy.start()
    low_tok[...] = total[...].astype(BF16)
    tok_near.start()
    tok_own.start()
    for copy in vec_near:
        copy.wait_recv()
    vec_b[...] = vec[2] + vec_a[1]
    vec_far.start()
    vec_s[0] = vec[0] + vec_a[0]
    tok_far.start()

    @pl.loop(10, count + 6 + extra)
    def _(i):
        @pl.when(i == count)
        def _():
            vec_far.wait()
            vec_s[0] = vec_s[0] + vec_r[0]
            vec_dp[0].start()

        for b in range(bits):
            @pl.when(i == count + 1 + b)
            def _(b=b):
                vec_dp[b].wait()
                value = vec_s[b] + vec_r[1 + b]
                if b + 1 < bits:
                    vec_s[b + 1] = value
                    vec_dp[b + 1].start()
                else:
                    vec_out[...] = value

        tick(i)

    tok_far.wait_recv()
    tok_pass.start()
    for copy in vec_near:
        copy.wait_send()
    for k in range(KINDS):
        for j in range(2):
            near_copy(k, j).wait_send()

    @pl.loop(0, count)
    def _(c):
        for copy in (far_copy, x_copy, p_copy, q_copy, gq_copy, gp_copy, gx_copy):
            copy(c).wait_send()

    tok_near.wait()
    tok_far.wait_send()
    tok_own.wait()
    tok_pass.wait()


def backward(
    d_query, extents, small_vectors, upstream, n1, inv1, n2, inv2, h1_low, act, slope, w_up, w_down,
    qkv, mixed, w_out, w_qkv, x, ndp, nmp, block,
):
    rows, wide = x.shape
    feat, hidden = mixed.shape[2], act.shape[2]
    count = KINDS * CHUNKS
    pieces = CHUNKS * PIECES
    small = wide // pieces
    bits = ndp.bit_length() - 1
    extra = max(bits - 3, 1)
    vmem, anywhere = pl.BlockSpec(memory_space=pltpu.VMEM), pl.BlockSpec(memory_space=pl.ANY)
    dma = pltpu.SemaphoreType.DMA
    sds = jax.ShapeDtypeStruct
    vec = (8, wide)
    low, full = (lambda *shape: pltpu.VMEM(shape, BF16)), (lambda *shape: pltpu.VMEM(shape, F32))
    two = lambda a: low(2, *a.shape[1:])
    pair = lambda *shape: [dma(shape), dma(shape)]
    scratch = [full(rows, wide), full(*n1.shape), full(*inv1.shape), full(*n2.shape), full(*inv2.shape)]
    scratch += [low(rows, wide), low(rows, wide), low(*act.shape), two(slope), two(w_up), two(w_down)]
    scratch += [two(qkv), two(mixed), two(w_out), two(w_qkv)]
    scratch += [low(rows, wide), low(rows, wide), low(rows, 3 * feat), low(rows, wide)]
    scratch += [low(KINDS, nmp, pieces, small, wide), full(nmp, *vec), low(KINDS, 2, pieces, small, wide)]
    scratch += [low(count, n, small, wide) for n in (8, 4, 2, 1)] + [low(extra, count, 1, small, wide)]
    scratch += [full(2, *vec), full(*vec), full(bits, *vec), full(bits + 1, *vec)]
    scratch += [dma((8,)), dma((2, 3)), dma((2, 4))]
    scratch += pair(2 * KINDS) + pair(count) * 4 + pair(extra, count) + pair(count) * 3
    scratch += pair(2) + pair(bits + 1) + pair(3) + [dma]
    out = pl.pallas_call(
        functools.partial(backward_kernel, ndp, nmp, block),
        out_shape=(sds((count, PIECES, small, wide), BF16), sds(vec, F32), sds((nmp, rows, wide), BF16)),
        in_specs=[vmem, pl.BlockSpec(memory_space=pltpu.SMEM), vmem] + [anywhere] * 15,
        out_specs=(vmem, vmem, anywhere),
        scratch_shapes=scratch,
        compiler_params=pltpu.CompilerParams(
            collective_id=1, has_side_effects=True, vmem_limit_bytes=67043328
        ),
        name="backward",
    )(
        d_query, extents, small_vectors, upstream, n1, inv1, n2, inv2, h1_low, act, slope, w_up, w_down,
        qkv, mixed, w_out, w_qkv, x,
    )
    return out[0].reshape(KINDS, wide, wide), out[1], out[2].reshape(-1, wide)


def local(
    encoder_rows,
    piece_extent_sequence,
    triple_projection_matrix,
    asker_content_shifts,
    mixing_result_matrix,
    mixing_result_offset_vector,
    mixing_normalizer_scale,
    mixing_normalizer_shift,
    widen_matrix,
    widen_shift_vector,
    narrow_matrix,
    narrow_shift_vector,
    perceptron_normalizer_scale,
    perceptron_normalizer_shift,
    document_vectors,
    sharpness_factor,
    correct_document_position,
    upstream_sensitivity,
    *,
    width,
    depth,
):
    nblock = piece_extent_sequence.shape[0]
    block = encoder_rows.shape[0] // nblock
    rows = encoder_rows.shape[0] // width
    feat = triple_projection_matrix.shape[2]
    hidden = widen_matrix.shape[1]
    wide = encoder_rows.shape[1]

    w_qkv = triple_projection_matrix.transpose(0, 2, 1)
    small = jnp.concatenate(
        [jnp.pad(asker_content_shifts, ((0, 0), (0, hidden - feat))), widen_shift_vector[None]]
    )
    (
        qkv, mixed, n1, inv1, n2, inv2, h1_low, act, slope, w_qkv, w_out, w_up, w_down, own_out, query, x,
    ), small_vectors = encode(
        encoder_rows, piece_extent_sequence, w_qkv, mixing_result_matrix, widen_matrix,
        narrow_matrix, small, mixing_result_offset_vector, mixing_normalizer_scale, mixing_normalizer_shift,
        narrow_shift_vector, perceptron_normalizer_scale, perceptron_normalizer_shift, block, width,
    )
    d_query, seg_loss, sharpness_derivative, layer_out = retrieval(
        query, own_out, document_vectors, correct_document_position[:, None], sharpness_factor, depth, width
    )
    layer_out = layer_out.reshape(-1, wide)
    sums, vectors, grad_tokens = backward(
        d_query, piece_extent_sequence, small_vectors, upstream_sensitivity, n1, inv1, n2, inv2, h1_low, act, slope,
        w_up, w_down, qkv, mixed, w_out, w_qkv, x, depth, width, block,
    )
    grad_tokens = grad_tokens.astype(F32)
    grad_qkv = sums[2, feat:].astype(F32).reshape(3, feat, wide).transpose(0, 2, 1)
    return (
        layer_out,
        seg_loss[0],
        grad_tokens,
        grad_qkv,
        jnp.stack([vectors[6, :feat], vectors[6, 2 * feat : 3 * feat]]),
        sums[2, :feat].astype(F32),
        vectors[0],
        vectors[1],
        vectors[2],
        sums[1].astype(F32),
        vectors[7, :hidden],
        sums[0].astype(F32),
        vectors[3],
        vectors[4],
        vectors[5],
        sharpness_derivative[0],
    )


def solution(mesh):
    in_specs = (
        P("dp", None),
        P("dp", None),
        P(None, None, "mp"),
        P(None, "mp"),
        P("mp", None),
        P(),
        P(),
        P(),
        P(None, "mp"),
        P("mp"),
        P("mp", None),
        P(),
        P(),
        P(),
        P(("dp", "mp"), None),
        P(),
        P(),
        P("dp", None),
    )
    out_specs = (
        P("dp", None),
        P(),
        P("dp", None),
        P(None, None, "mp"),
        P(None, "mp"),
        P("mp", None),
        P(),
        P(),
        P(),
        P(None, "mp"),
        P("mp"),
        P("mp", None),
        P(),
        P(),
        P(),
        P(),
    )
    width = mesh.shape["mp"]

    def step(*args):
        return local(*args, width=width, depth=mesh.shape["dp"])

    return jax.shard_map(step, mesh=mesh, in_specs=in_specs, out_specs=out_specs, check_vma=False)
```

```python
import functools
import math

import jax
import jax.numpy as jnp
from jax import lax
from jax.experimental import pallas as pl
from jax.experimental.pallas import tpu as pltpu
from jax.sharding import PartitionSpec as P

HEAD = 64
F32 = jnp.float32
BF16 = jnp.bfloat16
MESH = pl.DeviceIdType.MESH
norm_epsilon = 1e-05
masked_score = -1e30


def dot(a, b, ca, cb):
    return lax.dot_general(a, b, (((ca,), (cb,)), ((), ())), preferred_element_type=F32)


def norm_stats(resid):
    centre = jnp.mean(resid, axis=-1, keepdims=True)
    centred = resid - centre
    spread = jnp.mean(centred * centred, axis=-1, keepdims=True)
    inv = lax.rsqrt(spread + norm_epsilon)
    return centred * inv, inv


def norm_back(d_out, normed, inv, gain):
    e = d_out * gain
    return inv * (
        e - jnp.mean(e, axis=-1, keepdims=True) - normed * jnp.mean(e * normed, axis=-1, keepdims=True)
    )


def flip(index, step):
    return index + step * (1 - 2 * lax.rem(index // step, 2))


def retrieval_kernel(
    ndp, nmp, query_ref, own_ref, docs_hbm, gold_ref, sharp_ref, dq_ref, loss_ref, ds_ref, layer,
    queries, docs, low, stats, columns, part_u, part_g, send, got, doc_sem, q_send, q_recv, s_send, s_recv, d_send, d_recv,
    l_s, l_r, own_sem,
):
    n = ndp * nmp
    own = query_ref.shape[0]
    nseg = gold_ref.shape[1]
    tile = 256 if nseg <= 256 else 128
    dp, mp = lax.axis_index("dp"), lax.axis_index("mp")
    me = dp * nmp + mp
    load = pltpu.make_async_copy(docs_hbm, docs, doc_sem)
    load.start()
    barrier = pltpu.get_barrier_semaphore()

    def device(step):
        other = lax.rem(me + step, n)
        return other, (other // nmp, lax.rem(other, nmp))

    @pl.loop(1, n)
    def _(step):
        _, where = device(step)
        pl.semaphore_signal(barrier, inc=1, device_id=where, device_id_type=MESH)

    pl.semaphore_wait(barrier, n - 1)

    def push(source, target, send_sems, recv_sems):
        @pl.loop(1, n)
        def _(step):
            other, where = device(step)
            pltpu.make_async_remote_copy(
                source(other), target, send_sems.at[step], recv_sems.at[step], device_id=where, device_id_type=MESH
            ).start()

    def drain(source, target, send_sems, recv_sems):
        @pl.loop(1, n)
        def _(step):
            other, where = device(step)
            copy = pltpu.make_async_remote_copy(
                source(other), target, send_sems.at[step], recv_sems.at[step], device_id=where, device_id_type=MESH
            )
            copy.wait()

    push(lambda other: query_ref, queries.at[me], q_send, q_recv)
    queries[me] = query_ref[...]
    drain(lambda other: query_ref, queries.at[me], q_send, q_recv)
    near, far, across = (dp, flip(mp, 1)), (dp, flip(mp, 2)), flip(mp, 2)

    def spread(source, target, i, where):
        return pltpu.make_async_remote_copy(
            source, target, l_s.at[i], l_r.at[i], device_id=where, device_id_type=MESH
        )

    to_near = spread(own_ref, layer.at[mp], 0, near)
    to_far, to_pass, first = [], [], 0
    for i, part in enumerate((7, 6, 3)):
        strip = pl.ds(first, own_ref.shape[0] * part // 16)
        first += own_ref.shape[0] * part // 16
        passed = layer.at[across, strip]
        to_far.append(spread(own_ref.at[strip], layer.at[mp, strip], 1 + i, far))
        to_pass.append(spread(passed, passed, 4 + i, near))
    keep = pltpu.make_async_copy(own_ref, layer.at[mp], own_sem)
    to_far[0].start()
    to_near.start()
    keep.start()
    load.wait()

    sharp = sharp_ref[0]
    offset = me * docs.shape[0]
    ids = lax.broadcasted_iota(jnp.int32, (tile, docs.shape[0]), 1).astype(F32)
    columns[...] = jnp.broadcast_to((gold_ref[...] - offset).astype(F32), (128, nseg)).T
    lane = lax.broadcasted_iota(jnp.int32, (tile, 128), 1)
    per = tile // own

    @pl.loop(0, nseg // tile)
    def _(i):
        span = pl.ds(pl.multiple_of(i * tile, tile), tile)
        q = queries[pl.ds(i * per, per)].reshape(tile, queries.shape[2])
        logit = lax.dot_general(q, docs[...], (((1,), (1,)), ((), ())), preferred_element_type=F32) / sharp
        match = ids == columns[span, 0:1]
        top = jnp.max(logit, axis=1, keepdims=True)
        expo = jnp.exp(logit - top)
        total = jnp.sum(expo, axis=1, keepdims=True)
        tilt = jnp.sum(expo * logit, axis=1, keepdims=True)
        gold = jnp.sum(jnp.where(match, logit, 0.0), axis=1, keepdims=True)
        packed = jnp.where(lane == 0, top, jnp.where(lane == 1, total, jnp.where(lane == 2, tilt, gold)))
        stats[me, :, span] = packed.T[:4]
        low[span, :] = jnp.where(match, 0.0, expo).astype(BF16)

    push(lambda other: stats.at[me], stats.at[me], s_send, s_recv)
    to_far[1].start()

    @pl.loop(0, nseg // tile)
    def _(i):
        span = pl.ds(pl.multiple_of(i * tile, tile), tile)
        part_u[span, :] = jnp.dot(low[span, :], docs[...], preferred_element_type=F32)
        match = ids == columns[span, 0:1]
        part_g[span, :] = jnp.dot(
            match.astype(F32).astype(BF16), docs[...], preferred_element_type=F32
        ).astype(BF16)

    drain(lambda other: stats.at[me], stats.at[me], s_send, s_recv)
    to_far[0].wait_recv()
    to_pass[0].start()

    tops = stats[:, 0, :]
    top = jnp.max(tops, axis=0, keepdims=True)
    share = jnp.exp(tops - top)
    total = jnp.sum(stats[:, 1, :] * share, axis=0, keepdims=True)
    tilt = jnp.sum(stats[:, 2, :] * share, axis=0, keepdims=True)
    gold = jnp.sum(stats[:, 3, :], axis=0, keepdims=True)
    lse = top + jnp.log(total)
    loss_ref[...] = lse - gold
    ds_ref[...] = -jnp.sum(tilt / total - gold, axis=1, keepdims=True) / sharp
    scale = jnp.exp(stats[me, 0:1, :] - lse) / sharp
    gold_scale = (jnp.exp(gold - lse) - 1.0) / sharp
    row = lax.broadcasted_iota(jnp.int32, (128, nseg), 0)
    columns[...] = jnp.where(row == 0, scale, gold_scale).T

    @pl.loop(0, nseg // tile)
    def _(i):
        span = pl.ds(pl.multiple_of(i * tile, tile), tile)
        value = part_u[span, :] * columns[span, 0:1] + part_g[span, :].astype(F32) * columns[span, 1:2]
        send[pl.ds(i * per, per)] = value.astype(BF16).reshape(per, own, value.shape[1])

    push(lambda other: send.at[other], got.at[me], d_send, d_recv)
    to_far[2].start()
    to_far[1].wait_recv()
    to_pass[1].start()
    got[me] = send[me]
    drain(lambda other: send.at[other], got.at[me], d_send, d_recv)
    dq_ref[...] = jnp.sum(got[...].astype(F32), axis=0)
    to_far[2].wait_recv()
    to_pass[2].start()
    to_near.wait()
    for copy in to_far:
        copy.wait_send()
    for copy in to_pass:
        copy.wait()
    keep.wait()


def retrieval(query, own_out, docs, gold, sharp, ndp, nmp):
    n = ndp * nmp
    own, width = query.shape
    nseg = gold.shape[1]
    vmem = pl.BlockSpec(memory_space=pltpu.VMEM)
    return pl.pallas_call(
        functools.partial(retrieval_kernel, ndp, nmp),
        out_shape=(
            jax.ShapeDtypeStruct((own, width), F32),
            jax.ShapeDtypeStruct((1, nseg), F32),
            jax.ShapeDtypeStruct((1, 1), F32),
            jax.ShapeDtypeStruct((nmp,) + own_out.shape, BF16),
        ),
        in_specs=[vmem, vmem, pl.BlockSpec(memory_space=pl.ANY), vmem, pl.BlockSpec(memory_space=pltpu.SMEM)],
        out_specs=(vmem, vmem, vmem, pl.BlockSpec(memory_space=pl.ANY)),
        scratch_shapes=[
            pltpu.VMEM((n, own, width), BF16),
            pltpu.VMEM(docs.shape, BF16),
            pltpu.VMEM((nseg, docs.shape[0]), BF16),
            pltpu.VMEM((n, 4, nseg), F32),
            pltpu.VMEM((nseg, 128), F32),
            pltpu.VMEM((nseg, width), F32),
            pltpu.VMEM((nseg, width), BF16),
            pltpu.VMEM((n, own, width), BF16),
            pltpu.VMEM((n, own, width), BF16),
            pltpu.SemaphoreType.DMA,
        ]
        + [pltpu.SemaphoreType.DMA((n,))] * 6
        + [pltpu.SemaphoreType.DMA((7,))] * 2
        + [pltpu.SemaphoreType.DMA],
        compiler_params=pltpu.CompilerParams(
            collective_id=0, has_side_effects=True, vmem_limit_bytes=60 * 2**20
        ),
        name="retrieval",
    )(query, own_out, docs, gold, sharp)


def gelu_with_slope(u):
    z = jnp.abs(u) * (0.5**0.5)
    t = 1.0 / (1.0 + 0.5 * z)
    poly = 0.17087277
    for c in (
        -0.82215223, 1.48851587, -1.13520398, 0.27886807, -0.18628806, 0.09678418, 0.37409196, 1.00002368,
    ):
        poly = poly * t + c
    square = z * z
    tail = 0.5 * t * jnp.exp(poly * t - 1.26551223 - square)
    cdf = jnp.where(u < 0, tail, 1.0 - tail)
    return u * cdf, cdf + u * (jnp.exp(-square) * ((2 * math.pi) ** -0.5))


def encode_kernel(nmp, block, *refs):
    (
        rows_hbm, extents, w_qkv, w_out, w_up, w_down, small_ref, *vectors,
    ) = refs[:13]
    out_bias, gain1, shift1, down_bias, gain2, shift2 = (v[...][None] for v in vectors)
    (
        qkv_o, mixed_o, n1_o, inv1_o, n2_o, inv2_o, low_o, act_o, slope_o, w_qkv_o, w_out_o, w_up_o, w_down_o,
        own_o, query_o, x_o,
    ) = refs[13:29]
    (
        x, qkv, mixed, n1, n2, h1_low, act, slope, all_qkv, all_out, all_up, all_down, small, total,
        fill_sem, save_sem, n_s, n_r, m_s, m_r, y_s, y_r, f_s, f_r, g_s, g_r, h_s, h_r, sm_s, sm_r,
    ) = refs[29:]
    dp, mp = lax.axis_index("dp"), lax.axis_index("mp")
    near, far, side = (dp, flip(mp, 1)), (dp, flip(mp, 2)), (flip(dp, 1), mp)
    b = lax.rem(dp, 2)
    rows = x.shape[0]
    feat = w_out.shape[0] * w_out.shape[1]
    scale = HEAD ** (-0.5)

    own_rows = rows_hbm.at[pl.ds(pl.multiple_of(mp * rows, rows), rows)]
    fills = [
        pltpu.make_async_copy(source, target, fill_sem.at[i])
        for i, (source, target) in enumerate(
            [
                (own_rows, x), (w_qkv, all_qkv.at[0]), (w_out, all_out.at[0]), (w_up, all_up.at[0]),
                (w_down, all_down.at[0]),
            ]
        )
    ]
    for copy in fills:
        copy.start()
    barrier = pltpu.get_barrier_semaphore()
    for where in (near, far, side):
        pl.semaphore_signal(barrier, inc=1, device_id=where, device_id_type=MESH)
    pl.semaphore_wait(barrier, 3)

    def remote(source, target, send, recv, where):
        return pltpu.make_async_remote_copy(source, target, send, recv, device_id=where, device_id_type=MESH)

    pieces = [(w_qkv.at[k], all_qkv, k) for k in range(3)] + [(w_out, all_out, None)]
    pieces += [(w_up.at[s], all_up, s) for s in range(w_up.shape[0])]
    pieces += [(w_down.at[s], all_down, s) for s in range(w_down.shape[0])]
    count = len(pieces)

    def slot(i, r):
        _, held, s = pieces[i]
        return held.at[r] if s is None else held.at[r, s]

    near_own = [remote(pieces[i][0], slot(i, 1), n_s.at[i], n_r.at[i], near) for i in range(count)]
    far_own = [remote(pieces[i][0].at[b], slot(i, 2).at[b], y_s.at[i], y_r.at[i], far) for i in range(count)]
    pass_side = [remote(slot(i, 2).at[b], slot(i, 2).at[b], f_s.at[i], f_r.at[i], side) for i in range(count)]
    pass_near = [remote(slot(i, 2).at[b], slot(i, 3).at[b], g_s.at[i], g_r.at[i], near) for i in range(count)]
    pass_other = [
        remote(slot(i, 2).at[1 - b], slot(i, 3).at[1 - b], h_s.at[i], h_r.at[i], near) for i in range(count)
    ]
    small_near = remote(small_ref, small.at[1], sm_s.at[0], sm_r.at[0], near)
    small_far = remote(small_ref, small.at[2], sm_s.at[1], sm_r.at[1], far)
    small_pass = remote(small.at[2], small.at[3], sm_s.at[2], sm_r.at[2], near)

    small_near.start()
    small_far.start()
    for i in range(count):
        far_own[i].start()
        near_own[i].start()
    small[0] = small_ref[...]
    by_quarter = [
        (qkv, qkv_o), (mixed, mixed_o), (act, act_o), (slope, slope_o), (all_qkv, w_qkv_o), (all_out, w_out_o),
        (all_up, w_up_o), (all_down, w_down_o),
    ]
    at_once = [(x, x_o), (n1, n1_o), (h1_low, low_o), (n2, n2_o)]

    def save(i, r):
        source, target = by_quarter[i]
        return pltpu.make_async_copy(source.at[r], target.at[r], save_sem.at[4 * i + r])

    def save_whole(i):
        source, target = at_once[i]
        return pltpu.make_async_copy(source, target, save_sem.at[4 * len(by_quarter) + i])

    def relay(i):
        far_own[i].wait_recv()
        pass_side[i].start()
        pass_near[i].start()

    def relay_other(i):
        pass_side[i].wait_recv()
        pass_other[i].start()

    def last_arrived(i):
        pass_near[i].wait_recv()
        pass_other[i].wait_recv()

    iota_row = lax.broadcasted_iota(jnp.int32, (1, rows), 1)
    iota_col = lax.broadcasted_iota(jnp.int32, (rows, 1), 0)
    nblk = rows // block
    nseg = extents.shape[1]
    seg_row, seg_col = jnp.zeros_like(iota_row), jnp.zeros_like(iota_col)
    starts = []
    for i in range(nblk):
        end = jnp.int32(i * block)
        for j in range(nseg):
            starts.append(end)
            end = end + extents[mp * nblk + i, j]
            seg_row = seg_row + (iota_row >= end).astype(jnp.int32)
            seg_col = seg_col + (iota_col >= end).astype(jnp.int32)
    wide = x.shape[1]
    ups, downs = range(4, 4 + w_up.shape[0]), range(4 + w_up.shape[0], count)

    def head(r, h):
        lanes = slice(h * HEAD, (h + 1) * HEAD)
        q = qkv[r, 0, :, lanes] * BF16(scale)
        scores = dot(q, qkv[r, 1, :, lanes], 1, 1)
        scores = jnp.where(seg_col == seg_row, scores, masked_score)
        expo = jnp.exp(scores - jnp.max(scores, axis=1, keepdims=True))
        probs = (expo * (1.0 / jnp.sum(expo, axis=1, keepdims=True))).astype(BF16)
        mixed[r, :, lanes] = jnp.dot(probs, qkv[r, 2, :, lanes], preferred_element_type=F32).astype(BF16)

    def both(i):
        relay(i)
        relay_other(i - 1)

    def on(r, at, *steps):
        @pl.when(r == at)
        def _():
            for step in steps:
                step()

    near_in = lambda group: [near_own[i].wait_recv for i in group]
    last_in = lambda group: [functools.partial(last_arrived, i) for i in group]
    do = functools.partial
    fills[0].wait()
    fills[1].wait()
    save_whole(0).start()

    @pl.loop(0, nmp)
    def _(r):
        on(r, 1, small_near.wait_recv, *near_in(range(3)))
        on(
            r, 2, small_far.wait_recv, small_pass.start, do(relay, 0), do(relay, 1), do(relay_other, 0), do(relay, 2),
            do(relay_other, 1), do(relay, 3), do(relay_other, 2),
        )
        on(r, 3, small_pass.wait_recv, *last_in(range(3)))
        for k in range(3):
            value = dot(x[...], all_qkv[r, k].reshape(feat, wide), 1, 1)
            if k == 0:
                value = value + small[r, 0:1, :feat]
            if k == 2:
                value = value + small[r, 1:2, :feat]
            qkv[r, k] = value.astype(BF16)
        save(0, r).start()
        save(4, r).start()
        head(r, 0)
        on(r, 2, do(relay_other, 3))
        on(r, 3, do(both, 5))
        head(r, 1)
        on(r, 2, do(relay, 4))
        for h in range(2, feat // HEAD):
            head(r, h)
        save(1, r).start()

    fills[2].wait()
    near_own[3].wait_recv()
    last_arrived(3)
    total[...] = x[...].astype(F32) + out_bias

    @pl.loop(0, nmp)
    def _(r):
        total[...] += jnp.dot(mixed[r], all_out[r].reshape(feat, wide), preferred_element_type=F32)
        save(5, r).start()

    tile = 128

    @pl.loop(0, rows // tile)
    def _(t):
        span = pl.ds(pl.multiple_of(t * tile, tile), tile)
        normed, inv = norm_stats(total[span])
        n1[span] = normed
        inv1_o[span] = jnp.broadcast_to(inv, (tile, inv1_o.shape[1]))
        h1 = normed * gain1 + shift1
        total[span] = h1 + down_bias
        h1_low[span] = h1.astype(BF16)

    save_whole(1).start()
    save_whole(2).start()
    both(6)
    fills[3].wait()
    fills[4].wait()

    @pl.loop(0, nmp)
    def _(r):
        on(r, 1, *near_in(ups))
        on(r, 3, *last_in(ups))
        upper = jnp.dot(h1_low[...], all_up[r].reshape(wide, -1), preferred_element_type=F32) + small[r, 2:3, :]
        value, gradient = gelu_with_slope(upper)
        act[r] = value.astype(BF16)
        slope[r] = gradient.astype(BF16)
        for i in (2, 3, 6):
            save(i, r).start()
        on(r, 0, do(both, 7))
        on(r, 1, do(both, 8), *near_in(downs))
        on(r, 2, do(both, 9), do(relay_other, 9))
        on(r, 3, *last_in(downs))
        total[...] += jnp.dot(act[r], all_down[r].reshape(-1, wide), preferred_element_type=F32)
        save(7, r).start()

    @pl.loop(0, rows // tile)
    def _(t):
        span = pl.ds(pl.multiple_of(t * tile, tile), tile)
        normed, inv = norm_stats(total[span])
        n2[span] = normed
        inv2_o[span] = jnp.broadcast_to(inv, (tile, inv2_o.shape[1]))
        own_o[span] = (normed * gain2 + shift2).astype(BF16)

    save_whole(3).start()
    line = lax.broadcasted_iota(jnp.int32, (len(starts), rows), 0)
    first = jnp.zeros((len(starts), rows), jnp.int32)
    for j, start in enumerate(starts):
        first = jnp.where(line == j, start, first)
    pick = (lax.broadcasted_iota(jnp.int32, first.shape, 1) == first).astype(F32).astype(BF16)
    query_o[...] = jnp.dot(pick, own_o[...], preferred_element_type=F32).astype(BF16)
    for i in range(len(at_once)):
        save_whole(i).wait()

    @pl.loop(0, nmp)
    def _(r):
        for i in range(len(by_quarter)):
            save(i, r).wait()

    for copy in near_own + far_own + pass_side + pass_near + pass_other + [small_near, small_far, small_pass]:
        copy.wait_send()


STRIPS = 3


def encode(
    encoder_rows, extents, w_qkv, w_out, w_up, w_down, small, out_bias, gain1, shift1, down_bias, gain2, shift2,
    block, nmp,
):
    rows = encoder_rows.shape[0] // nmp
    wide = encoder_rows.shape[1]
    feat, hidden = w_qkv.shape[1], w_up.shape[1]
    nseg = extents.shape[0] * extents.shape[1] // nmp
    cut_qkv = w_qkv.reshape(3, 2, feat // 2, wide)
    cut_out = w_out.reshape(2, feat // 2, wide)
    cut_up = w_up.reshape(STRIPS, 2, wide // (2 * STRIPS), hidden)
    cut_down = w_down.reshape(STRIPS, 2, hidden // (2 * STRIPS), wide)
    vmem, anywhere = pl.BlockSpec(memory_space=pltpu.VMEM), pl.BlockSpec(memory_space=pl.ANY)
    sds = jax.ShapeDtypeStruct
    dma = pltpu.SemaphoreType.DMA
    every = lambda a: (nmp,) + a.shape
    held = [
        sds((nmp, 3, rows, feat), BF16),
        sds((nmp, rows, feat), BF16),
        sds((rows, wide), F32),
        sds((rows, 128), F32),
        sds((rows, wide), F32),
        sds((rows, 128), F32),
        sds((rows, wide), BF16),
        sds((nmp, rows, hidden), BF16),
        sds((nmp, rows, hidden), BF16),
        sds(every(cut_qkv), BF16),
        sds(every(cut_out), BF16),
        sds(every(cut_up), BF16),
        sds(every(cut_down), BF16),
        sds((rows, wide), BF16),
        sds((nseg, wide), BF16),
        sds((rows, wide), BF16),
    ]
    count = 4 + 2 * STRIPS
    scratch = [
        pltpu.VMEM((rows, wide), BF16),
        pltpu.VMEM(held[0].shape, BF16),
        pltpu.VMEM(held[1].shape, BF16),
        pltpu.VMEM((rows, wide), F32),
        pltpu.VMEM((rows, wide), F32),
        pltpu.VMEM((rows, wide), BF16),
        pltpu.VMEM(held[7].shape, BF16),
        pltpu.VMEM(held[8].shape, BF16),
    ]
    scratch += [pltpu.VMEM(h.shape, BF16) for h in held[9:13]]
    scratch += [pltpu.VMEM(every(small), F32), pltpu.VMEM((rows, wide), F32), dma((5,)), dma((36,))]
    scratch += [dma((count,))] * 12 + [dma((3,))] * 2
    outs = pl.pallas_call(
        functools.partial(encode_kernel, nmp, block),
        out_shape=tuple(held),
        in_specs=[anywhere, pl.BlockSpec(memory_space=pltpu.SMEM)] + [anywhere] * 4 + [vmem] * 7,
        out_specs=tuple(vmem if i in (3, 5, 13, 14) else anywhere for i in range(len(held))),
        scratch_shapes=scratch,
        compiler_params=pltpu.CompilerParams(collective_id=2, has_side_effects=True, vmem_limit_bytes=62 * 2**20),
        name="encode",
    )(encoder_rows, extents, cut_qkv, cut_out, cut_up, cut_down, small, out_bias, gain1, shift1, down_bias, gain2, shift2)
    outs = list(outs)
    outs[9] = outs[9].reshape(nmp, 3, feat, wide)
    outs[10] = outs[10].reshape(nmp, feat, wide)
    outs[11] = outs[11].reshape(nmp, wide, hidden)
    outs[12] = outs[12].reshape(nmp, hidden, wide)
    return outs


PIECES = 8
CHUNKS = 6
KINDS = 3
LAGS = (0, 2, 3, 5, 6, 8, 10)


def backward_kernel(ndp, nmp, block, *refs):
    (
        d_query, extents, gain1, gain2, upstream_h, n1_h, inv1_h, n2_h, inv2_h, low_h, act_h, slope_h, up_h, down_h,
        qkv_h, mixed_h, w_out_h, w_qkv_h, x_h,
    ) = refs[:19]
    out, vec_out, tok = refs[19:22]
    (
        total, n1, inv1, n2, inv2, h1_low, x, act, slope, w_up, w_down, qkv, mixed, w_out, w_qkv,
        d_ffn, d_attn, d_proj, low_tok, parts, vec, near, got_y, got_x, got_1, got_2, got_e,
        vec_a, vec_b, vec_s, vec_r,
        load_sem, ffn_sem, attn_sem, a_s, a_r, y_s, y_r, x_s, x_r, p_s, p_r, q_s, q_r, e_s, e_r,
        gq_s, gq_r, gp_s, gp_r, gx_s, gx_r, va_s, va_r, v_s, v_r, t_s, t_r, own_sem,
    ) = refs[22:]
    count = KINDS * CHUNKS
    bits = ndp.bit_length() - 1
    extra = bits - 3
    rows, wide = total.shape
    feat = mixed.shape[2]
    hidden = act.shape[2]
    dp, mp = lax.axis_index("dp"), lax.axis_index("mp")
    near_dev, far_dev = (dp, flip(mp, 1)), (dp, flip(mp, 2))
    dp_dev = [(flip(dp, 1 << b), mp) for b in range(bits)]
    b0, b1, b2 = (lax.rem(dp // (1 << b), 2) for b in range(3))
    ident = b0 * 4 + b1 * 2 + b2
    gain1, gain2 = gain1[...][None], gain2[...][None]

    own_rows = upstream_h.at[pl.ds(pl.multiple_of(mp * rows, rows), rows)]
    loads = [
        pltpu.make_async_copy(source, target, load_sem.at[i])
        for i, (source, target) in enumerate(
            [
                (own_rows, total), (n2_h, n2), (inv2_h, inv2), (act_h, act), (low_h, h1_low), (n1_h, n1),
                (inv1_h, inv1), (x_h, x),
            ]
        )
    ]

    def ffn_loads(i):
        r, slot = 3 - i, lax.rem(i, 2)
        return [
            pltpu.make_async_copy(source.at[r], target.at[slot], ffn_sem.at[slot, j])
            for j, (source, target) in enumerate([(down_h, w_down), (slope_h, slope), (up_h, w_up)])
        ]

    def attn_loads(i):
        r, slot = 3 - i, lax.rem(i, 2)
        return [
            pltpu.make_async_copy(source.at[r], target.at[slot], attn_sem.at[slot, j])
            for j, (source, target) in enumerate([(w_out_h, w_out), (qkv_h, qkv), (mixed_h, mixed), (w_qkv_h, w_qkv)])
        ]

    for copy in loads + ffn_loads(0):
        copy.start()
    barrier = pltpu.get_barrier_semaphore()
    for where in [near_dev, far_dev] + dp_dev:
        pl.semaphore_signal(barrier, inc=1, device_id=where, device_id_type=MESH)
    pl.semaphore_wait(barrier, 2 + bits)

    def remote(source, target, send, recv, where):
        return pltpu.make_async_remote_copy(source, target, send, recv, device_id=where, device_id_type=MESH)

    def part(c, r, first=0, many=PIECES):
        k = c // CHUNKS
        return parts.at[k, r, pl.ds((c - k * CHUNKS) * PIECES + first, many)]

    def near_copy(k, j):
        return remote(parts.at[k, 2 * j + 1], near.at[k, j], a_s.at[2 * k + j], a_r.at[2 * k + j], near_dev)

    def far_copy(c):
        return remote(part(c, 2), got_y.at[c], y_s.at[c], y_r.at[c], far_dev)

    def x_copy(c):
        return remote(part(c, 0, (1 - b0) * 4, 4), got_x.at[c], x_s.at[c], x_r.at[c], dp_dev[0])

    def p_copy(c):
        return remote(part(c, 0, b0 * 4 + (1 - b1) * 2, 2), got_1.at[c], p_s.at[c], p_r.at[c], dp_dev[1])

    def q_copy(c):
        return remote(part(c, 0, ident + 1 - 2 * b2, 1), got_2.at[c], q_s.at[c], q_r.at[c], dp_dev[2])

    def e_copy(c, e):
        return remote(part(c, 0, ident, 1), got_e.at[e, c], e_s.at[e, c], e_r.at[e, c], dp_dev[3 + e])

    def gq_copy(c):
        held = out.at[c, b0, b1, b2]
        return remote(held, held, gq_s.at[c], gq_r.at[c], dp_dev[2])

    def gp_copy(c):
        held = out.at[c, b0, b1]
        return remote(held, held, gp_s.at[c], gp_r.at[c], dp_dev[1])

    def gx_copy(c):
        held = out.at[c, b0]
        return remote(held, held, gx_s.at[c], gx_r.at[c], dp_dev[0])

    vec_near = [remote(vec.at[2 * j + 1], vec_a.at[j], va_s.at[j], va_r.at[j], near_dev) for j in range(2)]
    vec_far = remote(vec_b, vec_r.at[0], v_s.at[0], v_r.at[0], far_dev)
    vec_dp = [remote(vec_s.at[b], vec_r.at[1 + b], v_s.at[1 + b], v_r.at[1 + b], dp_dev[b]) for b in range(bits)]
    across = flip(mp, 2)
    tok_near = remote(low_tok, tok.at[mp], t_s.at[0], t_r.at[0], near_dev)
    tok_far = remote(low_tok, tok.at[mp], t_s.at[1], t_r.at[1], far_dev)
    tok_pass = remote(tok.at[across], tok.at[across], t_s.at[2], t_r.at[2], near_dev)
    tok_own = pltpu.make_async_copy(low_tok, tok.at[mp], own_sem)

    def add(a, b):
        return (a.astype(F32) + b.astype(F32)).astype(BF16)

    def exchange(k, r):
        j = r // 2

        @pl.when(lax.rem(r, 2) == 1)
        def _():
            near_copy(k, j).start()

        @pl.when(lax.rem(r, 2) == 0)
        def _():
            near_copy(k, j).wait_recv()

            @pl.loop(0, CHUNKS)
            def _(i):
                span = pl.ds(i * PIECES, PIECES)
                parts[k, r, span] = add(parts[k, r, span], near[k, j, span])

                @pl.when(j == 1)
                def _():
                    far_copy(k * CHUNKS + i).start()

    def tick(i):
        def at(lag, do):
            @pl.when((i >= lag) & (i - lag < count))
            def _():
                do(i - lag)

        def update(c, first, many, got):
            target = part(c, 0, first, many)
            target[...] = add(target[...], got[c])

        @functools.partial(at, LAGS[6] + extra)
        def _(c):
            gx_copy(c).wait_recv()

        @functools.partial(at, LAGS[5] + extra)
        def _(c):
            gp_copy(c).wait_recv()
            gx_copy(c).start()

        @functools.partial(at, LAGS[4] + extra)
        def _(c):
            gq_copy(c).wait_recv()
            gp_copy(c).start()

        for e in reversed(range(extra)):
            @functools.partial(at, LAGS[3] + 1 + e)
            def _(c, e=e):
                e_copy(c, e).wait()
                update(c, ident, 1, got_e.at[e])
                if e + 1 < extra:
                    e_copy(c, e + 1).start()
                else:
                    out[c, b0, b1, b2] = part(c, 0, ident, 1)[0]
                    gq_copy(c).start()

        @functools.partial(at, LAGS[3])
        def _(c):
            q_copy(c).wait_recv()
            if extra:
                update(c, ident, 1, got_2)
                e_copy(c, 0).start()
            else:
                out[c, b0, b1, b2] = add(part(c, 0, ident, 1)[0], got_2[c, 0])
                gq_copy(c).start()

        @functools.partial(at, LAGS[2])
        def _(c):
            p_copy(c).wait_recv()
            update(c, b0 * 4 + b1 * 2, 2, got_1)
            q_copy(c).start()

        @functools.partial(at, LAGS[1])
        def _(c):
            x_copy(c).wait_recv()
            update(c, b0 * 4, 4, got_x)
            p_copy(c).start()

        @functools.partial(at, 0)
        def _(c):
            far_copy(c).wait_recv()
            update(c, 0, PIECES, got_y)
            x_copy(c).start()

    tile = 128
    nblk = rows // block
    nseg = extents.shape[1]
    vec[...] = jnp.zeros_like(vec)
    for copy in loads[:3]:
        copy.wait()

    def count_up(row, value):
        vec[0, row : row + 1] += jnp.sum(value, axis=0, keepdims=True)

    @pl.loop(0, rows // tile)
    def _(t):
        span = pl.ds(pl.multiple_of(t * tile, tile), tile)
        line = lax.broadcasted_iota(jnp.int32, (tile, 1), 0) + t * tile
        d_h2 = total[span]
        for i in range(nblk):
            start = jnp.int32(i * block)
            for j in range(nseg):
                d_h2 = d_h2 + jnp.where(line == start, d_query[i * nseg + j, :][None], 0.0)
                start = start + extents[mp * nblk + i, j]
        normed = n2[span]
        count_up(5, d_h2)
        count_up(4, d_h2 * normed)
        d_r2 = norm_back(d_h2, normed, inv2[span, 0:1], gain2)
        count_up(3, d_r2)
        d_ffn[span] = d_r2.astype(BF16)
        total[span] = d_r2

    def store(k, r, first, value):
        pieces = value.shape[0] // parts.shape[3]
        parts[k, r, first : first + pieces] = value.astype(BF16).reshape(pieces, parts.shape[3], wide)

    loads[3].wait()

    @pl.loop(0, nmp)
    def _(i):
        r = 3 - i
        store(0, r, 0, dot(act[r], d_ffn[...], 0, 0))
        exchange(0, r)

    for copy in loads[4:]:
        copy.wait()
    for copy in attn_loads(0):
        copy.start()

    @pl.loop(0, nmp)
    def _(i):
        r, slot = 3 - i, lax.rem(i, 2)
        for copy in ffn_loads(i):
            copy.wait()

        @pl.when(i + 1 < nmp)
        def _():
            for copy in ffn_loads(i + 1):
                copy.start()

        d_up = (dot(d_ffn[...], w_down[slot], 1, 1) * slope[slot].astype(F32)).astype(BF16)
        vec[r, 7:8, :hidden] = jnp.sum(d_up.astype(F32), axis=0, keepdims=True)
        store(1, r, 0, dot(h1_low[...], d_up, 0, 0))
        exchange(1, r)
        total[...] += dot(d_up, w_up[slot], 1, 1)

        @pl.loop(i - (i + 2) // 3, i + i // 3)
        def _(n):
            tick(n)

    @pl.loop(0, rows // tile)
    def _(t):
        span = pl.ds(pl.multiple_of(t * tile, tile), tile)
        d_h1 = total[span]
        normed = n1[span]
        count_up(2, d_h1)
        count_up(1, d_h1 * normed)
        d_r1 = norm_back(d_h1, normed, inv1[span, 0:1], gain1)
        count_up(0, d_r1)
        d_attn[span] = d_r1.astype(BF16)
        total[span] = d_r1

    for r in range(1, nmp):
        vec[r, 0:6] = vec[0, 0:6]

    iota_row = lax.broadcasted_iota(jnp.int32, (1, rows), 1)
    iota_col = lax.broadcasted_iota(jnp.int32, (rows, 1), 0)
    seg_row, seg_col = jnp.zeros_like(iota_row), jnp.zeros_like(iota_col)
    for i in range(nblk):
        end = jnp.int32(i * block)
        for j in range(nseg):
            end = end + extents[mp * nblk + i, j]
            seg_row = seg_row + (iota_row >= end).astype(jnp.int32)
            seg_col = seg_col + (iota_col >= end).astype(jnp.int32)
    scale = HEAD ** (-0.5)

    @pl.loop(0, nmp)
    def _(i):
        r, slot = 3 - i, lax.rem(i, 2)
        for copy in attn_loads(i):
            copy.wait()

        @pl.when(i + 1 < nmp)
        def _():
            for copy in attn_loads(i + 1):
                copy.start()

        d_mixed = dot(d_attn[...], w_out[slot], 1, 1).astype(BF16)
        for h in range(feat // HEAD):
            lanes = slice(h * HEAD, (h + 1) * HEAD)
            q = qkv[slot, 0, :, lanes] * BF16(scale)
            k = qkv[slot, 1, :, lanes]
            v = qkv[slot, 2, :, lanes]
            d_o = d_mixed[:, lanes]
            scores = jnp.where(seg_col == seg_row, dot(q, k, 1, 1), masked_score)
            expo = jnp.exp(scores - jnp.max(scores, axis=1, keepdims=True))
            probs = expo * (1.0 / jnp.sum(expo, axis=1, keepdims=True))
            d_p = dot(d_o, v, 1, 1)
            d_s = (probs * (d_p - jnp.sum(d_p * probs, axis=1, keepdims=True))).astype(BF16)
            d_proj[:, h * HEAD : (h + 1) * HEAD] = (dot(d_s, k, 1, 0) * scale).astype(BF16)
            d_proj[:, feat + h * HEAD : feat + (h + 1) * HEAD] = dot(d_s, q, 0, 0).astype(BF16)
            d_proj[:, 2 * feat + h * HEAD : 2 * feat + (h + 1) * HEAD] = dot(probs.astype(BF16), d_o, 0, 0).astype(BF16)
        small = parts.shape[3]
        store(2, r, 0, dot(mixed[slot], d_attn[...], 0, 0))
        store(2, r, feat // small, dot(d_proj[...], x[...], 0, 0))
        exchange(2, r)
        vec[r, 6:7, : 3 * feat] = jnp.sum(d_proj[...].astype(F32), axis=0, keepdims=True)
        value = total[...]
        for j in range(3):
            value = value + dot(d_proj[:, j * feat : (j + 1) * feat], w_qkv[slot, j], 1, 0)
        total[...] = value

        @pl.loop(4 + 3 * ((i + 2) // 3) + i // 2 + 2 * (i // 3), 7 + i + i // 2 + i // 3)
        def _(n):
            tick(n)

    for copy in vec_near:
        copy.start()
    low_tok[...] = total[...].astype(BF16)
    tok_near.start()
    tok_own.start()
    for copy in vec_near:
        copy.wait_recv()
    vec_b[...] = vec[2] + vec_a[1]
    vec_far.start()
    vec_s[0] = vec[0] + vec_a[0]
    tok_far.start()

    @pl.loop(12, count + LAGS[6] + extra)
    def _(i):
        @pl.when(i == count)
        def _():
            vec_far.wait()
            vec_s[0] = vec_s[0] + vec_r[0]
            vec_dp[0].start()

        for b in range(bits):
            @pl.when(i == count + 1 + b)
            def _(b=b):
                vec_dp[b].wait()
                value = vec_s[b] + vec_r[1 + b]
                if b + 1 < bits:
                    vec_s[b + 1] = value
                    vec_dp[b + 1].start()
                else:
                    vec_out[...] = value

        tick(i)

    tok_far.wait_recv()
    tok_pass.start()
    for copy in vec_near:
        copy.wait_send()
    for k in range(KINDS):
        for j in range(2):
            near_copy(k, j).wait_send()

    @pl.loop(0, count)
    def _(c):
        for copy in (far_copy, x_copy, p_copy, q_copy, gq_copy, gp_copy, gx_copy):
            copy(c).wait_send()

    tok_near.wait()
    tok_far.wait_send()
    tok_own.wait()
    tok_pass.wait()


def backward(
    d_query, extents, gain1, gain2, upstream, n1, inv1, n2, inv2, h1_low, act, slope, w_up, w_down,
    qkv, mixed, w_out, w_qkv, x, ndp, nmp, block,
):
    rows, wide = x.shape
    feat, hidden = mixed.shape[2], act.shape[2]
    count = KINDS * CHUNKS
    pieces = CHUNKS * PIECES
    small = wide // pieces
    bits = ndp.bit_length() - 1
    extra = max(bits - 3, 1)
    vmem, anywhere = pl.BlockSpec(memory_space=pltpu.VMEM), pl.BlockSpec(memory_space=pl.ANY)
    dma = pltpu.SemaphoreType.DMA
    sds = jax.ShapeDtypeStruct
    vec = (8, wide)
    low, full = (lambda *shape: pltpu.VMEM(shape, BF16)), (lambda *shape: pltpu.VMEM(shape, F32))
    two = lambda a: low(2, *a.shape[1:])
    pair = lambda *shape: [dma(shape), dma(shape)]
    scratch = [full(rows, wide), full(*n1.shape), full(*inv1.shape), full(*n2.shape), full(*inv2.shape)]
    scratch += [low(rows, wide), low(rows, wide), low(*act.shape), two(slope), two(w_up), two(w_down)]
    scratch += [two(qkv), two(mixed), two(w_out), two(w_qkv)]
    scratch += [low(rows, wide), low(rows, wide), low(rows, 3 * feat), low(rows, wide)]
    scratch += [low(KINDS, nmp, pieces, small, wide), full(nmp, *vec), low(KINDS, 2, pieces, small, wide)]
    scratch += [low(count, n, small, wide) for n in (8, 4, 2, 1)] + [low(extra, count, 1, small, wide)]
    scratch += [full(2, *vec), full(*vec), full(bits, *vec), full(bits + 1, *vec)]
    scratch += [dma((8,)), dma((2, 3)), dma((2, 4))]
    scratch += pair(2 * KINDS) + pair(count) * 4 + pair(extra, count) + pair(count) * 3
    scratch += pair(2) + pair(bits + 1) + pair(3) + [dma]
    out = pl.pallas_call(
        functools.partial(backward_kernel, ndp, nmp, block),
        out_shape=(sds((count, 2, 2, 2, small, wide), BF16), sds(vec, F32), sds((nmp, rows, wide), BF16)),
        in_specs=[vmem, pl.BlockSpec(memory_space=pltpu.SMEM), vmem, vmem] + [anywhere] * 15,
        out_specs=(vmem, vmem, anywhere),
        scratch_shapes=scratch,
        compiler_params=pltpu.CompilerParams(
            collective_id=1, has_side_effects=True, vmem_limit_bytes=67043328
        ),
        name="backward",
    )(
        d_query, extents, gain1, gain2, upstream, n1, inv1, n2, inv2, h1_low, act, slope, w_up, w_down,
        qkv, mixed, w_out, w_qkv, x,
    )
    return out[0].reshape(KINDS, wide, wide), out[1], out[2].reshape(-1, wide)


def local(
    encoder_rows,
    piece_extent_sequence,
    triple_projection_matrix,
    asker_content_shifts,
    mixing_result_matrix,
    mixing_result_offset_vector,
    mixing_normalizer_scale,
    mixing_normalizer_shift,
    widen_matrix,
    widen_shift_vector,
    narrow_matrix,
    narrow_shift_vector,
    perceptron_normalizer_scale,
    perceptron_normalizer_shift,
    document_vectors,
    sharpness_factor,
    correct_document_position,
    upstream_sensitivity,
    *,
    width,
    depth,
):
    nblock = piece_extent_sequence.shape[0]
    block = encoder_rows.shape[0] // nblock
    rows = encoder_rows.shape[0] // width
    feat = triple_projection_matrix.shape[2]
    hidden = widen_matrix.shape[1]
    wide = encoder_rows.shape[1]

    w_qkv = triple_projection_matrix.transpose(0, 2, 1)
    small = jnp.concatenate(
        [jnp.pad(asker_content_shifts, ((0, 0), (0, hidden - feat))), widen_shift_vector[None]]
    )
    (
        qkv, mixed, n1, inv1, n2, inv2, h1_low, act, slope, w_qkv, w_out, w_up, w_down, own_out, query, x,
    ) = encode(
        encoder_rows, piece_extent_sequence, w_qkv, mixing_result_matrix, widen_matrix,
        narrow_matrix, small, mixing_result_offset_vector, mixing_normalizer_scale, mixing_normalizer_shift,
        narrow_shift_vector, perceptron_normalizer_scale, perceptron_normalizer_shift, block, width,
    )
    d_query, seg_loss, sharpness_derivative, layer_out = retrieval(
        query, own_out, document_vectors, correct_document_position[None], sharpness_factor, depth, width
    )
    layer_out = layer_out.reshape(-1, wide)
    sums, vectors, grad_tokens = backward(
        d_query, piece_extent_sequence, mixing_normalizer_scale, perceptron_normalizer_scale, upstream_sensitivity, n1, inv1, n2, inv2, h1_low, act, slope,
        w_up, w_down, qkv, mixed, w_out, w_qkv, x, depth, width, block,
    )
    grad_tokens = grad_tokens.astype(F32)
    grad_qkv = sums[2, feat:].astype(F32).reshape(3, feat, wide).transpose(0, 2, 1)
    return (
        layer_out,
        seg_loss[0],
        grad_tokens,
        grad_qkv,
        jnp.stack([vectors[6, :feat], vectors[6, 2 * feat : 3 * feat]]),
        sums[2, :feat].astype(F32),
        vectors[0],
        vectors[1],
        vectors[2],
        sums[1].astype(F32),
        vectors[7, :hidden],
        sums[0].astype(F32),
        vectors[3],
        vectors[4],
        vectors[5],
        sharpness_derivative[0],
    )


def solution(mesh):
    in_specs = (
        P("dp", None),
        P("dp", None),
        P(None, None, "mp"),
        P(None, "mp"),
        P("mp", None),
        P(),
        P(),
        P(),
        P(None, "mp"),
        P("mp"),
        P("mp", None),
        P(),
        P(),
        P(),
        P(("dp", "mp"), None),
        P(),
        P(),
        P("dp", None),
    )
    out_specs = (
        P("dp", None),
        P(),
        P("dp", None),
        P(None, None, "mp"),
        P(None, "mp"),
        P("mp", None),
        P(),
        P(),
        P(),
        P(None, "mp"),
        P("mp"),
        P("mp", None),
        P(),
        P(),
        P(),
        P(),
    )
    width = mesh.shape["mp"]

    def step(*args):
        return local(*args, width=width, depth=mesh.shape["dp"])

    return jax.shard_map(step, mesh=mesh, in_specs=in_specs, out_specs=out_specs, check_vma=False)
```

```python
import functools
import math

import jax
import jax.numpy as jnp
from jax import lax
from jax.experimental import pallas as pl
from jax.experimental.pallas import tpu as pltpu
from jax.sharding import PartitionSpec as P

HEAD = 64
F32 = jnp.float32
BF16 = jnp.bfloat16
MESH = pl.DeviceIdType.MESH
norm_epsilon = 1e-05
masked_score = -1e30


def dot(a, b, ca, cb):
    return lax.dot_general(a, b, (((ca,), (cb,)), ((), ())), preferred_element_type=F32)


def norm_stats(resid):
    centre = jnp.mean(resid, axis=-1, keepdims=True)
    centred = resid - centre
    spread = jnp.mean(centred * centred, axis=-1, keepdims=True)
    inv = lax.rsqrt(spread + norm_epsilon)
    return centred * inv, inv


def norm_back(d_out, normed, inv, gain):
    e = d_out * gain
    return inv * (
        e - jnp.mean(e, axis=-1, keepdims=True) - normed * jnp.mean(e * normed, axis=-1, keepdims=True)
    )


def flip(index, step):
    return index + step * (1 - 2 * lax.rem(index // step, 2))


def retrieval_kernel(
    ndp, nmp, query_ref, own_ref, docs_hbm, gold_ref, sharp_ref, dq_ref, loss_ref, ds_ref, layer,
    queries, docs, low, stats, columns, part_u, part_g, send, got, doc_sem, q_send, q_recv, s_send, s_recv, d_send, d_recv,
    l_s, l_r, own_sem,
):
    n = ndp * nmp
    own = query_ref.shape[0]
    nseg = gold_ref.shape[1]
    tile = 256 if nseg <= 256 else 128
    dp, mp = lax.axis_index("dp"), lax.axis_index("mp")
    me = dp * nmp + mp
    load = pltpu.make_async_copy(docs_hbm, docs, doc_sem)
    load.start()
    barrier = pltpu.get_barrier_semaphore()

    def device(step):
        other = lax.rem(me + step, n)
        return other, (other // nmp, lax.rem(other, nmp))

    @pl.loop(1, n)
    def _(step):
        _, where = device(step)
        pl.semaphore_signal(barrier, inc=1, device_id=where, device_id_type=MESH)

    pl.semaphore_wait(barrier, n - 1)

    def push(source, target, send_sems, recv_sems):
        @pl.loop(1, n)
        def _(step):
            other, where = device(step)
            pltpu.make_async_remote_copy(
                source(other), target, send_sems.at[step], recv_sems.at[step], device_id=where, device_id_type=MESH
            ).start()

    def drain(source, target, send_sems, recv_sems):
        @pl.loop(1, n)
        def _(step):
            other, where = device(step)
            copy = pltpu.make_async_remote_copy(
                source(other), target, send_sems.at[step], recv_sems.at[step], device_id=where, device_id_type=MESH
            )
            copy.wait()

    push(lambda other: query_ref, queries.at[me], q_send, q_recv)
    queries[me] = query_ref[...]
    drain(lambda other: query_ref, queries.at[me], q_send, q_recv)
    near, far, across = (dp, flip(mp, 1)), (dp, flip(mp, 2)), flip(mp, 2)

    def spread(source, target, i, where):
        return pltpu.make_async_remote_copy(
            source, target, l_s.at[i], l_r.at[i], device_id=where, device_id_type=MESH
        )

    to_near = spread(own_ref, layer.at[mp], 0, near)
    to_far, to_pass, first = [], [], 0
    for i, part in enumerate((7, 6, 3)):
        strip = pl.ds(first, own_ref.shape[0] * part // 16)
        first += own_ref.shape[0] * part // 16
        passed = layer.at[across, strip]
        to_far.append(spread(own_ref.at[strip], layer.at[mp, strip], 1 + i, far))
        to_pass.append(spread(passed, passed, 4 + i, near))
    keep = pltpu.make_async_copy(own_ref, layer.at[mp], own_sem)
    to_far[0].start()
    to_near.start()
    keep.start()
    load.wait()

    sharp = sharp_ref[0]
    offset = me * docs.shape[0]
    ids = lax.broadcasted_iota(jnp.int32, (tile, docs.shape[0]), 1).astype(F32)
    columns[...] = jnp.broadcast_to((gold_ref[...] - offset).astype(F32), (128, nseg)).T
    lane = lax.broadcasted_iota(jnp.int32, (tile, 128), 1)
    per = tile // own

    @pl.loop(0, nseg // tile)
    def _(i):
        span = pl.ds(pl.multiple_of(i * tile, tile), tile)
        q = queries[pl.ds(i * per, per)].reshape(tile, queries.shape[2])
        logit = lax.dot_general(q, docs[...], (((1,), (1,)), ((), ())), preferred_element_type=F32) / sharp
        match = ids == columns[span, 0:1]
        top = jnp.max(logit, axis=1, keepdims=True)
        expo = jnp.exp(logit - top)
        total = jnp.sum(expo, axis=1, keepdims=True)
        tilt = jnp.sum(expo * logit, axis=1, keepdims=True)
        gold = jnp.sum(jnp.where(match, logit, 0.0), axis=1, keepdims=True)
        packed = jnp.where(lane == 0, top, jnp.where(lane == 1, total, jnp.where(lane == 2, tilt, gold)))
        stats[me, :, span] = packed.T[:4]
        low[span, :] = jnp.where(match, 0.0, expo).astype(BF16)

    push(lambda other: stats.at[me], stats.at[me], s_send, s_recv)
    to_far[1].start()

    @pl.loop(0, nseg // tile)
    def _(i):
        span = pl.ds(pl.multiple_of(i * tile, tile), tile)
        part_u[span, :] = jnp.dot(low[span, :], docs[...], preferred_element_type=F32)
        match = ids == columns[span, 0:1]
        part_g[span, :] = jnp.dot(
            match.astype(F32).astype(BF16), docs[...], preferred_element_type=F32
        ).astype(BF16)

    drain(lambda other: stats.at[me], stats.at[me], s_send, s_recv)
    to_far[0].wait_recv()
    to_pass[0].start()

    tops = stats[:, 0, :]
    top = jnp.max(tops, axis=0, keepdims=True)
    share = jnp.exp(tops - top)
    total = jnp.sum(stats[:, 1, :] * share, axis=0, keepdims=True)
    tilt = jnp.sum(stats[:, 2, :] * share, axis=0, keepdims=True)
    gold = jnp.sum(stats[:, 3, :], axis=0, keepdims=True)
    lse = top + jnp.log(total)
    loss_ref[...] = lse - gold
    ds_ref[...] = -jnp.sum(tilt / total - gold, axis=1, keepdims=True) / sharp
    scale = jnp.exp(stats[me, 0:1, :] - lse) / sharp
    gold_scale = (jnp.exp(gold - lse) - 1.0) / sharp
    row = lax.broadcasted_iota(jnp.int32, (128, nseg), 0)
    columns[...] = jnp.where(row == 0, scale, gold_scale).T

    @pl.loop(0, nseg // tile)
    def _(i):
        span = pl.ds(pl.multiple_of(i * tile, tile), tile)
        value = part_u[span, :] * columns[span, 0:1] + part_g[span, :].astype(F32) * columns[span, 1:2]
        send[pl.ds(i * per, per)] = value.astype(BF16).reshape(per, own, value.shape[1])

    push(lambda other: send.at[other], got.at[me], d_send, d_recv)
    to_far[2].start()
    to_far[1].wait_recv()
    to_pass[1].start()
    got[me] = send[me]
    drain(lambda other: send.at[other], got.at[me], d_send, d_recv)
    dq_ref[...] = jnp.sum(got[...].astype(F32), axis=0)
    to_far[2].wait_recv()
    to_pass[2].start()
    to_near.wait()
    for copy in to_far:
        copy.wait_send()
    for copy in to_pass:
        copy.wait()
    keep.wait()


def retrieval(query, own_out, docs, gold, sharp, ndp, nmp):
    n = ndp * nmp
    own, width = query.shape
    nseg = gold.shape[1]
    vmem = pl.BlockSpec(memory_space=pltpu.VMEM)
    return pl.pallas_call(
        functools.partial(retrieval_kernel, ndp, nmp),
        out_shape=(
            jax.ShapeDtypeStruct((own, width), F32),
            jax.ShapeDtypeStruct((1, nseg), F32),
            jax.ShapeDtypeStruct((1, 1), F32),
            jax.ShapeDtypeStruct((nmp,) + own_out.shape, BF16),
        ),
        in_specs=[vmem, vmem, pl.BlockSpec(memory_space=pl.ANY), vmem, pl.BlockSpec(memory_space=pltpu.SMEM)],
        out_specs=(vmem, vmem, vmem, pl.BlockSpec(memory_space=pl.ANY)),
        scratch_shapes=[
            pltpu.VMEM((n, own, width), BF16),
            pltpu.VMEM(docs.shape, BF16),
            pltpu.VMEM((nseg, docs.shape[0]), BF16),
            pltpu.VMEM((n, 4, nseg), F32),
            pltpu.VMEM((nseg, 128), F32),
            pltpu.VMEM((nseg, width), F32),
            pltpu.VMEM((nseg, width), BF16),
            pltpu.VMEM((n, own, width), BF16),
            pltpu.VMEM((n, own, width), BF16),
            pltpu.SemaphoreType.DMA,
        ]
        + [pltpu.SemaphoreType.DMA((n,))] * 6
        + [pltpu.SemaphoreType.DMA((7,))] * 2
        + [pltpu.SemaphoreType.DMA],
        compiler_params=pltpu.CompilerParams(
            collective_id=0, has_side_effects=True, vmem_limit_bytes=60 * 2**20
        ),
        name="retrieval",
    )(query, own_out, docs, gold, sharp)


def gelu_with_slope(u):
    z = jnp.abs(u) * (0.5**0.5)
    t = 1.0 / (1.0 + 0.5 * z)
    poly = 0.17087277
    for c in (
        -0.82215223, 1.48851587, -1.13520398, 0.27886807, -0.18628806, 0.09678418, 0.37409196, 1.00002368,
    ):
        poly = poly * t + c
    square = z * z
    tail = 0.5 * t * jnp.exp(poly * t - 1.26551223 - square)
    cdf = jnp.where(u < 0, tail, 1.0 - tail)
    return u * cdf, cdf + u * (jnp.exp(-square) * ((2 * math.pi) ** -0.5))


def encode_kernel(nmp, block, *refs):
    (
        rows_hbm, extents, w_qkv, w_out, w_up, w_down, small_ref, *vectors,
    ) = refs[:13]
    out_bias, gain1, shift1, down_bias, gain2, shift2 = (v[...][None] for v in vectors)
    (
        qkv_o, mixed_o, n1_o, inv1_o, n2_o, inv2_o, low_o, act_o, slope_o, w_qkv_o, w_out_o, w_up_o, w_down_o,
        own_o, query_o, x_o,
    ) = refs[13:29]
    (
        x, qkv, mixed, n1, n2, h1_low, act, slope, all_qkv, all_out, all_up, all_down, small, total,
        fill_sem, save_sem, n_s, n_r, m_s, m_r, y_s, y_r, f_s, f_r, g_s, g_r, h_s, h_r, sm_s, sm_r,
    ) = refs[29:]
    dp, mp = lax.axis_index("dp"), lax.axis_index("mp")
    near, far, side = (dp, flip(mp, 1)), (dp, flip(mp, 2)), (flip(dp, 1), mp)
    b = lax.rem(dp, 2)
    rows = x.shape[0]
    feat = w_out.shape[0] * w_out.shape[1]
    scale = HEAD ** (-0.5)

    own_rows = rows_hbm.at[pl.ds(pl.multiple_of(mp * rows, rows), rows)]
    fills = [
        pltpu.make_async_copy(source, target, fill_sem.at[i])
        for i, (source, target) in enumerate(
            [
                (own_rows, x), (w_qkv, all_qkv.at[0]), (w_out, all_out.at[0]), (w_up, all_up.at[0]),
                (w_down, all_down.at[0]),
            ]
        )
    ]
    for copy in fills:
        copy.start()
    barrier = pltpu.get_barrier_semaphore()
    for where in (near, far, side):
        pl.semaphore_signal(barrier, inc=1, device_id=where, device_id_type=MESH)
    pl.semaphore_wait(barrier, 3)

    def remote(source, target, send, recv, where):
        return pltpu.make_async_remote_copy(source, target, send, recv, device_id=where, device_id_type=MESH)

    pieces = [(w_qkv.at[k], all_qkv, k) for k in range(3)] + [(w_out, all_out, None)]
    pieces += [(w_up.at[s], all_up, s) for s in range(w_up.shape[0])]
    pieces += [(w_down.at[s], all_down, s) for s in range(w_down.shape[0])]
    count = len(pieces)

    def slot(i, r):
        _, held, s = pieces[i]
        return held.at[r] if s is None else held.at[r, s]

    near_own = [remote(pieces[i][0], slot(i, 1), n_s.at[i], n_r.at[i], near) for i in range(count)]
    far_own = [remote(pieces[i][0].at[b], slot(i, 2).at[b], y_s.at[i], y_r.at[i], far) for i in range(count)]
    pass_side = [remote(slot(i, 2).at[b], slot(i, 2).at[b], f_s.at[i], f_r.at[i], side) for i in range(count)]
    pass_near = [remote(slot(i, 2).at[b], slot(i, 3).at[b], g_s.at[i], g_r.at[i], near) for i in range(count)]
    pass_other = [
        remote(slot(i, 2).at[1 - b], slot(i, 3).at[1 - b], h_s.at[i], h_r.at[i], near) for i in range(count)
    ]
    small_near = remote(small_ref, small.at[1], sm_s.at[0], sm_r.at[0], near)
    small_far = remote(small_ref, small.at[2], sm_s.at[1], sm_r.at[1], far)
    small_pass = remote(small.at[2], small.at[3], sm_s.at[2], sm_r.at[2], near)

    small_near.start()
    small_far.start()
    for i in range(count):
        far_own[i].start()
        near_own[i].start()
    small[0] = small_ref[...]
    by_quarter = [
        (qkv, qkv_o), (mixed, mixed_o), (act, act_o), (slope, slope_o), (all_qkv, w_qkv_o), (all_out, w_out_o),
        (all_up, w_up_o), (all_down, w_down_o),
    ]
    at_once = [(x, x_o), (n1, n1_o), (h1_low, low_o), (n2, n2_o)]

    def save(i, r):
        source, target = by_quarter[i]
        return pltpu.make_async_copy(source.at[r], target.at[r], save_sem.at[4 * i + r])

    def save_whole(i):
        source, target = at_once[i]
        return pltpu.make_async_copy(source, target, save_sem.at[4 * len(by_quarter) + i])

    def relay(i):
        far_own[i].wait_recv()
        pass_side[i].start()
        pass_near[i].start()

    def relay_other(i):
        pass_side[i].wait_recv()
        pass_other[i].start()

    def last_arrived(i):
        pass_near[i].wait_recv()
        pass_other[i].wait_recv()

    iota_row = lax.broadcasted_iota(jnp.int32, (1, rows), 1)
    iota_col = lax.broadcasted_iota(jnp.int32, (rows, 1), 0)
    nblk = rows // block
    nseg = extents.shape[1]
    seg_row, seg_col = jnp.zeros_like(iota_row), jnp.zeros_like(iota_col)
    starts = []
    for i in range(nblk):
        end = jnp.int32(i * block)
        for j in range(nseg):
            starts.append(end)
            end = end + extents[mp * nblk + i, j]
            seg_row = seg_row + (iota_row >= end).astype(jnp.int32)
            seg_col = seg_col + (iota_col >= end).astype(jnp.int32)
    wide = x.shape[1]
    ups, downs = range(4, 4 + w_up.shape[0]), range(4 + w_up.shape[0], count)

    def head(r, h):
        lanes = slice(h * HEAD, (h + 1) * HEAD)
        q = qkv[r, 0, :, lanes] * BF16(scale)
        scores = dot(q, qkv[r, 1, :, lanes], 1, 1)
        scores = jnp.where(seg_col == seg_row, scores, masked_score)
        expo = jnp.exp(scores - jnp.max(scores, axis=1, keepdims=True))
        probs = (expo * (1.0 / jnp.sum(expo, axis=1, keepdims=True))).astype(BF16)
        mixed[r, :, lanes] = jnp.dot(probs, qkv[r, 2, :, lanes], preferred_element_type=F32).astype(BF16)

    def both(i):
        relay(i)
        relay_other(i - 1)

    def on(r, at, *steps):
        @pl.when(r == at)
        def _():
            for step in steps:
                step()

    near_in = lambda group: [near_own[i].wait_recv for i in group]
    last_in = lambda group: [functools.partial(last_arrived, i) for i in group]
    do = functools.partial
    fills[0].wait()
    fills[1].wait()
    save_whole(0).start()

    @pl.loop(0, nmp)
    def _(r):
        on(r, 1, small_near.wait_recv, *near_in(range(3)))
        on(
            r, 2, small_far.wait_recv, small_pass.start, do(relay, 0), do(relay, 1), do(relay_other, 0), do(relay, 2),
            do(relay_other, 1), do(relay, 3), do(relay_other, 2),
        )
        on(r, 3, small_pass.wait_recv, *last_in(range(3)))
        for k in range(3):
            value = dot(x[...], all_qkv[r, k].reshape(feat, wide), 1, 1)
            if k == 0:
                value = value + small[r, 0:1, :feat]
            if k == 2:
                value = value + small[r, 1:2, :feat]
            qkv[r, k] = value.astype(BF16)
        save(0, r).start()
        save(4, r).start()
        head(r, 0)
        on(r, 2, do(relay_other, 3))
        on(r, 3, do(both, 5))
        head(r, 1)
        on(r, 2, do(relay, 4))
        for h in range(2, feat // HEAD):
            head(r, h)
        save(1, r).start()

    fills[2].wait()
    near_own[3].wait_recv()
    last_arrived(3)
    total[...] = x[...].astype(F32) + out_bias

    @pl.loop(0, nmp)
    def _(r):
        total[...] += jnp.dot(mixed[r], all_out[r].reshape(feat, wide), preferred_element_type=F32)
        save(5, r).start()

    tile = 128

    @pl.loop(0, rows // tile)
    def _(t):
        span = pl.ds(pl.multiple_of(t * tile, tile), tile)
        normed, inv = norm_stats(total[span])
        n1[span] = normed
        inv1_o[span] = jnp.broadcast_to(inv, (tile, inv1_o.shape[1]))
        h1 = normed * gain1 + shift1
        total[span] = h1 + down_bias
        h1_low[span] = h1.astype(BF16)

    save_whole(1).start()
    save_whole(2).start()
    both(6)
    fills[3].wait()
    fills[4].wait()

    @pl.loop(0, nmp)
    def _(r):
        on(r, 1, *near_in(ups))
        on(r, 3, *last_in(ups))
        upper = jnp.dot(h1_low[...], all_up[r].reshape(wide, -1), preferred_element_type=F32) + small[r, 2:3, :]
        value, gradient = gelu_with_slope(upper)
        act[r] = value.astype(BF16)
        slope[r] = gradient.astype(BF16)
        for i in (2, 3, 6):
            save(i, r).start()
        on(r, 0, do(both, 7))
        on(r, 1, do(both, 8), *near_in(downs))
        on(r, 2, do(both, 9), do(relay_other, 9))
        on(r, 3, *last_in(downs))
        total[...] += jnp.dot(act[r], all_down[r].reshape(-1, wide), preferred_element_type=F32)
        save(7, r).start()

    @pl.loop(0, rows // tile)
    def _(t):
        span = pl.ds(pl.multiple_of(t * tile, tile), tile)
        normed, inv = norm_stats(total[span])
        n2[span] = normed
        inv2_o[span] = jnp.broadcast_to(inv, (tile, inv2_o.shape[1]))
        own_o[span] = (normed * gain2 + shift2).astype(BF16)

    save_whole(3).start()
    line = lax.broadcasted_iota(jnp.int32, (len(starts), rows), 0)
    first = jnp.zeros((len(starts), rows), jnp.int32)
    for j, start in enumerate(starts):
        first = jnp.where(line == j, start, first)
    pick = (lax.broadcasted_iota(jnp.int32, first.shape, 1) == first).astype(F32).astype(BF16)
    query_o[...] = jnp.dot(pick, own_o[...], preferred_element_type=F32).astype(BF16)
    for i in range(len(at_once)):
        save_whole(i).wait()

    @pl.loop(0, nmp)
    def _(r):
        for i in range(len(by_quarter)):
            save(i, r).wait()

    for copy in near_own + far_own + pass_side + pass_near + pass_other + [small_near, small_far, small_pass]:
        copy.wait_send()


STRIPS = 3


def encode(
    encoder_rows, extents, w_qkv, w_out, w_up, w_down, small, out_bias, gain1, shift1, down_bias, gain2, shift2,
    block, nmp,
):
    rows = encoder_rows.shape[0] // nmp
    wide = encoder_rows.shape[1]
    feat, hidden = w_qkv.shape[1], w_up.shape[1]
    nseg = extents.shape[0] * extents.shape[1] // nmp
    cut_qkv = w_qkv.reshape(3, 2, feat // 2, wide)
    cut_out = w_out.reshape(2, feat // 2, wide)
    cut_up = w_up.reshape(STRIPS, 2, wide // (2 * STRIPS), hidden)
    cut_down = w_down.reshape(STRIPS, 2, hidden // (2 * STRIPS), wide)
    vmem, anywhere = pl.BlockSpec(memory_space=pltpu.VMEM), pl.BlockSpec(memory_space=pl.ANY)
    sds = jax.ShapeDtypeStruct
    dma = pltpu.SemaphoreType.DMA
    every = lambda a: (nmp,) + a.shape
    held = [
        sds((nmp, 3, rows, feat), BF16),
        sds((nmp, rows, feat), BF16),
        sds((rows, wide), F32),
        sds((rows, 128), F32),
        sds((rows, wide), F32),
        sds((rows, 128), F32),
        sds((rows, wide), BF16),
        sds((nmp, rows, hidden), BF16),
        sds((nmp, rows, hidden), BF16),
        sds(every(cut_qkv), BF16),
        sds(every(cut_out), BF16),
        sds(every(cut_up), BF16),
        sds(every(cut_down), BF16),
        sds((rows, wide), BF16),
        sds((nseg, wide), BF16),
        sds((rows, wide), BF16),
    ]
    count = 4 + 2 * STRIPS
    scratch = [
        pltpu.VMEM((rows, wide), BF16),
        pltpu.VMEM(held[0].shape, BF16),
        pltpu.VMEM(held[1].shape, BF16),
        pltpu.VMEM((rows, wide), F32),
        pltpu.VMEM((rows, wide), F32),
        pltpu.VMEM((rows, wide), BF16),
        pltpu.VMEM(held[7].shape, BF16),
        pltpu.VMEM(held[8].shape, BF16),
    ]
    scratch += [pltpu.VMEM(h.shape, BF16) for h in held[9:13]]
    scratch += [pltpu.VMEM(every(small), F32), pltpu.VMEM((rows, wide), F32), dma((5,)), dma((36,))]
    scratch += [dma((count,))] * 12 + [dma((3,))] * 2
    outs = pl.pallas_call(
        functools.partial(encode_kernel, nmp, block),
        out_shape=tuple(held),
        in_specs=[anywhere, pl.BlockSpec(memory_space=pltpu.SMEM)] + [anywhere] * 4 + [vmem] * 7,
        out_specs=tuple(vmem if i in (3, 5, 13, 14) else anywhere for i in range(len(held))),
        scratch_shapes=scratch,
        compiler_params=pltpu.CompilerParams(collective_id=2, has_side_effects=True, vmem_limit_bytes=62 * 2**20),
        name="encode",
    )(encoder_rows, extents, cut_qkv, cut_out, cut_up, cut_down, small, out_bias, gain1, shift1, down_bias, gain2, shift2)
    outs = list(outs)
    outs[9] = outs[9].reshape(nmp, 3, feat, wide)
    outs[10] = outs[10].reshape(nmp, feat, wide)
    outs[11] = outs[11].reshape(nmp, wide, hidden)
    outs[12] = outs[12].reshape(nmp, hidden, wide)
    return outs


PIECES = 8
CHUNKS = 6
KINDS = 3
PACE = 2
LAGS = (0, 4, 7, 10, 13, 16, 20)


def backward_kernel(ndp, nmp, block, *refs):
    (
        d_query, extents, gain1, gain2, upstream_h, n1_h, inv1_h, n2_h, inv2_h, low_h, act_h, slope_h, up_h, down_h,
        qkv_h, mixed_h, w_out_h, w_qkv_h, x_h,
    ) = refs[:19]
    out, vec_out, tok = refs[19:22]
    (
        total, n1, inv1, n2, inv2, h1_low, x, act, slope, w_up, w_down, qkv, mixed, w_out, w_qkv,
        d_ffn, d_attn, d_proj, low_tok, parts, vec, near, got_y, got_x, got_1, got_2, got_e,
        vec_a, vec_b, vec_s, vec_r,
        load_sem, ffn_sem, attn_sem, a_s, a_r, y_s, y_r, x_s, x_r, p_s, p_r, q_s, q_r, e_s, e_r,
        gq_s, gq_r, gp_s, gp_r, gx_s, gx_r, va_s, va_r, v_s, v_r, t_s, t_r, own_sem,
    ) = refs[22:]
    count = KINDS * CHUNKS
    bits = ndp.bit_length() - 1
    extra = bits - 3
    rows, wide = total.shape
    feat = mixed.shape[2]
    hidden = act.shape[2]
    dp, mp = lax.axis_index("dp"), lax.axis_index("mp")
    near_dev, far_dev = (dp, flip(mp, 1)), (dp, flip(mp, 2))
    dp_dev = [(flip(dp, 1 << b), mp) for b in range(bits)]
    b0, b1, b2 = (lax.rem(dp // (1 << b), 2) for b in range(3))
    ident = b0 * 4 + b1 * 2 + b2
    gain1, gain2 = gain1[...][None], gain2[...][None]

    own_rows = upstream_h.at[pl.ds(pl.multiple_of(mp * rows, rows), rows)]
    loads = [
        pltpu.make_async_copy(source, target, load_sem.at[i])
        for i, (source, target) in enumerate(
            [
                (own_rows, total), (n2_h, n2), (inv2_h, inv2), (act_h, act), (low_h, h1_low), (n1_h, n1),
                (inv1_h, inv1), (x_h, x),
            ]
        )
    ]

    def ffn_loads(i):
        r, slot = 3 - i, lax.rem(i, 2)
        return [
            pltpu.make_async_copy(source.at[r], target.at[slot], ffn_sem.at[slot, j])
            for j, (source, target) in enumerate([(down_h, w_down), (slope_h, slope), (up_h, w_up)])
        ]

    def attn_loads(i):
        r, slot = 3 - i, lax.rem(i, 2)
        return [
            pltpu.make_async_copy(source.at[r], target.at[slot], attn_sem.at[slot, j])
            for j, (source, target) in enumerate([(w_out_h, w_out), (qkv_h, qkv), (mixed_h, mixed), (w_qkv_h, w_qkv)])
        ]

    for copy in loads + ffn_loads(0):
        copy.start()
    barrier = pltpu.get_barrier_semaphore()
    for where in [near_dev, far_dev] + dp_dev:
        pl.semaphore_signal(barrier, inc=1, device_id=where, device_id_type=MESH)
    pl.semaphore_wait(barrier, 2 + bits)

    def remote(source, target, send, recv, where):
        return pltpu.make_async_remote_copy(source, target, send, recv, device_id=where, device_id_type=MESH)

    def part(c, r, first=0, many=PIECES):
        k = c // CHUNKS
        return parts.at[k, r, pl.ds((c - k * CHUNKS) * PIECES + first, many)]

    def near_copy(k, j):
        return remote(parts.at[k, 2 * j + 1], near.at[k, j], a_s.at[2 * k + j], a_r.at[2 * k + j], near_dev)

    def far_copy(c):
        return remote(part(c, 2), got_y.at[c], y_s.at[c], y_r.at[c], far_dev)

    def x_copy(c):
        return remote(part(c, 0, (1 - b0) * 4, 4), got_x.at[c], x_s.at[c], x_r.at[c], dp_dev[0])

    def p_copy(c):
        return remote(part(c, 0, b0 * 4 + (1 - b1) * 2, 2), got_1.at[c], p_s.at[c], p_r.at[c], dp_dev[1])

    def q_copy(c):
        return remote(part(c, 0, ident + 1 - 2 * b2, 1), got_2.at[c], q_s.at[c], q_r.at[c], dp_dev[2])

    def e_copy(c, e):
        return remote(part(c, 0, ident, 1), got_e.at[e, c], e_s.at[e, c], e_r.at[e, c], dp_dev[3 + e])

    def gq_copy(c):
        held = out.at[c, b0, b1, b2]
        return remote(held, held, gq_s.at[c], gq_r.at[c], dp_dev[2])

    def gp_copy(c):
        held = out.at[c, b0, b1]
        return remote(held, held, gp_s.at[c], gp_r.at[c], dp_dev[1])

    def gx_copy(c):
        held = out.at[c, b0]
        return remote(held, held, gx_s.at[c], gx_r.at[c], dp_dev[0])

    vec_near = [remote(vec.at[2 * j + 1], vec_a.at[j], va_s.at[j], va_r.at[j], near_dev) for j in range(2)]
    vec_far = remote(vec_b, vec_r.at[0], v_s.at[0], v_r.at[0], far_dev)
    vec_dp = [remote(vec_s.at[b], vec_r.at[1 + b], v_s.at[1 + b], v_r.at[1 + b], dp_dev[b]) for b in range(bits)]
    across = flip(mp, 2)
    tok_near = remote(low_tok, tok.at[mp], t_s.at[0], t_r.at[0], near_dev)
    tok_far = remote(low_tok, tok.at[mp], t_s.at[1], t_r.at[1], far_dev)
    tok_pass = remote(tok.at[across], tok.at[across], t_s.at[2], t_r.at[2], near_dev)
    tok_own = pltpu.make_async_copy(low_tok, tok.at[mp], own_sem)

    def add(a, b):
        return (a.astype(F32) + b.astype(F32)).astype(BF16)

    def exchange(k, r):
        j = r // 2

        @pl.when(lax.rem(r, 2) == 1)
        def _():
            near_copy(k, j).start()

        @pl.when(lax.rem(r, 2) == 0)
        def _():
            near_copy(k, j).wait_recv()

            @pl.loop(0, CHUNKS)
            def _(i):
                span = pl.ds(i * PIECES, PIECES)
                parts[k, r, span] = add(parts[k, r, span], near[k, j, span])

                @pl.when(j == 1)
                def _():
                    far_copy(k * CHUNKS + i).start()

    def tick(i):
        def at(lag, do):
            since = i - lag

            @pl.when((since >= 0) & (since < PACE * count) & (lax.rem(since, PACE) == 0))
            def _():
                do(since // PACE)

        def update(c, first, many, got):
            target = part(c, 0, first, many)
            target[...] = add(target[...], got[c])

        @functools.partial(at, LAGS[6] + PACE * extra)
        def _(c):
            gx_copy(c).wait_recv()

        @functools.partial(at, LAGS[5] + PACE * extra)
        def _(c):
            gp_copy(c).wait_recv()
            gx_copy(c).start()

        @functools.partial(at, LAGS[4] + PACE * extra)
        def _(c):
            gq_copy(c).wait_recv()
            gp_copy(c).start()

        for e in reversed(range(extra)):
            @functools.partial(at, LAGS[3] + PACE * (1 + e))
            def _(c, e=e):
                e_copy(c, e).wait()
                update(c, ident, 1, got_e.at[e])
                if e + 1 < extra:
                    e_copy(c, e + 1).start()
                else:
                    out[c, b0, b1, b2] = part(c, 0, ident, 1)[0]
                    gq_copy(c).start()

        @functools.partial(at, LAGS[3])
        def _(c):
            q_copy(c).wait_recv()
            if extra:
                update(c, ident, 1, got_2)
                e_copy(c, 0).start()
            else:
                out[c, b0, b1, b2] = add(part(c, 0, ident, 1)[0], got_2[c, 0])
                gq_copy(c).start()

        @functools.partial(at, LAGS[2])
        def _(c):
            p_copy(c).wait_recv()
            update(c, b0 * 4 + b1 * 2, 2, got_1)
            q_copy(c).start()

        @functools.partial(at, LAGS[1])
        def _(c):
            x_copy(c).wait_recv()
            update(c, b0 * 4, 4, got_x)
            p_copy(c).start()

        @functools.partial(at, 0)
        def _(c):
            far_copy(c).wait_recv()
            update(c, 0, PIECES, got_y)
            x_copy(c).start()

    tile = 128
    nblk = rows // block
    nseg = extents.shape[1]
    vec[...] = jnp.zeros_like(vec)
    for copy in loads[:3]:
        copy.wait()

    def count_up(row, value):
        vec[0, row : row + 1] += jnp.sum(value, axis=0, keepdims=True)

    @pl.loop(0, rows // tile)
    def _(t):
        span = pl.ds(pl.multiple_of(t * tile, tile), tile)
        line = lax.broadcasted_iota(jnp.int32, (tile, 1), 0) + t * tile
        d_h2 = total[span]
        for i in range(nblk):
            start = jnp.int32(i * block)
            for j in range(nseg):
                d_h2 = d_h2 + jnp.where(line == start, d_query[i * nseg + j, :][None], 0.0)
                start = start + extents[mp * nblk + i, j]
        normed = n2[span]
        count_up(5, d_h2)
        count_up(4, d_h2 * normed)
        d_r2 = norm_back(d_h2, normed, inv2[span, 0:1], gain2)
        count_up(3, d_r2)
        d_ffn[span] = d_r2.astype(BF16)
        total[span] = d_r2

    def store(k, r, first, value):
        pieces = value.shape[0] // parts.shape[3]
        parts[k, r, first : first + pieces] = value.astype(BF16).reshape(pieces, parts.shape[3], wide)

    loads[3].wait()

    @pl.loop(0, nmp)
    def _(i):
        r = 3 - i
        store(0, r, 0, dot(act[r], d_ffn[...], 0, 0))
        exchange(0, r)

    for copy in loads[4:]:
        copy.wait()
    for copy in attn_loads(0):
        copy.start()

    @pl.loop(0, nmp)
    def _(i):
        r, slot = 3 - i, lax.rem(i, 2)
        for copy in ffn_loads(i):
            copy.wait()

        @pl.when(i + 1 < nmp)
        def _():
            for copy in ffn_loads(i + 1):
                copy.start()

        d_up = (dot(d_ffn[...], w_down[slot], 1, 1) * slope[slot].astype(F32)).astype(BF16)
        vec[r, 7:8, :hidden] = jnp.sum(d_up.astype(F32), axis=0, keepdims=True)
        store(1, r, 0, dot(h1_low[...], d_up, 0, 0))
        exchange(1, r)
        total[...] += dot(d_up, w_up[slot], 1, 1)

        @pl.loop(PACE * (i - (i + 2) // 3), PACE * (i + i // 3))
        def _(n):
            tick(n)

    @pl.loop(0, rows // tile)
    def _(t):
        span = pl.ds(pl.multiple_of(t * tile, tile), tile)
        d_h1 = total[span]
        normed = n1[span]
        count_up(2, d_h1)
        count_up(1, d_h1 * normed)
        d_r1 = norm_back(d_h1, normed, inv1[span, 0:1], gain1)
        count_up(0, d_r1)
        d_attn[span] = d_r1.astype(BF16)
        total[span] = d_r1

    for r in range(1, nmp):
        vec[r, 0:6] = vec[0, 0:6]

    iota_row = lax.broadcasted_iota(jnp.int32, (1, rows), 1)
    iota_col = lax.broadcasted_iota(jnp.int32, (rows, 1), 0)
    seg_row, seg_col = jnp.zeros_like(iota_row), jnp.zeros_like(iota_col)
    for i in range(nblk):
        end = jnp.int32(i * block)
        for j in range(nseg):
            end = end + extents[mp * nblk + i, j]
            seg_row = seg_row + (iota_row >= end).astype(jnp.int32)
            seg_col = seg_col + (iota_col >= end).astype(jnp.int32)
    scale = HEAD ** (-0.5)

    @pl.loop(0, nmp)
    def _(i):
        r, slot = 3 - i, lax.rem(i, 2)
        for copy in attn_loads(i):
            copy.wait()

        @pl.when(i + 1 < nmp)
        def _():
            for copy in attn_loads(i + 1):
                copy.start()

        d_mixed = dot(d_attn[...], w_out[slot], 1, 1).astype(BF16)
        for h in range(feat // HEAD):
            lanes = slice(h * HEAD, (h + 1) * HEAD)
            q = qkv[slot, 0, :, lanes] * BF16(scale)
            k = qkv[slot, 1, :, lanes]
            v = qkv[slot, 2, :, lanes]
            d_o = d_mixed[:, lanes]
            scores = jnp.where(seg_col == seg_row, dot(q, k, 1, 1), masked_score)
            expo = jnp.exp(scores - jnp.max(scores, axis=1, keepdims=True))
            probs = expo * (1.0 / jnp.sum(expo, axis=1, keepdims=True))
            d_p = dot(d_o, v, 1, 1)
            d_s = (probs * (d_p - jnp.sum(d_p * probs, axis=1, keepdims=True))).astype(BF16)
            d_proj[:, h * HEAD : (h + 1) * HEAD] = (dot(d_s, k, 1, 0) * scale).astype(BF16)
            d_proj[:, feat + h * HEAD : feat + (h + 1) * HEAD] = dot(d_s, q, 0, 0).astype(BF16)
            d_proj[:, 2 * feat + h * HEAD : 2 * feat + (h + 1) * HEAD] = dot(probs.astype(BF16), d_o, 0, 0).astype(BF16)
        small = parts.shape[3]
        store(2, r, 0, dot(mixed[slot], d_attn[...], 0, 0))
        store(2, r, feat // small, dot(d_proj[...], x[...], 0, 0))
        exchange(2, r)
        vec[r, 6:7, : 3 * feat] = jnp.sum(d_proj[...].astype(F32), axis=0, keepdims=True)
        value = total[...]
        for j in range(3):
            value = value + dot(d_proj[:, j * feat : (j + 1) * feat], w_qkv[slot, j], 1, 0)
        total[...] = value

        @pl.loop(PACE * (4 + 3 * ((i + 2) // 3) + i // 2 + 2 * (i // 3)), PACE * (7 + i + i // 2 + i // 3))
        def _(n):
            tick(n)

    for copy in vec_near:
        copy.start()
    low_tok[...] = total[...].astype(BF16)
    tok_near.start()
    tok_own.start()
    for copy in vec_near:
        copy.wait_recv()
    vec_b[...] = vec[2] + vec_a[1]
    vec_far.start()
    vec_s[0] = vec[0] + vec_a[0]
    tok_far.start()

    @pl.loop(PACE * 12, PACE * (count - 1 + extra) + LAGS[6] + 1)
    def _(i):
        @pl.when(i == PACE * count)
        def _():
            vec_far.wait()
            vec_s[0] = vec_s[0] + vec_r[0]
            vec_dp[0].start()

        for b in range(bits):
            @pl.when(i == PACE * (count + 1 + b))
            def _(b=b):
                vec_dp[b].wait()
                value = vec_s[b] + vec_r[1 + b]
                if b + 1 < bits:
                    vec_s[b + 1] = value
                    vec_dp[b + 1].start()
                else:
                    vec_out[...] = value

        tick(i)

    tok_far.wait_recv()
    tok_pass.start()
    for copy in vec_near:
        copy.wait_send()
    for k in range(KINDS):
        for j in range(2):
            near_copy(k, j).wait_send()

    @pl.loop(0, count)
    def _(c):
        for copy in (far_copy, x_copy, p_copy, q_copy, gq_copy, gp_copy, gx_copy):
            copy(c).wait_send()

    tok_near.wait()
    tok_far.wait_send()
    tok_own.wait()
    tok_pass.wait()


def backward(
    d_query, extents, gain1, gain2, upstream, n1, inv1, n2, inv2, h1_low, act, slope, w_up, w_down,
    qkv, mixed, w_out, w_qkv, x, ndp, nmp, block,
):
    rows, wide = x.shape
    feat, hidden = mixed.shape[2], act.shape[2]
    count = KINDS * CHUNKS
    pieces = CHUNKS * PIECES
    small = wide // pieces
    bits = ndp.bit_length() - 1
    extra = max(bits - 3, 1)
    vmem, anywhere = pl.BlockSpec(memory_space=pltpu.VMEM), pl.BlockSpec(memory_space=pl.ANY)
    dma = pltpu.SemaphoreType.DMA
    sds = jax.ShapeDtypeStruct
    vec = (8, wide)
    low, full = (lambda *shape: pltpu.VMEM(shape, BF16)), (lambda *shape: pltpu.VMEM(shape, F32))
    two = lambda a: low(2, *a.shape[1:])
    pair = lambda *shape: [dma(shape), dma(shape)]
    scratch = [full(rows, wide), full(*n1.shape), full(*inv1.shape), full(*n2.shape), full(*inv2.shape)]
    scratch += [low(rows, wide), low(rows, wide), low(*act.shape), two(slope), two(w_up), two(w_down)]
    scratch += [two(qkv), two(mixed), two(w_out), two(w_qkv)]
    scratch += [low(rows, wide), low(rows, wide), low(rows, 3 * feat), low(rows, wide)]
    scratch += [low(KINDS, nmp, pieces, small, wide), full(nmp, *vec), low(KINDS, 2, pieces, small, wide)]
    scratch += [low(count, n, small, wide) for n in (8, 4, 2, 1)] + [low(extra, count, 1, small, wide)]
    scratch += [full(2, *vec), full(*vec), full(bits, *vec), full(bits + 1, *vec)]
    scratch += [dma((8,)), dma((2, 3)), dma((2, 4))]
    scratch += pair(2 * KINDS) + pair(count) * 4 + pair(extra, count) + pair(count) * 3
    scratch += pair(2) + pair(bits + 1) + pair(3) + [dma]
    out = pl.pallas_call(
        functools.partial(backward_kernel, ndp, nmp, block),
        out_shape=(sds((count, 2, 2, 2, small, wide), BF16), sds(vec, F32), sds((nmp, rows, wide), BF16)),
        in_specs=[vmem, pl.BlockSpec(memory_space=pltpu.SMEM), vmem, vmem] + [anywhere] * 15,
        out_specs=(vmem, vmem, anywhere),
        scratch_shapes=scratch,
        compiler_params=pltpu.CompilerParams(
            collective_id=1, has_side_effects=True, vmem_limit_bytes=67043328
        ),
        name="backward",
    )(
        d_query, extents, gain1, gain2, upstream, n1, inv1, n2, inv2, h1_low, act, slope, w_up, w_down,
        qkv, mixed, w_out, w_qkv, x,
    )
    return out[0].reshape(KINDS, wide, wide), out[1], out[2].reshape(-1, wide)


def local(
    encoder_rows,
    piece_extent_sequence,
    triple_projection_matrix,
    asker_content_shifts,
    mixing_result_matrix,
    mixing_result_offset_vector,
    mixing_normalizer_scale,
    mixing_normalizer_shift,
    widen_matrix,
    widen_shift_vector,
    narrow_matrix,
    narrow_shift_vector,
    perceptron_normalizer_scale,
    perceptron_normalizer_shift,
    document_vectors,
    sharpness_factor,
    correct_document_position,
    upstream_sensitivity,
    *,
    width,
    depth,
):
    nblock = piece_extent_sequence.shape[0]
    block = encoder_rows.shape[0] // nblock
    rows = encoder_rows.shape[0] // width
    feat = triple_projection_matrix.shape[2]
    hidden = widen_matrix.shape[1]
    wide = encoder_rows.shape[1]

    w_qkv = triple_projection_matrix.transpose(0, 2, 1)
    small = jnp.concatenate(
        [jnp.pad(asker_content_shifts, ((0, 0), (0, hidden - feat))), widen_shift_vector[None]]
    )
    (
        qkv, mixed, n1, inv1, n2, inv2, h1_low, act, slope, w_qkv, w_out, w_up, w_down, own_out, query, x,
    ) = encode(
        encoder_rows, piece_extent_sequence, w_qkv, mixing_result_matrix, widen_matrix,
        narrow_matrix, small, mixing_result_offset_vector, mixing_normalizer_scale, mixing_normalizer_shift,
        narrow_shift_vector, perceptron_normalizer_scale, perceptron_normalizer_shift, block, width,
    )
    d_query, seg_loss, sharpness_derivative, layer_out = retrieval(
        query, own_out, document_vectors, correct_document_position[None], sharpness_factor, depth, width
    )
    layer_out = layer_out.reshape(-1, wide)
    sums, vectors, grad_tokens = backward(
        d_query, piece_extent_sequence, mixing_normalizer_scale, perceptron_normalizer_scale, upstream_sensitivity, n1, inv1, n2, inv2, h1_low, act, slope,
        w_up, w_down, qkv, mixed, w_out, w_qkv, x, depth, width, block,
    )
    grad_tokens = grad_tokens.astype(F32)
    grad_qkv = sums[2, feat:].astype(F32).reshape(3, feat, wide).transpose(0, 2, 1)
    return (
        layer_out,
        seg_loss[0],
        grad_tokens,
        grad_qkv,
        jnp.stack([vectors[6, :feat], vectors[6, 2 * feat : 3 * feat]]),
        sums[2, :feat].astype(F32),
        vectors[0],
        vectors[1],
        vectors[2],
        sums[1].astype(F32),
        vectors[7, :hidden],
        sums[0].astype(F32),
        vectors[3],
        vectors[4],
        vectors[5],
        sharpness_derivative[0],
    )


def solution(mesh):
    in_specs = (
        P("dp", None),
        P("dp", None),
        P(None, None, "mp"),
        P(None, "mp"),
        P("mp", None),
        P(),
        P(),
        P(),
        P(None, "mp"),
        P("mp"),
        P("mp", None),
        P(),
        P(),
        P(),
        P(("dp", "mp"), None),
        P(),
        P(),
        P("dp", None),
    )
    out_specs = (
        P("dp", None),
        P(),
        P("dp", None),
        P(None, None, "mp"),
        P(None, "mp"),
        P("mp", None),
        P(),
        P(),
        P(),
        P(None, "mp"),
        P("mp"),
        P("mp", None),
        P(),
        P(),
        P(),
        P(),
    )
    width = mesh.shape["mp"]

    def step(*args):
        return local(*args, width=width, depth=mesh.shape["dp"])

    return jax.shard_map(step, mesh=mesh, in_specs=in_specs, out_specs=out_specs, check_vma=False)
```

```python
import functools
import math

import jax
import jax.numpy as jnp
from jax import lax
from jax.experimental import pallas as pl
from jax.experimental.pallas import tpu as pltpu
from jax.sharding import PartitionSpec as P

HEAD = 64
F32 = jnp.float32
BF16 = jnp.bfloat16
MESH = pl.DeviceIdType.MESH
norm_epsilon = 1e-05
masked_score = -1e30


def dot(a, b, ca, cb):
    return lax.dot_general(a, b, (((ca,), (cb,)), ((), ())), preferred_element_type=F32)


def norm_stats(resid):
    centre = jnp.mean(resid, axis=-1, keepdims=True)
    centred = resid - centre
    spread = jnp.mean(centred * centred, axis=-1, keepdims=True)
    inv = lax.rsqrt(spread + norm_epsilon)
    return centred * inv, inv


def norm_back(d_out, normed, inv, gain):
    e = d_out * gain
    return inv * (
        e - jnp.mean(e, axis=-1, keepdims=True) - normed * jnp.mean(e * normed, axis=-1, keepdims=True)
    )


def flip(index, step):
    return index + step * (1 - 2 * lax.rem(index // step, 2))


def retrieval_kernel(
    ndp, nmp, query_ref, own_ref, docs_hbm, gold_ref, sharp_ref, dq_ref, loss_ref, ds_ref, layer,
    queries, docs, low, stats, columns, part_u, part_g, send, got, doc_sem, q_send, q_recv, s_send, s_recv, d_send, d_recv,
    l_s, l_r, own_sem,
):
    n = ndp * nmp
    own = query_ref.shape[0]
    nseg = gold_ref.shape[1]
    tile = 256 if nseg <= 256 else 128
    dp, mp = lax.axis_index("dp"), lax.axis_index("mp")
    me = dp * nmp + mp
    load = pltpu.make_async_copy(docs_hbm, docs, doc_sem)
    load.start()
    barrier = pltpu.get_barrier_semaphore()

    def device(step):
        other = lax.rem(me + step, n)
        return other, (other // nmp, lax.rem(other, nmp))

    @pl.loop(1, n)
    def _(step):
        _, where = device(step)
        pl.semaphore_signal(barrier, inc=1, device_id=where, device_id_type=MESH)

    pl.semaphore_wait(barrier, n - 1)

    def push(source, target, send_sems, recv_sems):
        @pl.loop(1, n)
        def _(step):
            other, where = device(step)
            pltpu.make_async_remote_copy(
                source(other), target, send_sems.at[step], recv_sems.at[step], device_id=where, device_id_type=MESH
            ).start()

    def drain(source, target, send_sems, recv_sems):
        @pl.loop(1, n)
        def _(step):
            other, where = device(step)
            copy = pltpu.make_async_remote_copy(
                source(other), target, send_sems.at[step], recv_sems.at[step], device_id=where, device_id_type=MESH
            )
            copy.wait()

    push(lambda other: query_ref, queries.at[me], q_send, q_recv)
    queries[me] = query_ref[...]
    drain(lambda other: query_ref, queries.at[me], q_send, q_recv)
    near, far, across = (dp, flip(mp, 1)), (dp, flip(mp, 2)), flip(mp, 2)

    def spread(source, target, i, where):
        return pltpu.make_async_remote_copy(
            source, target, l_s.at[i], l_r.at[i], device_id=where, device_id_type=MESH
        )

    to_near = spread(own_ref, layer.at[mp], 0, near)
    to_far, to_pass, first = [], [], 0
    for i, part in enumerate((7, 6, 3)):
        strip = pl.ds(first, own_ref.shape[0] * part // 16)
        first += own_ref.shape[0] * part // 16
        passed = layer.at[across, strip]
        to_far.append(spread(own_ref.at[strip], layer.at[mp, strip], 1 + i, far))
        to_pass.append(spread(passed, passed, 4 + i, near))
    keep = pltpu.make_async_copy(own_ref, layer.at[mp], own_sem)
    to_far[0].start()
    to_near.start()
    keep.start()
    load.wait()

    sharp = sharp_ref[0]
    offset = me * docs.shape[0]
    ids = lax.broadcasted_iota(jnp.int32, (tile, docs.shape[0]), 1).astype(F32)
    columns[...] = jnp.broadcast_to((gold_ref[...] - offset).astype(F32), (128, nseg)).T
    lane = lax.broadcasted_iota(jnp.int32, (tile, 128), 1)
    per = tile // own

    @pl.loop(0, nseg // tile)
    def _(i):
        span = pl.ds(pl.multiple_of(i * tile, tile), tile)
        q = queries[pl.ds(i * per, per)].reshape(tile, queries.shape[2])
        logit = lax.dot_general(q, docs[...], (((1,), (1,)), ((), ())), preferred_element_type=F32) / sharp
        match = ids == columns[span, 0:1]
        top = jnp.max(logit, axis=1, keepdims=True)
        expo = jnp.exp(logit - top)
        total = jnp.sum(expo, axis=1, keepdims=True)
        tilt = jnp.sum(expo * logit, axis=1, keepdims=True)
        gold = jnp.sum(jnp.where(match, logit, 0.0), axis=1, keepdims=True)
        packed = jnp.where(lane == 0, top, jnp.where(lane == 1, total, jnp.where(lane == 2, tilt, gold)))
        stats[me, :, span] = packed.T[:4]
        low[span, :] = jnp.where(match, 0.0, expo).astype(BF16)

    push(lambda other: stats.at[me], stats.at[me], s_send, s_recv)
    to_far[1].start()

    @pl.loop(0, nseg // tile)
    def _(i):
        span = pl.ds(pl.multiple_of(i * tile, tile), tile)
        part_u[span, :] = jnp.dot(low[span, :], docs[...], preferred_element_type=F32)
        match = ids == columns[span, 0:1]
        part_g[span, :] = jnp.dot(
            match.astype(F32).astype(BF16), docs[...], preferred_element_type=F32
        ).astype(BF16)

    drain(lambda other: stats.at[me], stats.at[me], s_send, s_recv)
    to_far[0].wait_recv()
    to_pass[0].start()

    tops = stats[:, 0, :]
    top = jnp.max(tops, axis=0, keepdims=True)
    share = jnp.exp(tops - top)
    total = jnp.sum(stats[:, 1, :] * share, axis=0, keepdims=True)
    tilt = jnp.sum(stats[:, 2, :] * share, axis=0, keepdims=True)
    gold = jnp.sum(stats[:, 3, :], axis=0, keepdims=True)
    lse = top + jnp.log(total)
    loss_ref[...] = lse - gold
    ds_ref[...] = -jnp.sum(tilt / total - gold, axis=1, keepdims=True) / sharp
    scale = jnp.exp(stats[me, 0:1, :] - lse) / sharp
    gold_scale = (jnp.exp(gold - lse) - 1.0) / sharp
    row = lax.broadcasted_iota(jnp.int32, (128, nseg), 0)
    columns[...] = jnp.where(row == 0, scale, gold_scale).T

    @pl.loop(0, nseg // tile)
    def _(i):
        span = pl.ds(pl.multiple_of(i * tile, tile), tile)
        value = part_u[span, :] * columns[span, 0:1] + part_g[span, :].astype(F32) * columns[span, 1:2]
        send[pl.ds(i * per, per)] = value.astype(BF16).reshape(per, own, value.shape[1])

    push(lambda other: send.at[other], got.at[me], d_send, d_recv)
    to_far[2].start()
    to_far[1].wait_recv()
    to_pass[1].start()
    got[me] = send[me]
    drain(lambda other: send.at[other], got.at[me], d_send, d_recv)
    dq_ref[...] = jnp.sum(got[...].astype(F32), axis=0)
    to_far[2].wait_recv()
    to_pass[2].start()
    to_near.wait()
    for copy in to_far:
        copy.wait_send()
    for copy in to_pass:
        copy.wait()
    keep.wait()


def retrieval(query, own_out, docs, gold, sharp, ndp, nmp):
    n = ndp * nmp
    own, width = query.shape
    nseg = gold.shape[1]
    vmem = pl.BlockSpec(memory_space=pltpu.VMEM)
    return pl.pallas_call(
        functools.partial(retrieval_kernel, ndp, nmp),
        out_shape=(
            jax.ShapeDtypeStruct((own, width), F32),
            jax.ShapeDtypeStruct((1, nseg), F32),
            jax.ShapeDtypeStruct((1, 1), F32),
            jax.ShapeDtypeStruct((nmp,) + own_out.shape, BF16),
        ),
        in_specs=[vmem, vmem, pl.BlockSpec(memory_space=pl.ANY), vmem, pl.BlockSpec(memory_space=pltpu.SMEM)],
        out_specs=(vmem, vmem, vmem, pl.BlockSpec(memory_space=pl.ANY)),
        scratch_shapes=[
            pltpu.VMEM((n, own, width), BF16),
            pltpu.VMEM(docs.shape, BF16),
            pltpu.VMEM((nseg, docs.shape[0]), BF16),
            pltpu.VMEM((n, 4, nseg), F32),
            pltpu.VMEM((nseg, 128), F32),
            pltpu.VMEM((nseg, width), F32),
            pltpu.VMEM((nseg, width), BF16),
            pltpu.VMEM((n, own, width), BF16),
            pltpu.VMEM((n, own, width), BF16),
            pltpu.SemaphoreType.DMA,
        ]
        + [pltpu.SemaphoreType.DMA((n,))] * 6
        + [pltpu.SemaphoreType.DMA((7,))] * 2
        + [pltpu.SemaphoreType.DMA],
        compiler_params=pltpu.CompilerParams(
            collective_id=0, has_side_effects=True, vmem_limit_bytes=60 * 2**20
        ),
        name="retrieval",
    )(query, own_out, docs, gold, sharp)


def gelu_with_slope(u):
    z = jnp.abs(u) * (0.5**0.5)
    t = 1.0 / (1.0 + 0.5 * z)
    poly = 0.17087277
    for c in (
        -0.82215223, 1.48851587, -1.13520398, 0.27886807, -0.18628806, 0.09678418, 0.37409196, 1.00002368,
    ):
        poly = poly * t + c
    square = z * z
    tail = 0.5 * t * jnp.exp(poly * t - 1.26551223 - square)
    cdf = jnp.where(u < 0, tail, 1.0 - tail)
    return u * cdf, cdf + u * (jnp.exp(-square) * ((2 * math.pi) ** -0.5))


def encode_kernel(nmp, block, *refs):
    (
        rows_hbm, extents, w_qkv, w_out, w_up, w_down, small_ref, *vectors,
    ) = refs[:13]
    out_bias, gain1, shift1, down_bias, gain2, shift2 = (v[...][None] for v in vectors)
    (
        qkv_o, mixed_o, n1_o, inv1_o, n2_o, inv2_o, low_o, act_o, slope_o, w_qkv_o, w_out_o, w_up_o, w_down_o,
        own_o, query_o, x_o,
    ) = refs[13:29]
    (
        x, qkv, mixed, n1, n2, h1_low, act, slope, all_qkv, all_out, all_up, all_down, small, total,
        fill_sem, save_sem, n_s, n_r, m_s, m_r, y_s, y_r, f_s, f_r, g_s, g_r, h_s, h_r, sm_s, sm_r,
    ) = refs[29:]
    dp, mp = lax.axis_index("dp"), lax.axis_index("mp")
    near, far, side = (dp, flip(mp, 1)), (dp, flip(mp, 2)), (flip(dp, 1), mp)
    b = lax.rem(dp, 2)
    rows = x.shape[0]
    feat = w_out.shape[0] * w_out.shape[1]
    scale = HEAD ** (-0.5)

    own_rows = rows_hbm.at[pl.ds(pl.multiple_of(mp * rows, rows), rows)]
    fills = [
        pltpu.make_async_copy(source, target, fill_sem.at[i])
        for i, (source, target) in enumerate(
            [
                (own_rows, x), (w_qkv, all_qkv.at[0]), (w_out, all_out.at[0]), (w_up, all_up.at[0]),
                (w_down, all_down.at[0]),
            ]
        )
    ]
    for copy in fills:
        copy.start()
    barrier = pltpu.get_barrier_semaphore()
    for where in (near, far, side):
        pl.semaphore_signal(barrier, inc=1, device_id=where, device_id_type=MESH)
    pl.semaphore_wait(barrier, 3)

    def remote(source, target, send, recv, where):
        return pltpu.make_async_remote_copy(source, target, send, recv, device_id=where, device_id_type=MESH)

    pieces = [(w_qkv.at[k], all_qkv, k) for k in range(3)] + [(w_out, all_out, None)]
    pieces += [(w_up.at[s], all_up, s) for s in range(w_up.shape[0])]
    pieces += [(w_down.at[s], all_down, s) for s in range(w_down.shape[0])]
    count = len(pieces)

    def slot(i, r):
        _, held, s = pieces[i]
        return held.at[r] if s is None else held.at[r, s]

    near_own = [remote(pieces[i][0], slot(i, 1), n_s.at[i], n_r.at[i], near) for i in range(count)]
    far_own = [remote(pieces[i][0].at[b], slot(i, 2).at[b], y_s.at[i], y_r.at[i], far) for i in range(count)]
    pass_side = [remote(slot(i, 2).at[b], slot(i, 2).at[b], f_s.at[i], f_r.at[i], side) for i in range(count)]
    pass_near = [remote(slot(i, 2).at[b], slot(i, 3).at[b], g_s.at[i], g_r.at[i], near) for i in range(count)]
    pass_other = [
        remote(slot(i, 2).at[1 - b], slot(i, 3).at[1 - b], h_s.at[i], h_r.at[i], near) for i in range(count)
    ]
    small_near = remote(small_ref, small.at[1], sm_s.at[0], sm_r.at[0], near)
    small_far = remote(small_ref, small.at[2], sm_s.at[1], sm_r.at[1], far)
    small_pass = remote(small.at[2], small.at[3], sm_s.at[2], sm_r.at[2], near)

    small_near.start()
    small_far.start()
    for i in range(count):
        far_own[i].start()
        near_own[i].start()
    small[0] = small_ref[...]
    by_quarter = [
        (qkv, qkv_o), (mixed, mixed_o), (act, act_o), (slope, slope_o), (all_qkv, w_qkv_o), (all_out, w_out_o),
        (all_up, w_up_o), (all_down, w_down_o),
    ]
    at_once = [(x, x_o), (n1, n1_o), (h1_low, low_o), (n2, n2_o)]

    def save(i, r):
        source, target = by_quarter[i]
        return pltpu.make_async_copy(source.at[r], target.at[r], save_sem.at[4 * i + r])

    def save_whole(i):
        source, target = at_once[i]
        return pltpu.make_async_copy(source, target, save_sem.at[4 * len(by_quarter) + i])

    def relay(i):
        far_own[i].wait_recv()
        pass_side[i].start()
        pass_near[i].start()

    def relay_other(i):
        pass_side[i].wait_recv()
        pass_other[i].start()

    def last_arrived(i):
        pass_near[i].wait_recv()
        pass_other[i].wait_recv()

    iota_row = lax.broadcasted_iota(jnp.int32, (1, rows), 1)
    iota_col = lax.broadcasted_iota(jnp.int32, (rows, 1), 0)
    nblk = rows // block
    nseg = extents.shape[1]
    seg_row, seg_col = jnp.zeros_like(iota_row), jnp.zeros_like(iota_col)
    starts = []
    for i in range(nblk):
        end = jnp.int32(i * block)
        for j in range(nseg):
            starts.append(end)
            end = end + extents[mp * nblk + i, j]
            seg_row = seg_row + (iota_row >= end).astype(jnp.int32)
            seg_col = seg_col + (iota_col >= end).astype(jnp.int32)
    wide = x.shape[1]
    ups, downs = range(4, 4 + w_up.shape[0]), range(4 + w_up.shape[0], count)

    def head(r, h):
        lanes = slice(h * HEAD, (h + 1) * HEAD)
        q = qkv[r, 0, :, lanes] * BF16(scale)
        scores = dot(q, qkv[r, 1, :, lanes], 1, 1)
        scores = jnp.where(seg_col == seg_row, scores, masked_score)
        expo = jnp.exp(scores - jnp.max(scores, axis=1, keepdims=True))
        probs = (expo * (1.0 / jnp.sum(expo, axis=1, keepdims=True))).astype(BF16)
        mixed[r, :, lanes] = jnp.dot(probs, qkv[r, 2, :, lanes], preferred_element_type=F32).astype(BF16)

    def both(i):
        relay(i)
        relay_other(i - 1)

    def on(r, at, *steps):
        @pl.when(r == at)
        def _():
            for step in steps:
                step()

    near_in = lambda group: [near_own[i].wait_recv for i in group]
    last_in = lambda group: [functools.partial(last_arrived, i) for i in group]
    do = functools.partial
    fills[0].wait()
    fills[1].wait()
    save_whole(0).start()

    @pl.loop(0, nmp)
    def _(r):
        on(r, 1, small_near.wait_recv, *near_in(range(3)))
        on(
            r, 2, small_far.wait_recv, small_pass.start, do(relay, 0), do(relay, 1), do(relay_other, 0), do(relay, 2),
            do(relay_other, 1), do(relay, 3), do(relay_other, 2),
        )
        on(r, 3, small_pass.wait_recv, *last_in(range(3)))
        for k in range(3):
            value = dot(x[...], all_qkv[r, k].reshape(feat, wide), 1, 1)
            if k == 0:
                value = value + small[r, 0:1, :feat]
            if k == 2:
                value = value + small[r, 1:2, :feat]
            qkv[r, k] = value.astype(BF16)
        save(0, r).start()
        save(4, r).start()
        head(r, 0)
        on(r, 2, do(relay_other, 3))
        on(r, 3, do(both, 5))
        head(r, 1)
        on(r, 2, do(relay, 4))
        for h in range(2, feat // HEAD):
            head(r, h)
        save(1, r).start()

    fills[2].wait()
    near_own[3].wait_recv()
    last_arrived(3)
    total[...] = x[...].astype(F32) + out_bias

    @pl.loop(0, nmp)
    def _(r):
        total[...] += jnp.dot(mixed[r], all_out[r].reshape(feat, wide), preferred_element_type=F32)
        save(5, r).start()

    tile = 128

    @pl.loop(0, rows // tile)
    def _(t):
        span = pl.ds(pl.multiple_of(t * tile, tile), tile)
        normed, inv = norm_stats(total[span])
        n1[span] = normed
        inv1_o[span] = jnp.broadcast_to(inv, (tile, inv1_o.shape[1]))
        h1 = normed * gain1 + shift1
        total[span] = h1 + down_bias
        h1_low[span] = h1.astype(BF16)

    save_whole(1).start()
    save_whole(2).start()
    both(6)
    fills[3].wait()
    fills[4].wait()

    @pl.loop(0, nmp)
    def _(r):
        on(r, 1, *near_in(ups))
        on(r, 3, *last_in(ups))
        upper = jnp.dot(h1_low[...], all_up[r].reshape(wide, -1), preferred_element_type=F32) + small[r, 2:3, :]
        value, gradient = gelu_with_slope(upper)
        act[r] = value.astype(BF16)
        slope[r] = gradient.astype(BF16)
        for i in (2, 3, 6):
            save(i, r).start()
        on(r, 0, do(both, 7))
        on(r, 1, do(both, 8), *near_in(downs))
        on(r, 2, do(both, 9), do(relay_other, 9))
        on(r, 3, *last_in(downs))
        total[...] += jnp.dot(act[r], all_down[r].reshape(-1, wide), preferred_element_type=F32)
        save(7, r).start()

    @pl.loop(0, rows // tile)
    def _(t):
        span = pl.ds(pl.multiple_of(t * tile, tile), tile)
        normed, inv = norm_stats(total[span])
        n2[span] = normed
        inv2_o[span] = jnp.broadcast_to(inv, (tile, inv2_o.shape[1]))
        own_o[span] = (normed * gain2 + shift2).astype(BF16)

    save_whole(3).start()
    line = lax.broadcasted_iota(jnp.int32, (len(starts), rows), 0)
    first = jnp.zeros((len(starts), rows), jnp.int32)
    for j, start in enumerate(starts):
        first = jnp.where(line == j, start, first)
    pick = (lax.broadcasted_iota(jnp.int32, first.shape, 1) == first).astype(F32).astype(BF16)
    query_o[...] = jnp.dot(pick, own_o[...], preferred_element_type=F32).astype(BF16)
    for i in range(len(at_once)):
        save_whole(i).wait()

    @pl.loop(0, nmp)
    def _(r):
        for i in range(len(by_quarter)):
            save(i, r).wait()

    for copy in near_own + far_own + pass_side + pass_near + pass_other + [small_near, small_far, small_pass]:
        copy.wait_send()


STRIPS = 3


def encode(
    encoder_rows, extents, w_qkv, w_out, w_up, w_down, small, out_bias, gain1, shift1, down_bias, gain2, shift2,
    block, nmp,
):
    rows = encoder_rows.shape[0] // nmp
    wide = encoder_rows.shape[1]
    feat, hidden = w_qkv.shape[1], w_up.shape[1]
    nseg = extents.shape[0] * extents.shape[1] // nmp
    cut_qkv = w_qkv.reshape(3, 2, feat // 2, wide)
    cut_out = w_out.reshape(2, feat // 2, wide)
    cut_up = w_up.reshape(STRIPS, 2, wide // (2 * STRIPS), hidden)
    cut_down = w_down.reshape(STRIPS, 2, hidden // (2 * STRIPS), wide)
    vmem, anywhere = pl.BlockSpec(memory_space=pltpu.VMEM), pl.BlockSpec(memory_space=pl.ANY)
    sds = jax.ShapeDtypeStruct
    dma = pltpu.SemaphoreType.DMA
    every = lambda a: (nmp,) + a.shape
    held = [
        sds((nmp, 3, rows, feat), BF16),
        sds((nmp, rows, feat), BF16),
        sds((rows, wide), F32),
        sds((rows, 128), F32),
        sds((rows, wide), F32),
        sds((rows, 128), F32),
        sds((rows, wide), BF16),
        sds((nmp, rows, hidden), BF16),
        sds((nmp, rows, hidden), BF16),
        sds(every(cut_qkv), BF16),
        sds(every(cut_out), BF16),
        sds(every(cut_up), BF16),
        sds(every(cut_down), BF16),
        sds((rows, wide), BF16),
        sds((nseg, wide), BF16),
        sds((rows, wide), BF16),
    ]
    count = 4 + 2 * STRIPS
    scratch = [
        pltpu.VMEM((rows, wide), BF16),
        pltpu.VMEM(held[0].shape, BF16),
        pltpu.VMEM(held[1].shape, BF16),
        pltpu.VMEM((rows, wide), F32),
        pltpu.VMEM((rows, wide), F32),
        pltpu.VMEM((rows, wide), BF16),
        pltpu.VMEM(held[7].shape, BF16),
        pltpu.VMEM(held[8].shape, BF16),
    ]
    scratch += [pltpu.VMEM(h.shape, BF16) for h in held[9:13]]
    scratch += [pltpu.VMEM(every(small), F32), pltpu.VMEM((rows, wide), F32), dma((5,)), dma((36,))]
    scratch += [dma((count,))] * 12 + [dma((3,))] * 2
    outs = pl.pallas_call(
        functools.partial(encode_kernel, nmp, block),
        out_shape=tuple(held),
        in_specs=[anywhere, pl.BlockSpec(memory_space=pltpu.SMEM)] + [anywhere] * 4 + [vmem] * 7,
        out_specs=tuple(vmem if i in (3, 5, 13, 14) else anywhere for i in range(len(held))),
        scratch_shapes=scratch,
        compiler_params=pltpu.CompilerParams(collective_id=2, has_side_effects=True, vmem_limit_bytes=62 * 2**20),
        name="encode",
    )(encoder_rows, extents, cut_qkv, cut_out, cut_up, cut_down, small, out_bias, gain1, shift1, down_bias, gain2, shift2)
    outs = list(outs)
    outs[9] = outs[9].reshape(nmp, 3, feat, wide)
    outs[10] = outs[10].reshape(nmp, feat, wide)
    outs[11] = outs[11].reshape(nmp, wide, hidden)
    outs[12] = outs[12].reshape(nmp, hidden, wide)
    return outs


PIECES = 8
CHUNKS = 6
KINDS = 3
PACE = 4
LAGS = (0, 7, 12, 18, 24, 29, 36)


def backward_kernel(ndp, nmp, block, *refs):
    (
        d_query, extents, gain1, gain2, upstream_h, n1_h, inv1_h, n2_h, inv2_h, low_h, act_h, slope_h, up_h, down_h,
        qkv_h, mixed_h, w_out_h, w_qkv_h, x_h,
    ) = refs[:19]
    out, vec_out, tok = refs[19:22]
    (
        total, n1, inv1, n2, inv2, h1_low, x, act, slope, w_up, w_down, qkv, mixed, w_out, w_qkv,
        d_ffn, d_attn, d_proj, low_tok, parts, vec, near, got_y, got_x, got_1, got_2, got_e,
        vec_a, vec_b, vec_s, vec_r,
        load_sem, ffn_sem, attn_sem, a_s, a_r, y_s, y_r, x_s, x_r, p_s, p_r, q_s, q_r, e_s, e_r,
        gq_s, gq_r, gp_s, gp_r, gx_s, gx_r, va_s, va_r, v_s, v_r, t_s, t_r, own_sem,
    ) = refs[22:]
    count = KINDS * CHUNKS
    bits = ndp.bit_length() - 1
    extra = bits - 3
    rows, wide = total.shape
    feat = mixed.shape[2]
    hidden = act.shape[2]
    dp, mp = lax.axis_index("dp"), lax.axis_index("mp")
    near_dev, far_dev = (dp, flip(mp, 1)), (dp, flip(mp, 2))
    dp_dev = [(flip(dp, 1 << b), mp) for b in range(bits)]
    b0, b1, b2 = (lax.rem(dp // (1 << b), 2) for b in range(3))
    ident = b0 * 4 + b1 * 2 + b2
    gain1, gain2 = gain1[...][None], gain2[...][None]

    own_rows = upstream_h.at[pl.ds(pl.multiple_of(mp * rows, rows), rows)]
    loads = [
        pltpu.make_async_copy(source, target, load_sem.at[i])
        for i, (source, target) in enumerate(
            [
                (own_rows, total), (n2_h, n2), (inv2_h, inv2), (act_h, act), (low_h, h1_low), (n1_h, n1),
                (inv1_h, inv1), (x_h, x),
            ]
        )
    ]

    def ffn_loads(i):
        r, slot = 3 - i, lax.rem(i, 2)
        return [
            pltpu.make_async_copy(source.at[r], target.at[slot], ffn_sem.at[slot, j])
            for j, (source, target) in enumerate([(down_h, w_down), (slope_h, slope), (up_h, w_up)])
        ]

    def attn_loads(i):
        r, slot = 3 - i, lax.rem(i, 2)
        return [
            pltpu.make_async_copy(source.at[r], target.at[slot], attn_sem.at[slot, j])
            for j, (source, target) in enumerate([(w_out_h, w_out), (qkv_h, qkv), (mixed_h, mixed), (w_qkv_h, w_qkv)])
        ]

    for copy in loads + ffn_loads(0):
        copy.start()
    barrier = pltpu.get_barrier_semaphore()
    for where in [near_dev, far_dev] + dp_dev:
        pl.semaphore_signal(barrier, inc=1, device_id=where, device_id_type=MESH)
    pl.semaphore_wait(barrier, 2 + bits)

    def remote(source, target, send, recv, where):
        return pltpu.make_async_remote_copy(source, target, send, recv, device_id=where, device_id_type=MESH)

    def part(c, r, first=0, many=PIECES):
        k = c // CHUNKS
        return parts.at[k, r, pl.ds((c - k * CHUNKS) * PIECES + first, many)]

    def near_copy(k, j):
        return remote(parts.at[k, 2 * j + 1], near.at[k, j], a_s.at[2 * k + j], a_r.at[2 * k + j], near_dev)

    def far_copy(c):
        return remote(part(c, 2), got_y.at[c], y_s.at[c], y_r.at[c], far_dev)

    def x_copy(c):
        return remote(part(c, 0, (1 - b0) * 4, 4), got_x.at[c], x_s.at[c], x_r.at[c], dp_dev[0])

    def p_copy(c):
        return remote(part(c, 0, b0 * 4 + (1 - b1) * 2, 2), got_1.at[c], p_s.at[c], p_r.at[c], dp_dev[1])

    def q_copy(c):
        return remote(part(c, 0, ident + 1 - 2 * b2, 1), got_2.at[c], q_s.at[c], q_r.at[c], dp_dev[2])

    def e_copy(c, e):
        return remote(part(c, 0, ident, 1), got_e.at[e, c], e_s.at[e, c], e_r.at[e, c], dp_dev[3 + e])

    def gq_copy(c):
        held = out.at[c, b0, b1, b2]
        return remote(held, held, gq_s.at[c], gq_r.at[c], dp_dev[2])

    def gp_copy(c):
        held = out.at[c, b0, b1]
        return remote(held, held, gp_s.at[c], gp_r.at[c], dp_dev[1])

    def gx_copy(c):
        held = out.at[c, b0]
        return remote(held, held, gx_s.at[c], gx_r.at[c], dp_dev[0])

    vec_near = [remote(vec.at[2 * j + 1], vec_a.at[j], va_s.at[j], va_r.at[j], near_dev) for j in range(2)]
    vec_far = remote(vec_b, vec_r.at[0], v_s.at[0], v_r.at[0], far_dev)
    vec_dp = [remote(vec_s.at[b], vec_r.at[1 + b], v_s.at[1 + b], v_r.at[1 + b], dp_dev[b]) for b in range(bits)]
    across = flip(mp, 2)
    tok_near = remote(low_tok, tok.at[mp], t_s.at[0], t_r.at[0], near_dev)
    tok_far = remote(low_tok, tok.at[mp], t_s.at[1], t_r.at[1], far_dev)
    tok_pass = remote(tok.at[across], tok.at[across], t_s.at[2], t_r.at[2], near_dev)
    tok_own = pltpu.make_async_copy(low_tok, tok.at[mp], own_sem)

    def add(a, b):
        return (a.astype(F32) + b.astype(F32)).astype(BF16)

    def exchange(k, r):
        j = r // 2

        @pl.when(lax.rem(r, 2) == 1)
        def _():
            near_copy(k, j).start()

        @pl.when(lax.rem(r, 2) == 0)
        def _():
            near_copy(k, j).wait_recv()

            @pl.loop(0, CHUNKS)
            def _(i):
                span = pl.ds(i * PIECES, PIECES)
                parts[k, r, span] = add(parts[k, r, span], near[k, j, span])

                @pl.when(j == 1)
                def _():
                    far_copy(k * CHUNKS + i).start()

    def tick(i):
        def at(lag, do):
            since = i - lag

            @pl.when((since >= 0) & (since < PACE * count) & (lax.rem(since, PACE) == 0))
            def _():
                do(since // PACE)

        def update(c, first, many, got):
            target = part(c, 0, first, many)
            target[...] = add(target[...], got[c])

        @functools.partial(at, LAGS[6] + PACE * extra)
        def _(c):
            gx_copy(c).wait_recv()

        @functools.partial(at, LAGS[5] + PACE * extra)
        def _(c):
            gp_copy(c).wait_recv()
            gx_copy(c).start()

        @functools.partial(at, LAGS[4] + PACE * extra)
        def _(c):
            gq_copy(c).wait_recv()
            gp_copy(c).start()

        for e in reversed(range(extra)):
            @functools.partial(at, LAGS[3] + PACE * (1 + e))
            def _(c, e=e):
                e_copy(c, e).wait()
                update(c, ident, 1, got_e.at[e])
                if e + 1 < extra:
                    e_copy(c, e + 1).start()
                else:
                    out[c, b0, b1, b2] = part(c, 0, ident, 1)[0]
                    gq_copy(c).start()

        @functools.partial(at, LAGS[3])
        def _(c):
            q_copy(c).wait_recv()
            if extra:
                update(c, ident, 1, got_2)
                e_copy(c, 0).start()
            else:
                out[c, b0, b1, b2] = add(part(c, 0, ident, 1)[0], got_2[c, 0])
                gq_copy(c).start()

        @functools.partial(at, LAGS[2])
        def _(c):
            p_copy(c).wait_recv()
            update(c, b0 * 4 + b1 * 2, 2, got_1)
            q_copy(c).start()

        @functools.partial(at, LAGS[1])
        def _(c):
            x_copy(c).wait_recv()
            update(c, b0 * 4, 4, got_x)
            p_copy(c).start()

        @functools.partial(at, 0)
        def _(c):
            far_copy(c).wait_recv()
            update(c, 0, PIECES, got_y)
            x_copy(c).start()

    tile = 128
    nblk = rows // block
    nseg = extents.shape[1]
    vec[...] = jnp.zeros_like(vec)
    for copy in loads[:3]:
        copy.wait()

    def count_up(row, value):
        vec[0, row : row + 1] += jnp.sum(value, axis=0, keepdims=True)

    @pl.loop(0, rows // tile)
    def _(t):
        span = pl.ds(pl.multiple_of(t * tile, tile), tile)
        line = lax.broadcasted_iota(jnp.int32, (tile, 1), 0) + t * tile
        d_h2 = total[span]
        for i in range(nblk):
            start = jnp.int32(i * block)
            for j in range(nseg):
                d_h2 = d_h2 + jnp.where(line == start, d_query[i * nseg + j, :][None], 0.0)
                start = start + extents[mp * nblk + i, j]
        normed = n2[span]
        count_up(5, d_h2)
        count_up(4, d_h2 * normed)
        d_r2 = norm_back(d_h2, normed, inv2[span, 0:1], gain2)
        count_up(3, d_r2)
        d_ffn[span] = d_r2.astype(BF16)
        total[span] = d_r2

    def store(k, r, first, value):
        pieces = value.shape[0] // parts.shape[3]
        parts[k, r, first : first + pieces] = value.astype(BF16).reshape(pieces, parts.shape[3], wide)

    loads[3].wait()

    @pl.loop(0, nmp)
    def _(i):
        r = 3 - i
        store(0, r, 0, dot(act[r], d_ffn[...], 0, 0))
        exchange(0, r)

    for copy in loads[4:]:
        copy.wait()
    for copy in attn_loads(0):
        copy.start()

    @pl.loop(0, nmp)
    def _(i):
        r, slot = 3 - i, lax.rem(i, 2)
        for copy in ffn_loads(i):
            copy.wait()

        @pl.when(i + 1 < nmp)
        def _():
            for copy in ffn_loads(i + 1):
                copy.start()

        d_up = (dot(d_ffn[...], w_down[slot], 1, 1) * slope[slot].astype(F32)).astype(BF16)
        vec[r, 7:8, :hidden] = jnp.sum(d_up.astype(F32), axis=0, keepdims=True)
        store(1, r, 0, dot(h1_low[...], d_up, 0, 0))
        exchange(1, r)
        total[...] += dot(d_up, w_up[slot], 1, 1)

        @pl.loop(PACE * (i - (i + 2) // 3), PACE * (i + i // 3))
        def _(n):
            tick(n)

    @pl.loop(0, rows // tile)
    def _(t):
        span = pl.ds(pl.multiple_of(t * tile, tile), tile)
        d_h1 = total[span]
        normed = n1[span]
        count_up(2, d_h1)
        count_up(1, d_h1 * normed)
        d_r1 = norm_back(d_h1, normed, inv1[span, 0:1], gain1)
        count_up(0, d_r1)
        d_attn[span] = d_r1.astype(BF16)
        total[span] = d_r1

    for r in range(1, nmp):
        vec[r, 0:6] = vec[0, 0:6]

    iota_row = lax.broadcasted_iota(jnp.int32, (1, rows), 1)
    iota_col = lax.broadcasted_iota(jnp.int32, (rows, 1), 0)
    seg_row, seg_col = jnp.zeros_like(iota_row), jnp.zeros_like(iota_col)
    for i in range(nblk):
        end = jnp.int32(i * block)
        for j in range(nseg):
            end = end + extents[mp * nblk + i, j]
            seg_row = seg_row + (iota_row >= end).astype(jnp.int32)
            seg_col = seg_col + (iota_col >= end).astype(jnp.int32)
    scale = HEAD ** (-0.5)

    @pl.loop(0, nmp)
    def _(i):
        r, slot = 3 - i, lax.rem(i, 2)
        for copy in attn_loads(i):
            copy.wait()

        @pl.when(i + 1 < nmp)
        def _():
            for copy in attn_loads(i + 1):
                copy.start()

        d_mixed = dot(d_attn[...], w_out[slot], 1, 1).astype(BF16)
        for h in range(feat // HEAD):
            lanes = slice(h * HEAD, (h + 1) * HEAD)
            q = qkv[slot, 0, :, lanes] * BF16(scale)
            k = qkv[slot, 1, :, lanes]
            v = qkv[slot, 2, :, lanes]
            d_o = d_mixed[:, lanes]
            scores = jnp.where(seg_col == seg_row, dot(q, k, 1, 1), masked_score)
            expo = jnp.exp(scores - jnp.max(scores, axis=1, keepdims=True))
            probs = expo * (1.0 / jnp.sum(expo, axis=1, keepdims=True))
            d_p = dot(d_o, v, 1, 1)
            d_s = (probs * (d_p - jnp.sum(d_p * probs, axis=1, keepdims=True))).astype(BF16)
            d_proj[:, h * HEAD : (h + 1) * HEAD] = (dot(d_s, k, 1, 0) * scale).astype(BF16)
            d_proj[:, feat + h * HEAD : feat + (h + 1) * HEAD] = dot(d_s, q, 0, 0).astype(BF16)
            d_proj[:, 2 * feat + h * HEAD : 2 * feat + (h + 1) * HEAD] = dot(probs.astype(BF16), d_o, 0, 0).astype(BF16)
        small = parts.shape[3]
        store(2, r, 0, dot(mixed[slot], d_attn[...], 0, 0))
        store(2, r, feat // small, dot(d_proj[...], x[...], 0, 0))
        exchange(2, r)
        vec[r, 6:7, : 3 * feat] = jnp.sum(d_proj[...].astype(F32), axis=0, keepdims=True)
        value = total[...]
        for j in range(3):
            value = value + dot(d_proj[:, j * feat : (j + 1) * feat], w_qkv[slot, j], 1, 0)
        total[...] = value

        @pl.loop(PACE * (4 + 3 * ((i + 2) // 3) + i // 2 + 2 * (i // 3)), PACE * (7 + i + i // 2 + i // 3))
        def _(n):
            tick(n)

    for copy in vec_near:
        copy.start()
    low_tok[...] = total[...].astype(BF16)
    tok_near.start()
    tok_own.start()
    for copy in vec_near:
        copy.wait_recv()
    vec_b[...] = vec[2] + vec_a[1]
    vec_far.start()
    vec_s[0] = vec[0] + vec_a[0]
    tok_far.start()

    @pl.loop(PACE * 12, PACE * (count - 1 + extra) + LAGS[6] + 1)
    def _(i):
        @pl.when(i == PACE * count)
        def _():
            vec_far.wait()
            vec_s[0] = vec_s[0] + vec_r[0]
            vec_dp[0].start()

        for b in range(bits):
            @pl.when(i == PACE * (count + 1 + b))
            def _(b=b):
                vec_dp[b].wait()
                value = vec_s[b] + vec_r[1 + b]
                if b + 1 < bits:
                    vec_s[b + 1] = value
                    vec_dp[b + 1].start()
                else:
                    vec_out[...] = value

        tick(i)

    tok_far.wait_recv()
    tok_pass.start()
    for copy in vec_near:
        copy.wait_send()
    for k in range(KINDS):
        for j in range(2):
            near_copy(k, j).wait_send()

    @pl.loop(0, count)
    def _(c):
        for copy in (far_copy, x_copy, p_copy, q_copy, gq_copy, gp_copy, gx_copy):
            copy(c).wait_send()

    tok_near.wait()
    tok_far.wait_send()
    tok_own.wait()
    tok_pass.wait()


def backward(
    d_query, extents, gain1, gain2, upstream, n1, inv1, n2, inv2, h1_low, act, slope, w_up, w_down,
    qkv, mixed, w_out, w_qkv, x, ndp, nmp, block,
):
    rows, wide = x.shape
    feat, hidden = mixed.shape[2], act.shape[2]
    count = KINDS * CHUNKS
    pieces = CHUNKS * PIECES
    small = wide // pieces
    bits = ndp.bit_length() - 1
    extra = max(bits - 3, 1)
    vmem, anywhere = pl.BlockSpec(memory_space=pltpu.VMEM), pl.BlockSpec(memory_space=pl.ANY)
    dma = pltpu.SemaphoreType.DMA
    sds = jax.ShapeDtypeStruct
    vec = (8, wide)
    low, full = (lambda *shape: pltpu.VMEM(shape, BF16)), (lambda *shape: pltpu.VMEM(shape, F32))
    two = lambda a: low(2, *a.shape[1:])
    pair = lambda *shape: [dma(shape), dma(shape)]
    scratch = [full(rows, wide), full(*n1.shape), full(*inv1.shape), full(*n2.shape), full(*inv2.shape)]
    scratch += [low(rows, wide), low(rows, wide), low(*act.shape), two(slope), two(w_up), two(w_down)]
    scratch += [two(qkv), two(mixed), two(w_out), two(w_qkv)]
    scratch += [low(rows, wide), low(rows, wide), low(rows, 3 * feat), low(rows, wide)]
    scratch += [low(KINDS, nmp, pieces, small, wide), full(nmp, *vec), low(KINDS, 2, pieces, small, wide)]
    scratch += [low(count, n, small, wide) for n in (8, 4, 2, 1)] + [low(extra, count, 1, small, wide)]
    scratch += [full(2, *vec), full(*vec), full(bits, *vec), full(bits + 1, *vec)]
    scratch += [dma((8,)), dma((2, 3)), dma((2, 4))]
    scratch += pair(2 * KINDS) + pair(count) * 4 + pair(extra, count) + pair(count) * 3
    scratch += pair(2) + pair(bits + 1) + pair(3) + [dma]
    out = pl.pallas_call(
        functools.partial(backward_kernel, ndp, nmp, block),
        out_shape=(sds((count, 2, 2, 2, small, wide), BF16), sds(vec, F32), sds((nmp, rows, wide), BF16)),
        in_specs=[vmem, pl.BlockSpec(memory_space=pltpu.SMEM), vmem, vmem] + [anywhere] * 15,
        out_specs=(vmem, vmem, anywhere),
        scratch_shapes=scratch,
        compiler_params=pltpu.CompilerParams(
            collective_id=1, has_side_effects=True, vmem_limit_bytes=67043328
        ),
        name="backward",
    )(
        d_query, extents, gain1, gain2, upstream, n1, inv1, n2, inv2, h1_low, act, slope, w_up, w_down,
        qkv, mixed, w_out, w_qkv, x,
    )
    return out[0].reshape(KINDS, wide, wide), out[1], out[2].reshape(-1, wide)


def local(
    encoder_rows,
    piece_extent_sequence,
    triple_projection_matrix,
    asker_content_shifts,
    mixing_result_matrix,
    mixing_result_offset_vector,
    mixing_normalizer_scale,
    mixing_normalizer_shift,
    widen_matrix,
    widen_shift_vector,
    narrow_matrix,
    narrow_shift_vector,
    perceptron_normalizer_scale,
    perceptron_normalizer_shift,
    document_vectors,
    sharpness_factor,
    correct_document_position,
    upstream_sensitivity,
    *,
    width,
    depth,
):
    nblock = piece_extent_sequence.shape[0]
    block = encoder_rows.shape[0] // nblock
    rows = encoder_rows.shape[0] // width
    feat = triple_projection_matrix.shape[2]
    hidden = widen_matrix.shape[1]
    wide = encoder_rows.shape[1]

    w_qkv = triple_projection_matrix.transpose(0, 2, 1)
    small = jnp.concatenate(
        [jnp.pad(asker_content_shifts, ((0, 0), (0, hidden - feat))), widen_shift_vector[None]]
    )
    (
        qkv, mixed, n1, inv1, n2, inv2, h1_low, act, slope, w_qkv, w_out, w_up, w_down, own_out, query, x,
    ) = encode(
        encoder_rows, piece_extent_sequence, w_qkv, mixing_result_matrix, widen_matrix,
        narrow_matrix, small, mixing_result_offset_vector, mixing_normalizer_scale, mixing_normalizer_shift,
        narrow_shift_vector, perceptron_normalizer_scale, perceptron_normalizer_shift, block, width,
    )
    d_query, seg_loss, sharpness_derivative, layer_out = retrieval(
        query, own_out, document_vectors, correct_document_position[None], sharpness_factor, depth, width
    )
    layer_out = layer_out.reshape(-1, wide)
    sums, vectors, grad_tokens = backward(
        d_query, piece_extent_sequence, mixing_normalizer_scale, perceptron_normalizer_scale, upstream_sensitivity, n1, inv1, n2, inv2, h1_low, act, slope,
        w_up, w_down, qkv, mixed, w_out, w_qkv, x, depth, width, block,
    )
    grad_tokens = grad_tokens.astype(F32)
    grad_qkv = sums[2, feat:].astype(F32).reshape(3, feat, wide).transpose(0, 2, 1)
    return (
        layer_out,
        seg_loss[0],
        grad_tokens,
        grad_qkv,
        jnp.stack([vectors[6, :feat], vectors[6, 2 * feat : 3 * feat]]),
        sums[2, :feat].astype(F32),
        vectors[0],
        vectors[1],
        vectors[2],
        sums[1].astype(F32),
        vectors[7, :hidden],
        sums[0].astype(F32),
        vectors[3],
        vectors[4],
        vectors[5],
        sharpness_derivative[0],
    )


def solution(mesh):
    in_specs = (
        P("dp", None),
        P("dp", None),
        P(None, None, "mp"),
        P(None, "mp"),
        P("mp", None),
        P(),
        P(),
        P(),
        P(None, "mp"),
        P("mp"),
        P("mp", None),
        P(),
        P(),
        P(),
        P(("dp", "mp"), None),
        P(),
        P(),
        P("dp", None),
    )
    out_specs = (
        P("dp", None),
        P(),
        P("dp", None),
        P(None, None, "mp"),
        P(None, "mp"),
        P("mp", None),
        P(),
        P(),
        P(),
        P(None, "mp"),
        P("mp"),
        P("mp", None),
        P(),
        P(),
        P(),
        P(),
    )
    width = mesh.shape["mp"]

    def step(*args):
        return local(*args, width=width, depth=mesh.shape["dp"])

    return jax.shard_map(step, mesh=mesh, in_specs=in_specs, out_specs=out_specs, check_vma=False)
```
